32 devices in a mesh: seq: 4 (over y, x), fsdp: 8 (over z, core).
Axes of the slice: x: 2, y: 2, z: 4, core: 2. Of those that a mesh axis runs over, the one named last changes fastest.
Arguments:
- inputs: bfloat16 [8, 1536, 768], P(None, ('seq', 'fsdp')), may hold values from -6 to 6
- w_query: bfloat16 [768, 768], P('fsdp'), may hold values from -0.21875 to 0.21875
- w_key: bfloat16 [768, 768], P('fsdp'), may hold values from -0.21875 to 0.21875
- w_value: bfloat16 [768, 768], P('fsdp'), may hold values from -0.21875 to 0.21875
- b_value: bfloat16 [768], P('fsdp'), may hold values from -3 to 3
- w_out: bfloat16 [768, 768], P('fsdp'), may hold values from -0.625 to 0.625
- b_out: bfloat16 [768], P('fsdp'), may hold values from -3 to 3
- norm1_gain: bfloat16 [768], P('fsdp'), may hold values from 0.099609375 to 1.8984375
- norm1_bias: bfloat16 [768], P('fsdp'), may hold values from -3 to 3
- w_in: bfloat16 [768, 3072], P('fsdp'), may hold values from -0.21875 to 0.21875
- b_in: bfloat16 [3072], P('fsdp'), may hold values from -3 to 3
- w_back: bfloat16 [3072, 768], P('fsdp'), may hold values from -0.15625 to 0.15625
- b_back: bfloat16 [768], P('fsdp'), may hold values from -3 to 3
- norm2_gain: bfloat16 [768], P('fsdp'), may hold values from 0.099609375 to 1.8984375
- norm2_bias: bfloat16 [768], P('fsdp'), may hold values from -3 to 3
- w_relative: bfloat16 [768, 12, 64], P('fsdp', 'seq'), may hold values from -0.21875 to 0.21875
- bias_content: bfloat16 [12, 64], P('seq', 'fsdp'), may hold values from -5 to 5
- bias_position: bfloat16 [12, 64], P('seq', 'fsdp'), may hold values from -5 to 5
- bias_type: bfloat16 [12, 64], P('seq', 'fsdp'), may hold values from -5 to 5
- type_embed: bfloat16 [2, 12, 64], P(None, 'seq', 'fsdp'), may hold values from -5 to 5
- lengths: int32 [8, 3], replicated, may hold values from 1 to 1024, 1536 in all within a row
- token_types: int32 [8, 1536], replicated, may hold values from 0 to 1
- owners: int32 [8], replicated, may hold values from 0 to 7, each once
- grad_output: bfloat16 [8, 1536, 768], P('fsdp', 'seq'), may hold values from -6 to 6
Outputs:
- activations: bfloat16 [8, 1536, 768], P('fsdp', 'seq')
- input_grad: bfloat16 [8, 1536, 768], P(None, ('seq', 'fsdp'))
- grad_w_query: float32 [768, 768], P(('seq', 'fsdp'))
- grad_w_key: float32 [768, 768], P(('seq', 'fsdp'))
- grad_w_value: float32 [768, 768], P(('seq', 'fsdp'))
- grad_b_value: float32 [768], P(('seq', 'fsdp'))
- grad_w_out: float32 [768, 768], P(('seq', 'fsdp'))
- grad_b_out: float32 [768], P(('seq', 'fsdp'))
- grad_norm1_gain: float32 [768], P(('seq', 'fsdp'))
- grad_norm1_bias: float32 [768], P(('seq', 'fsdp'))
- grad_w_in: float32 [768, 3072], P(('seq', 'fsdp'))
- grad_b_in: float32 [3072], P(('seq', 'fsdp'))
- grad_w_back: float32 [3072, 768], P(('seq', 'fsdp'))
- grad_b_back: float32 [768], P(('seq', 'fsdp'))
- grad_norm2_gain: float32 [768], P(('seq', 'fsdp'))
- grad_norm2_bias: float32 [768], P(('seq', 'fsdp'))
- grad_w_relative: float32 [768, 12, 64], P('fsdp', 'seq')
- grad_bias_content: float32 [12, 64], P('seq', 'fsdp')
- grad_bias_position: float32 [12, 64], P('seq', 'fsdp')
- grad_bias_type: float32 [12, 64], P('seq', 'fsdp')
- grad_type_embed: float32 [2, 12, 64], P(None, 'seq', 'fsdp')
The draws below stay inside these ranges and needn't reach their ends.
Inputs may be any that keep to these rules, and one draw needn't show every extreme that they name: Each row holds the lengths of the 3 sequences of one pack, in order; a row sums to 1536 and its largest entry is 1024. Pack j is processed by fsdp index owners[j]; every index owns one pack.
All inputs are finite; a program needn't handle non-finite values.
Results may differ from the reference program's by a relative error of at most 0.017.
The reference program's roundings to bfloat16 on the way count: a program that leaves them out, or rounds other values in their place, can miss the bound.
Values may be sent and summed in bfloat16 or wider, within the bound.
No kernel may reach another device: no remote copies, remote signals or barrier semaphores. Data moves between devices by JAX's collectives and lax.ppermute only.
A program may use at most 192 MiB of HBM per device.

```python
import math
import jax
import jax.numpy as jnp
import numpy as np
from jax import lax

D = 768
HEADS = 12
DH = 64
FF = 3072
NSEG = 3
GRP = 1536
NPACK = 8
LONGEST = 1024


def touch_ends(array, key, smallest, high):
    extent = array.shape
    place = [jax.random.randint(jax.random.fold_in(key, axis), (), 0, extent[axis]) for axis in range(len(extent))]
    array = array.at[tuple(place)].set(smallest)
    longest = extent.index(max(extent))
    place[longest] = (place[longest] + 1) % extent[longest]
    return array.at[tuple(place)].set(high)


def block_scale(own_key, shape, pieces, least, high):
    level, own = 1.0, jax.random.fold_in(own_key, 6)
    for dim, shards_of in pieces:
        draws = jnp.exp(jax.random.uniform(jax.random.fold_in(own, dim), (shards_of,), jnp.float32, least / len(pieces), high / len(pieces)))
        level = level * jnp.repeat(draws, shape[dim] // shards_of).reshape([-1 if axis == dim else 1 for axis in range(len(shape))])
    return level


def length_profile(amount, total, limit, lean):
    weights = [(1 << 20) // math.isqrt(standing ** lean) + 1 for standing in range(2, amount + 1)]
    surplus, holding = total - limit - (amount - 1), [1] * (amount - 1)
    while surplus > 0:
        candidates = [i for i in range(amount - 1) if holding[i] < limit]
        whole, left = sum([weights[i] for i in candidates]), surplus
        for i in candidates:
            addition = min(limit - holding[i], max(1, left * weights[i] // whole), surplus)
            holding[i] = holding[i] + addition
            surplus = surplus - addition
    return np.array([limit] + holding)


def uneven(rng, count, total, most, skew):
    if count == 2:
        one = jax.random.randint(rng, (), max(1, total - most), min(most, total - 1) + 1)
        return jnp.stack([one, total - one])
    sizes = jnp.asarray(length_profile(count, total, most, skew), jnp.int32)
    couples = (count - 1) // 2
    source_of, taker = sizes[1:1 + 2 * couples:2], sizes[2:2 + 2 * couples:2]
    room = jnp.minimum(source_of - 1, most - taker)
    moved = jax.random.randint(jax.random.fold_in(rng, 1), (couples,), 0, 1 << 20) % (room + 1)
    sizes = sizes.at[1:1 + 2 * couples:2].set(source_of - moved).at[2:2 + 2 * couples:2].set(taker + moved)
    return sizes[jax.random.permutation(jax.random.fold_in(rng, 2), count)]


def scatter_about(stream_key, dims, deviation, limit, shards=(), held_as=jnp.bfloat16):
    drawn = jax.random.normal(stream_key, dims, jnp.float32) * deviation
    if len(shards) > 0:
        drawn = block_scale(stream_key, dims, shards, -0.22, 0.18) * drawn
    return jnp.clip(drawn, min=-limit, max=limit).astype(held_as)


def setup_inputs(seed: int = 0) -> dict:
    arg_keys = jax.random.split(jax.random.key(seed), 25)
    return {
        "inputs": scatter_about(arg_keys[0], (NPACK, GRP, D), 1.0, 6.0, ((1, 32),)),
        "w_query": scatter_about(arg_keys[1], (D, D), D ** -0.5, 0.21875, ((0, 8),)),
        "w_key": scatter_about(arg_keys[2], (D, D), D ** -0.5, 0.21875, ((0, 8),)),
        "w_value": scatter_about(arg_keys[3], (D, D), D ** -0.5, 0.21875, ((0, 8),)),
        "b_value": scatter_about(arg_keys[4], (D,), 0.5, 3.0, ((0, 8),)),
        "w_out": scatter_about(arg_keys[5], (D, D), (D // 8) ** -0.5, 0.625, ((0, 8),)),
        "b_out": scatter_about(arg_keys[6], (D,), 0.5, 3.0, ((0, 8),)),
        "norm1_gain": jnp.clip(1.0 + 0.18 * jax.random.normal(arg_keys[7], (D,), jnp.float32), 0.099609375, 1.8984375).astype(jnp.bfloat16),
        "norm1_bias": scatter_about(arg_keys[8], (D,), 0.5, 3.0, ((0, 8),)),
        "w_in": scatter_about(arg_keys[9], (D, FF), D ** -0.5, 0.21875, ((0, 8),)),
        "b_in": scatter_about(arg_keys[10], (FF,), 0.5, 3.0, ((0, 8),)),
        "w_back": scatter_about(arg_keys[11], (FF, D), (FF // 2) ** -0.5, 0.15625, ((0, 8),)),
        "b_back": scatter_about(arg_keys[12], (D,), 0.5, 3.0, ((0, 8),)),
        "norm2_gain": jnp.clip(1.0 + 0.18 * jax.random.normal(arg_keys[13], (D,), jnp.float32), 0.099609375, 1.8984375).astype(jnp.bfloat16),
        "norm2_bias": scatter_about(arg_keys[14], (D,), 0.5, 3.0, ((0, 8),)),
        "w_relative": scatter_about(arg_keys[15], (D, HEADS, DH), D ** -0.5, 0.21875, ((0, 8), (1, 4))),
        "bias_content": scatter_about(arg_keys[16], (HEADS, DH), 1.0, 5.0, ((0, 4), (1, 8))),
        "bias_position": scatter_about(arg_keys[17], (HEADS, DH), 1.0, 5.0, ((0, 4), (1, 8))),
        "bias_type": scatter_about(arg_keys[18], (HEADS, DH), 1.0, 5.0, ((0, 4), (1, 8))),
        "type_embed": scatter_about(arg_keys[19], (2, HEADS, DH), 1.0, 5.0, ((1, 4), (2, 8))),
        "lengths": jax.vmap(lambda own: uneven(own, NSEG, GRP, LONGEST, 1))(jax.random.split(arg_keys[20], NPACK)).reshape((NPACK, NSEG)).astype(jnp.int32),
        "token_types": touch_ends(jax.random.randint(arg_keys[21], (NPACK, GRP), 0, 2), jax.random.fold_in(arg_keys[21], 1), 0, 1).astype(jnp.int32),
        "owners": jax.random.permutation(arg_keys[22], NPACK).astype(jnp.int32),
        "grad_output": scatter_about(arg_keys[23], (NPACK, GRP, D), 1.0, 6.0, ((0, 8), (1, 4))),
    }


EPS = 1e-09
NEG = -1e+30
HIGH = lax.Precision.HIGHEST

@jax.custom_vjp
def low(v):
    return lax.optimization_barrier(v.astype(jnp.bfloat16)).astype(jnp.float32)

@jax.custom_vjp
def low_back(v):
    return v

def low_keep(v):
    return (low(v), None)

def low_pass(kept, grad):
    return (grad,)

def back_keep(v):
    return (v, None)

def back_low(kept, grad):
    return (low(grad),)
low.defvjp(low_keep, low_pass)
low_back.defvjp(back_keep, back_low)

def rounded(values):
    return low(low_back(values))

def norm_rows(values, gain_vec, shift_vec):
    center = values - lax.optimization_barrier(jnp.mean(values, axis=-1, keepdims=True))
    inverse = lax.rsqrt(lax.optimization_barrier(jnp.mean(center * center, axis=-1, keepdims=True)) + EPS)
    normed = center * inverse
    return normed * gain_vec + shift_vec

def pack_layout(seq_sizes, row_total):
    seq_sizes = seq_sizes.astype(jnp.int32)
    seq_ends = jnp.cumsum(seq_sizes).astype(jnp.int32)
    row_index = jnp.arange(row_total, dtype=jnp.int32)
    passed = (row_index[:, None] >= seq_ends[None, :]).astype(jnp.int32)
    segment = lax.optimization_barrier(jnp.sum(passed, axis=1)).astype(jnp.int32)
    start_row = lax.optimization_barrier(jnp.sum(passed * seq_sizes[None, :], axis=1)).astype(jnp.int32)
    return (segment, row_index - start_row)

def angles_of(position, width):
    half_width = width // 2
    rate_table = 10000.0 ** (-(jnp.arange(half_width, dtype=jnp.float32) / half_width))
    turned = position.astype(jnp.float32)[:, None] * rate_table[None, :]
    return (jnp.sin(turned), jnp.cos(turned))

def one_pack(params, pack_in, pack_types, pack_sizes):
    w_query, w_key, w_value, b_value, w_out, b_out, gain_one, shift_one, w_in, b_in, w_back, b_back, gain_two, shift_two, w_relative, bias_content, bias_position, bias_type, type_embed = params
    row_total = pack_in.shape[0]
    width = pack_in.shape[1]
    half_width = width // 2
    scale = DH ** (-0.5)
    segment, position = pack_layout(pack_sizes, row_total)
    query = rounded(jnp.dot(pack_in, w_query, precision=HIGH)).reshape(row_total, HEADS, DH)
    key_all = rounded(jnp.dot(pack_in, w_key, precision=HIGH)).reshape(row_total, HEADS, DH)
    value_all = rounded(jnp.dot(pack_in, w_value, precision=HIGH) + b_value).reshape(row_total, HEADS, DH)
    content_q = low((query + bias_content) * scale)
    position_q = low((query + bias_position) * scale)
    typed_q = (query + bias_type) * scale
    type_score = jnp.einsum('nhe,the->nht', typed_q, type_embed, precision=HIGH)
    rel_proj = low_back(jnp.einsum('nhe,dhe->nhd', position_q, w_relative, precision=HIGH))
    sine, cosine = angles_of(position, width)
    first_half = rel_proj[..., :half_width]
    second_half = rel_proj[..., half_width:]
    query_pos = low(jnp.concatenate([first_half * sine[:, None, :] + second_half * cosine[:, None, :], second_half * sine[:, None, :] - first_half * cosine[:, None, :]], axis=-1))
    key_pos = low(jnp.concatenate([cosine, sine], axis=-1))
    block_rows = min(512, row_total)
    block_count = row_total // block_rows

    def attend(start_row):
        block_cq = lax.dynamic_slice_in_dim(content_q, start_row, block_rows, 0)
        block_pq = lax.dynamic_slice_in_dim(query_pos, start_row, block_rows, 0)
        block_ts = lax.dynamic_slice_in_dim(type_score, start_row, block_rows, 0)
        block_kind = lax.dynamic_slice_in_dim(pack_types, start_row, block_rows, 0)
        block_part = lax.dynamic_slice_in_dim(segment, start_row, block_rows, 0)
        raw_score = jnp.einsum('ihe,jhe->hij', block_cq, key_all, precision=HIGH)
        raw_score = raw_score + jnp.einsum('ihd,jd->hij', block_pq, key_pos, precision=HIGH)
        same_kind = block_kind[:, None] == pack_types[None, :]
        raw_score = raw_score + jnp.where(same_kind[None], jnp.transpose(block_ts[..., 1])[:, :, None], jnp.transpose(block_ts[..., 0])[:, :, None])
        raw_score = low_back(raw_score)
        allowed = block_part[:, None] == segment[None, :]
        masked = jnp.where(allowed[None], raw_score, NEG)
        row_max = lax.optimization_barrier(jnp.max(masked, axis=-1, keepdims=True))
        exponent = jnp.exp(masked - row_max)
        row_total_sum = lax.optimization_barrier(jnp.sum(exponent, axis=-1, keepdims=True))
        probs = exponent / row_total_sum
        return jnp.einsum('hij,jhe->ihe', low(probs), value_all, precision=HIGH)
    starts = jnp.arange(block_count, dtype=jnp.int32) * block_rows
    mixed = lax.map(jax.checkpoint(attend), starts).reshape(row_total, width)
    attn_rows = rounded(mixed)
    branch = low_back(jnp.dot(attn_rows, w_out, precision=HIGH) + b_out)
    hidden_one = norm_rows(pack_in + branch, gain_one, shift_one)
    pre_act = low_back(jnp.dot(low(hidden_one), w_in, precision=HIGH) + b_in)
    act_low = low(jax.nn.gelu(pre_act))
    ffn_out = low_back(jnp.dot(act_low, w_back, precision=HIGH) + b_back)
    return norm_rows(hidden_one + ffn_out, gain_two, shift_two)

def reference(inputs, w_query, w_key, w_value, b_value, w_out, b_out, norm1_gain, norm1_bias, w_in, b_in, w_back, b_back, norm2_gain, norm2_bias, w_relative, bias_content, bias_position, bias_type, type_embed, lengths, token_types, owners, grad_output):
    params = tuple((member.astype(jnp.float32) for member in (w_query, w_key, w_value, b_value, w_out, b_out, norm1_gain, norm1_bias, w_in, b_in, w_back, b_back, norm2_gain, norm2_bias, w_relative, bias_content, bias_position, bias_type, type_embed)))
    owned_types = jnp.zeros_like(token_types).at[owners].set(token_types)
    owned_sizes = jnp.zeros_like(lengths).at[owners].set(lengths)

    def forward(flat_in, weights):
        owned = jnp.zeros_like(flat_in).at[owners].set(flat_in)

        def per_pack(carry, item):
            pack_in, pack_types, pack_sizes = item
            return (carry, one_pack(weights, pack_in, pack_types, pack_sizes))
        carry_zero = jnp.zeros((), jnp.float32)
        return lax.scan(jax.checkpoint(per_pack), carry_zero, (owned, owned_types, owned_sizes))[1]
    activations, pullback = jax.vjp(forward, inputs.astype(jnp.float32), params)
    input_grad, grads = pullback(grad_output.astype(jnp.float32))
    return (activations.astype(jnp.bfloat16), input_grad.astype(jnp.bfloat16), grads[0], grads[1], grads[2], grads[3], grads[4], grads[5], grads[6], grads[7], grads[8], grads[9], grads[10], grads[11], grads[12], grads[13], grads[14], grads[15], grads[16], grads[17], grads[18])
```

```python
import jax
import jax.numpy as jnp
from jax import lax
from jax.experimental import pallas as pl
from jax.experimental.pallas import tpu as pltpu
from jax.sharding import PartitionSpec as P

DH = 64
LONGEST = 1024
QB = 256
BLOCKED = -1e30
BF = jnp.bfloat16
F32 = jnp.float32
VM = pl.BlockSpec(memory_space=pltpu.VMEM)
SM = pl.BlockSpec(memory_space=pltpu.SMEM)
VMEM_LIMIT = 60 * 1024 * 1024


def lanes_of(rows, width=128):
    return lax.broadcasted_iota(jnp.int32, (rows, width), 1)


def split3(value):
    high = value.astype(BF).astype(F32)
    rest = value - high
    middle = rest.astype(BF).astype(F32)
    return high, middle, rest - middle


def pick(lane, first, columns, base):
    for number, column in enumerate(columns):
        base = jnp.where(lane == first + number, column, base)
    return base


def project_body(place, x0, x1, x2, x3, w_ref, head_ref, tcol_ref, qx_ref, pq_ref, kx_ref, kxt_ref, vx_ref, vxt_ref, rolled):
    own, start, near = place[0], place[1], place[2]
    scale = DH ** -0.5
    rows = qx_ref.shape[1]
    part = x0.shape[0]
    for number, piece in enumerate((x0, x1, x2, x3)):
        y = jnp.dot(piece[...], w_ref[...], preferred_element_type=F32)
        base = pl.multiple_of((own ^ number) * part, 8)
        for c in range(5):
            column = y[:, c * 128 : (c + 1) * 128]
            rolled[c, pl.ds(base, part), :] = column
            rolled[c, pl.ds(pl.multiple_of(base + rows, 8), part), :] = column

    def block(r, carry):
        row = pl.multiple_of(r * QB, QB)
        lane = lanes_of(QB)
        kind = tcol_ref[pl.ds(row, QB), :]
        index = row + lax.broadcasted_iota(jnp.int32, (QB, 1), 0)
        small = index >= LONGEST
        first = jnp.where(small & (index < LONGEST + near), 1.0, 0.0)
        second = jnp.where(small & (index >= LONGEST + near), 1.0, 0.0)
        one = jnp.where(kind == 1, 1.0, 0.0)
        zero = 1.0 - one
        for h in range(3):
            both = rolled[h, pl.ds(start + row, QB), :].astype(BF).astype(F32)
            if h < 2:
                v = rolled[3, pl.ds(start + row, QB), :]
                v = v if h == 0 else pltpu.roll(v, 64, 1)
            else:
                v = rolled[4, pl.ds(start + row, QB), :]
            head = head_ref[h]
            content = (both + head[0:1]) * scale
            position = ((both + head[1:2]) * scale).astype(BF)
            typed = (both + head[2:3]) * scale
            differ = jnp.sum(typed * head[3:4], axis=1, keepdims=True)
            same = jnp.sum(typed * head[4:5], axis=1, keepdims=True)
            for_zero = jnp.where(kind == 1, differ, same)
            for_one = jnp.where(kind == 1, same, differ)
            columns = [*split3(for_zero), *split3(for_one), second * BLOCKED, first * BLOCKED]
            qx = pick(lane, 64, columns, jnp.where(lane < 64, content, 0.0)).astype(BF)
            qx_ref[h, pl.ds(row, QB), :] = qx
            raw = pltpu.roll(both, 64, 1)
            pq_ref[h, pl.ds(row, QB), :] = jnp.where(lane < 64, position.astype(F32), raw).astype(BF)
            kx = pick(lane, 64, [zero, zero, zero, one, one, one, first, second], jnp.where(lane < 64, raw, 0.0))
            kx_ref[h, pl.ds(row, QB), :] = kx.astype(BF)
            kxt_ref[h, :, pl.ds(row, QB)] = jnp.transpose(kx, (1, 0)).astype(BF)
            vx = jnp.where(lane < 64, v + head[5:6], jnp.where(lane < 67, 1.0, 0.0)).astype(BF)
            vx_ref[h, pl.ds(row, QB), :] = vx
            vxt_ref[h, :, pl.ds(row, QB)] = jnp.transpose(vx.astype(F32), (1, 0)).astype(BF)
        return carry

    lax.fori_loop(0, rows // QB, block, 0)


def project(place, pieces, w_qkv, head, tcol):
    rows = 4 * pieces[0].shape[0]
    tall = jax.ShapeDtypeStruct((3, rows, 128), BF)
    wide = jax.ShapeDtypeStruct((3, 128, rows), BF)
    return pl.pallas_call(
        project_body,
        in_specs=[SM] + [VM] * 7,
        out_specs=[VM] * 6,
        out_shape=[tall, tall, tall, wide, tall, wide],
        scratch_shapes=[pltpu.VMEM((5, 2 * rows, 128), F32)],
        compiler_params=pltpu.CompilerParams(vmem_limit_bytes=VMEM_LIMIT),
        cost_estimate=pl.CostEstimate(flops=2 * rows * 768 * 640, bytes_accessed=10_000_000, transcendentals=0),
        name="project",
    )(place, *pieces, w_qkv, head, tcol)


def attend_body(place, qx_ref, pq_ref, kxt_ref, vx_ref, kpt_ref, wrt_ref, sn_ref, cs_ref, big_ref, small_ref, ox_ref, o0, o1, o2, o3, keys, left, outs):
    h, i = pl.program_id(0), pl.program_id(1)
    own, start = place[0], place[1]
    width = kpt_ref.shape[0]
    half = width // 2
    rows = kpt_ref.shape[1]

    @pl.when((h == 0) & (i == 0))
    def _():
        keys[0:width, :] = kpt_ref[...]

    @pl.when(i == 0)
    def _():
        keys[width:, :] = kxt_ref[0]

    rel = jnp.dot(pq_ref[0], wrt_ref[0], preferred_element_type=F32)
    r1, r2 = rel[:, :half], rel[:, half:]
    sn, cs = sn_ref[...], cs_ref[...]
    left[:, 0:half] = (r1 * sn + r2 * cs).astype(BF)
    left[:, half:width] = (r2 * sn - r1 * cs).astype(BF)
    left[:, width:] = qx_ref[0]

    def attend(low, high, store):
        score = jnp.dot(left[...], keys[:, low:high], preferred_element_type=F32)
        top = jnp.max(score, axis=1, keepdims=True)
        raised = jnp.exp(score - top).astype(BF)
        store[0] = raised
        mixed = jnp.dot(raised, vx_ref[0, low:high, :], preferred_element_type=F32)
        inverse = 1.0 / mixed[:, 64:65]
        lane = lanes_of(QB)
        ox = jnp.where(lane < 64, mixed * inverse, jnp.where(lane == 64, inverse, 0.0))
        ox_ref[0] = ox
        row = pl.multiple_of(i * QB, QB)
        outs[h, pl.ds(row, QB), :] = ox
        outs[h, pl.ds(pl.multiple_of(row + rows, QB), QB), :] = ox

    @pl.when(i < LONGEST // QB)
    def _():
        attend(0, LONGEST, big_ref)

    @pl.when(i >= LONGEST // QB)
    def _():
        attend(LONGEST, rows, small_ref)

    @pl.when((h == 2) & (i == pl.num_programs(1) - 1))
    def _():
        part = o0.shape[0]
        for number, out in enumerate((o0, o1, o2, o3)):
            at = lax.rem((own ^ number) * part + rows - start, rows)
            out[...] = jnp.concatenate([outs[g, pl.ds(at, part), :][:, 0:64] for g in range(3)], axis=1).astype(BF)


def attend(place, qx, pq, kxt, vx, kpt, wrt, sn, cs):
    rows = qx.shape[1]
    width = kpt.shape[0]
    blocks = rows // QB
    bigs = LONGEST // QB
    rest = rows - LONGEST
    per_block = lambda h, i: (h, i, 0)
    per_head = lambda h, i: (h, 0, 0)
    whole2 = lambda h, i: (0, 0)
    part = rows // 4
    out_piece = jax.ShapeDtypeStruct((part, 192), BF)
    return pl.pallas_call(
        attend_body,
        grid=(3, blocks),
        in_specs=[
            SM,
            pl.BlockSpec((1, QB, 128), per_block),
            pl.BlockSpec((1, QB, 128), per_block),
            pl.BlockSpec((1, 128, rows), per_head),
            pl.BlockSpec((1, rows, 128), per_head),
            pl.BlockSpec((width, rows), whole2, pipeline_mode=pl.Buffered(1)),
            pl.BlockSpec((1, 128, width), per_head),
            pl.BlockSpec((QB, width // 2), lambda h, i: (i, 0)),
            pl.BlockSpec((QB, width // 2), lambda h, i: (i, 0)),
        ],
        out_specs=[
            pl.BlockSpec((1, QB, LONGEST), lambda h, i: (h, jnp.minimum(i, bigs - 1), 0)),
            pl.BlockSpec((1, QB, rest), lambda h, i: (h, jnp.maximum(i - bigs, 0), 0)),
            pl.BlockSpec((1, QB, 128), per_block),
        ]
        + [pl.BlockSpec((part, 192), whole2)] * 4,
        out_shape=[
            jax.ShapeDtypeStruct((3, LONGEST, LONGEST), BF),
            jax.ShapeDtypeStruct((3, rest, rest), BF),
            jax.ShapeDtypeStruct((3, rows, 128), F32),
        ]
        + [out_piece] * 4,
        scratch_shapes=[
            pltpu.VMEM((width + 128, rows), BF),
            pltpu.VMEM((QB, width + 128), BF),
            pltpu.VMEM((3, 2 * rows, 128), F32),
        ],
        compiler_params=pltpu.CompilerParams(vmem_limit_bytes=VMEM_LIMIT, dimension_semantics=("arbitrary", "arbitrary")),
        cost_estimate=pl.CostEstimate(flops=12_000_000_000, bytes_accessed=20_000_000, transcendentals=4_000_000),
        name="attend",
    )(place, qx, pq, kxt, vx, kpt, wrt, sn, cs)


def back_body(place, d0, d1, d2, d3, big_ref, small_ref, ox_ref, qx_ref, pq_ref, kx_ref, vxt_ref, kp_ref, wr_ref, sn_ref, cs_ref, tcol_ref, head_ref, g0, g1, g2, g3, gw_ref, sum_ref, keys, douts, dkt, dvt, grads):
    h, i = pl.program_id(0), pl.program_id(1)
    own, start = place[0], place[1]
    rows, width = kp_ref.shape
    half = width // 2
    scale = DH ** -0.5
    part = d0.shape[0]
    last = pl.num_programs(1) - 1
    row = pl.multiple_of(i * QB, QB)
    again = pl.multiple_of(row + rows, QB)

    @pl.when((h == 0) & (i == 0))
    def _():
        keys[:, 0:width] = kp_ref[...]
        blank = jnp.zeros((part, 64), F32)
        for number, piece in enumerate((d0, d1, d2, d3)):
            values = piece[...].astype(F32)
            base = pl.multiple_of((own ^ number) * part, 8)
            for g in range(3):
                padded = jnp.concatenate([values[:, g * 64 : (g + 1) * 64], blank], axis=1)
                douts[g, pl.ds(base, part), :] = padded
                douts[g, pl.ds(pl.multiple_of(base + rows, 8), part), :] = padded

    @pl.when(i == 0)
    def _():
        keys[:, width:] = kx_ref[0]
        dkt[...] = jnp.zeros_like(dkt)
        dvt[...] = jnp.zeros_like(dvt)
        gw_ref[...] = jnp.zeros_like(gw_ref)
        sum_ref[...] = jnp.zeros_like(sum_ref)

    lane = lanes_of(QB)
    dout = douts[h, pl.ds(start + row, QB), :]
    ox = ox_ref[0]
    inverse = ox[:, 64:65]
    dot_row = jnp.sum(dout * ox, axis=1, keepdims=True)
    dox = pick(lane, 64, [-x for x in split3(dot_row)], dout).astype(BF)
    dout_t = jnp.transpose(dout * inverse, (1, 0))[0:64].astype(BF)
    qx = qx_ref[0]
    qc_t = jnp.transpose(qx.astype(F32), (1, 0))[0:64].astype(BF)
    pq = pq_ref[0].astype(F32)
    qp_t = jnp.transpose(pq, (1, 0))[0:64].astype(BF)
    sn, cs = sn_ref[...], cs_ref[...]

    def back(low, high, saved):
        raised = saved[0]
        dprob = jnp.dot(dox, vxt_ref[0, :, low:high], preferred_element_type=F32)
        dscore = (raised.astype(F32) * (dprob * inverse)).astype(BF)
        dvt[:, low:high] += jnp.dot(dout_t, raised, preferred_element_type=F32)
        dkt[:, low:high] += jnp.dot(qc_t, dscore, preferred_element_type=F32)
        dleft = jnp.dot(dscore, keys[low:high, :], preferred_element_type=F32)
        da1, da2 = dleft[:, 0:half], dleft[:, half:width]
        drel = jnp.concatenate([(da1 * sn - da2 * cs).astype(BF), (da1 * cs + da2 * sn).astype(BF)], axis=1)
        dqp = jnp.dot(drel, wr_ref[0], preferred_element_type=F32)
        gw_ref[0] += jnp.dot(qp_t, drel, preferred_element_type=F32)
        dqx = dleft[:, width:]
        kind = tcol_ref[...]
        over_zero, over_one = dqx[:, 64:65], dqx[:, 67:68]
        same = jnp.where(kind == 1, over_one, over_zero)
        differ = jnp.where(kind == 1, over_zero, over_one)
        head = head_ref[0]
        dqt = differ * head[3:4] + same * head[4:5]
        dqc = jnp.where(lane < 64, dqx, 0.0)
        dq = (dqc + dqp + dqt) * scale
        grads[h, pl.ds(row, QB), :] = dq
        typed = (pltpu.roll(pq, 64, 1) + head[2:3]) * scale
        sums = [dqc * scale, dqp * scale, dqt * scale, differ * typed, same * typed]
        for number, values in enumerate(sums):
            sum_ref[0, number : number + 1, :] += jnp.sum(values, axis=0, keepdims=True)

    @pl.when(i < LONGEST // QB)
    def _():
        back(0, LONGEST, big_ref)

    @pl.when(i >= LONGEST // QB)
    def _():
        back(LONGEST, rows, small_ref)

    @pl.when(i == last)
    def _():
        dk = jnp.transpose(dkt[...], (1, 0))
        dq = grads[h, 0:rows, :]
        pair = jnp.concatenate([dq[:, 0:64], dk], axis=1)
        grads[h, 0:rows, :] = pair
        grads[h, rows : 2 * rows, :] = pair
        dv = jnp.transpose(dvt[...], (1, 0)).astype(BF).astype(F32)
        sum_ref[0, 5:6, 0:64] = jnp.sum(dv, axis=0, keepdims=True)
        blank = jnp.zeros_like(dv)

        @pl.when(h == 0)
        def _():
            padded = jnp.concatenate([dv, blank], axis=1)
            grads[3, 0:rows, :] = padded
            grads[3, rows : 2 * rows, :] = padded

        @pl.when(h == 1)
        def _():
            padded = grads[3, 0:rows, :] + jnp.concatenate([blank, dv], axis=1)
            grads[3, 0:rows, :] = padded
            grads[3, rows : 2 * rows, :] = padded

        @pl.when(h == 2)
        def _():
            padded = jnp.concatenate([dv, blank], axis=1)
            grads[4, 0:rows, :] = padded
            grads[4, rows : 2 * rows, :] = padded
            for number, out in enumerate((g0, g1, g2, g3)):
                at = lax.rem((own ^ number) * part + rows - start, rows)
                for c in range(5):
                    out[:, c * 128 : (c + 1) * 128] = grads[c, pl.ds(at, part), :].astype(BF)


def attend_back(place, douts, big, small, ox, qx, pq, kx, vxt, kp, wr, sn, cs, tcol, head):
    rows, width = kp.shape
    blocks = rows // QB
    bigs = LONGEST // QB
    rest = rows - LONGEST
    part = rows // 4
    per_block = lambda h, i: (h, i, 0)
    per_head = lambda h, i: (h, 0, 0)
    whole2 = lambda h, i: (0, 0)
    return pl.pallas_call(
        back_body,
        grid=(3, blocks),
        in_specs=[SM]
        + [pl.BlockSpec((part, 192), whole2)] * 4
        + [
            pl.BlockSpec((1, QB, LONGEST), lambda h, i: (h, jnp.minimum(i, bigs - 1), 0)),
            pl.BlockSpec((1, QB, rest), lambda h, i: (h, jnp.maximum(i - bigs, 0), 0)),
            pl.BlockSpec((1, QB, 128), per_block),
            pl.BlockSpec((1, QB, 128), per_block),
            pl.BlockSpec((1, QB, 128), per_block),
            pl.BlockSpec((1, rows, 128), per_head),
            pl.BlockSpec((1, 128, rows), per_head),
            pl.BlockSpec((rows, width), whole2, pipeline_mode=pl.Buffered(1)),
            pl.BlockSpec((1, width, 128), per_head),
            pl.BlockSpec((QB, width // 2), lambda h, i: (i, 0)),
            pl.BlockSpec((QB, width // 2), lambda h, i: (i, 0)),
            pl.BlockSpec((QB, 1), lambda h, i: (i, 0)),
            pl.BlockSpec((1, 8, 128), per_head),
        ],
        out_specs=[pl.BlockSpec((part, 640), whole2)] * 4
        + [pl.BlockSpec((1, 64, width), per_head), pl.BlockSpec((1, 8, 128), per_head)],
        out_shape=[jax.ShapeDtypeStruct((part, 640), BF)] * 4
        + [jax.ShapeDtypeStruct((3, 64, width), F32), jax.ShapeDtypeStruct((3, 8, 128), F32)],
        scratch_shapes=[
            pltpu.VMEM((rows, width + 128), BF),
            pltpu.VMEM((3, 2 * rows, 128), F32),
            pltpu.VMEM((64, rows), F32),
            pltpu.VMEM((64, rows), F32),
            pltpu.VMEM((5, 2 * rows, 128), F32),
        ],
        compiler_params=pltpu.CompilerParams(vmem_limit_bytes=VMEM_LIMIT, dimension_semantics=("arbitrary", "arbitrary")),
        cost_estimate=pl.CostEstimate(flops=20_000_000_000, bytes_accessed=25_000_000, transcendentals=0),
        name="attend_back",
    )(place, *douts, big, small, ox, qx, pq, kx, vxt, kp, wr, sn, cs, tcol, head)


EPS = 1e-09
HIGH = lax.Precision.HIGHEST


def norm_rows(values, gain_vec, shift_vec):
    center = values - jnp.mean(values, axis=-1, keepdims=True)
    inverse = lax.rsqrt(jnp.mean(center * center, axis=-1, keepdims=True) + EPS)
    normed = center * inverse
    return (normed * gain_vec + shift_vec, normed, inverse)


def norm_back(gradient, normed, inverse, gain_vec):
    scaled = gradient * gain_vec
    inner_term = scaled - jnp.mean(scaled, axis=-1, keepdims=True)
    inner_term = inner_term - normed * jnp.mean(scaled * normed, axis=-1, keepdims=True)
    return (inner_term * inverse, jnp.sum(gradient * normed, axis=0), jnp.sum(gradient, axis=0))


def angles_of(position, width):
    half_width = width // 2
    rate_table = 10000.0 ** (-(jnp.arange(half_width, dtype=jnp.float32) / half_width))
    turned = position.astype(jnp.float32)[:, None] * rate_table[None, :]
    return (jnp.sin(turned), jnp.cos(turned))


def contract_rows(left, right):
    return lax.dot_general(
        left, right, (((0,), (0,)), ((), ())), preferred_element_type=jnp.float32
    )


def contract_cols(left, right):
    return lax.dot_general(
        left, right, (((1,), (1,)), ((), ())), preferred_element_type=jnp.float32
    )


def across(values, other):
    seqs, fsdps = lax.axis_size("seq"), lax.axis_size("fsdp")
    pairs = []
    for s in range(seqs):
        for f in range(fsdps):
            to_s, to_f = other(s, f)
            pairs.append((s * fsdps + f, to_s * fsdps + to_f))
    return lax.ppermute(values, ("seq", "fsdp"), pairs)


def to_core(values):
    return across(values, lambda s, f: (s, f ^ 1))


def to_first(values):
    return across(values, lambda s, f: (s ^ (2 if f & 1 else 1), f))


def to_second(values):
    return across(values, lambda s, f: (s ^ (1 if f & 1 else 2), f))


def to_near(values):
    return across(values, lambda s, f: (s, f ^ 2))


def to_far(values):
    return across(values, lambda s, f: (s, f ^ 4))


def to_seq(values, k):
    return across(values, lambda s, f: (s ^ k, f))


def halve(kept, got, hops):
    kept, got = kept.astype(F32), [got.astype(F32)]
    count = kept.shape[0]
    for hop in hops:
        count //= 2
        out = kept[count : 2 * count]
        for g in got:
            out = out + g[count : 2 * count]
        got.append(hop(out.astype(BF)).astype(F32))
    total = kept[0]
    for g in got:
        total = total + g[0]
    return total


def back_blocks_body(place, u_ref, df_ref, keep_ref, send_ref):
    core = lax.rem(place[0], 2)
    group = u_ref.shape[1] // 4
    for g in range(1):
        acc = lax.dot_general(u_ref[...], df_ref[...], (((0,), (0,)), ((), ())), preferred_element_type=F32)
        at = pl.program_id(0) * 4
        for j in range(4):
            slot = place[1 + at + j]
            value = acc[j * group : (j + 1) * group].astype(BF)

            @pl.when(core == j % 2)
            def _():
                keep_ref[slot] = value

            @pl.when(core != j % 2)
            def _():
                send_ref[slot] = value


def back_blocks(place, u, df):
    rows, hidden = u.shape
    width = df.shape[1]
    out = jax.ShapeDtypeStruct((16, hidden // 32, width), BF)
    return pl.pallas_call(
        back_blocks_body,
        grid=(8,),
        in_specs=[SM, pl.BlockSpec((rows, hidden // 8), lambda g: (0, g)), pl.BlockSpec((rows, width), lambda g: (0, 0))],
        out_specs=[pl.BlockSpec((16, hidden // 32, width), lambda g: (0, 0, 0))] * 2,
        out_shape=[out, out],
        compiler_params=pltpu.CompilerParams(vmem_limit_bytes=VMEM_LIMIT, dimension_semantics=("arbitrary",)),
        cost_estimate=pl.CostEstimate(flops=2 * rows * hidden * width, bytes_accessed=8_000_000, transcendentals=0),
        name="back_blocks",
    )(place, u, df)


def in_blocks_body(place, h_ref, dz_ref, a_ref, db_ref, vec_ref, keep_ref, send_ref):
    core = lax.rem(place[0], 2)
    own = lax.div(place[0], 8)
    step = pl.program_id(0)

    def put(block, odd, low, value):
        slot = place[1 + block]
        high = low + value.shape[0]

        @pl.when(core == odd)
        def _():
            keep_ref[slot, low:high, :] = value

        @pl.when(core != odd)
        def _():
            send_ref[slot, low:high, :] = value

    def chunk(which):
        for g in range(2):
            acc = lax.dot_general(
                h_ref[:, g * 384 : (g + 1) * 384], dz_ref[...], (((0,), (0,)), ((), ())), preferred_element_type=F32
            )
            for j in range(16):
                put(g * 16 + j, j % 2, which * 24, acc[j * 24 : (j + 1) * 24].astype(BF))

    for which in range(4):
        pl.when(step == which)(lambda which=which: chunk(which))

    @pl.when(step == 4)
    def _():
        for g in range(2):
            acc = lax.dot_general(
                a_ref[:, g * 384 : (g + 1) * 384], db_ref[...], (((0,), (0,)), ((), ())), preferred_element_type=F32
            )
            for j in range(16):
                block = (own ^ (2 * g + j // 8)) * 8 + j % 8
                put(block, j % 2, 96, acc[j * 24 : (j + 1) * 24].astype(BF))
        for j in range(32):
            put(j, j % 2, 120, vec_ref[j])


def in_blocks(place, hidden_low, dz, attn, dbr, vec):
    rows, width = hidden_low.shape
    chunks = dz.shape[1] // width
    out = jax.ShapeDtypeStruct((16, 128, width), BF)
    whole = pl.BlockSpec((rows, width), lambda g: (0, 0))
    return pl.pallas_call(
        in_blocks_body,
        grid=(chunks + 1,),
        in_specs=[
            SM,
            whole,
            pl.BlockSpec((rows, width), lambda g: (0, jnp.minimum(g, chunks - 1))),
            whole,
            whole,
            pl.BlockSpec((32, 8, width), lambda g: (0, 0, 0)),
        ],
        out_specs=[pl.BlockSpec((16, 128, width), lambda g: (0, 0, 0))] * 2,
        out_shape=[out, out],
        compiler_params=pltpu.CompilerParams(vmem_limit_bytes=VMEM_LIMIT, dimension_semantics=("arbitrary",)),
        cost_estimate=pl.CostEstimate(flops=2 * rows * width * (dz.shape[1] + width), bytes_accessed=12_000_000, transcendentals=0),
        name="in_blocks",
    )(place, hidden_low, dz, attn, dbr, vec)


def shards(
    inputs,
    w_query,
    w_key,
    w_value,
    b_value,
    w_out,
    b_out,
    norm1_gain,
    norm1_bias,
    w_in,
    b_in,
    w_back,
    b_back,
    norm2_gain,
    norm2_bias,
    w_relative,
    bias_content,
    bias_position,
    bias_type,
    type_embed,
    lengths,
    token_types,
    owners,
    grad_output,
):
    seqs, fsdps = lax.axis_size("seq"), lax.axis_size("fsdp")
    direct = seqs == 4 and fsdps == 8
    own, rank = lax.axis_index("seq"), lax.axis_index("fsdp")
    pack_count = owners.shape[0]
    sliver_rows = inputs.shape[1]
    width = inputs.shape[2]
    local_rows = w_query.shape[0]
    local_cols = width // seqs
    local_heads = w_relative.shape[1]
    scale = DH ** -0.5
    owner_table = owners[None, :] == jnp.arange(pack_count, dtype=jnp.int32)[:, None]
    owner_low = owner_table.astype(BF)
    dealt = jnp.dot(
        owner_low, inputs.reshape(pack_count, sliver_rows * width), preferred_element_type=F32
    )
    dealt = dealt.astype(BF).reshape(pack_count, sliver_rows, width)
    mine = lax.all_to_all(dealt, "fsdp", split_axis=0, concat_axis=1, tiled=True)[0]
    row_count = mine.shape[0]
    chosen = (owners == rank).astype(jnp.int32)
    pack_types = jnp.sum(chosen[:, None] * token_types, axis=0)
    pack_sizes = jnp.sum(chosen[:, None] * lengths, axis=0)
    pack_rows = pack_types.shape[0]

    def head_columns(weight):
        return lax.dynamic_slice_in_dim(weight, own * local_cols, local_cols, 1)

    paired = jnp.concatenate(
        [
            head_columns(w_query).reshape(local_rows, local_heads, DH),
            head_columns(w_key).reshape(local_rows, local_heads, DH),
        ],
        axis=2,
    ).reshape(local_rows, 2 * local_cols)
    block = jnp.concatenate(
        [paired, head_columns(w_value), w_relative.reshape(local_rows, local_cols)], axis=1
    )
    long_vectors = (b_value, b_out, norm1_gain, norm1_bias, b_back, norm2_gain, norm2_bias, b_in)
    head_vectors = (bias_content, bias_position, bias_type, type_embed)
    vector = jnp.concatenate([v.reshape(-1) for v in long_vectors + head_vectors])
    extra = -(-vector.shape[0] // width)
    extra = -(-extra // 8) * 8
    vector = jnp.pad(vector, (0, extra * width - vector.shape[0])).reshape(extra, width)
    early = lax.all_gather(jnp.concatenate([block, vector], axis=0), "fsdp", axis=0)
    qkvr = early[:, :local_rows].reshape(width, width)
    vectors = early[:, local_rows:].reshape(fsdps, extra * width).astype(F32)
    at, full = 0, []
    for v in long_vectors:
        full.append(vectors[:, at : at + v.shape[0]].reshape(-1))
        at += v.shape[0]
    bv_full, bo_full, gain_one, shift_one, bback_full, gain_two, shift_two, bin_full = full
    heads = []
    for v in head_vectors:
        each = vectors[:, at : at + v.size].reshape((fsdps,) + v.shape)
        heads.append(jnp.moveaxis(each, 0, -2).reshape(v.shape[:-1] + (DH,)))
        at += v.size
    content_full, position_full, typebias_full, embed_full = heads
    bv_own = lax.dynamic_slice_in_dim(bv_full, own * local_cols, local_cols, 0)
    head = jnp.stack(
        [
            content_full,
            position_full,
            typebias_full,
            embed_full[0],
            embed_full[1],
            bv_own.reshape(local_heads, DH),
        ],
        axis=1,
    )
    head = jnp.pad(head, ((0, 0), (0, 2), (0, 64)))

    def quarter(weight):
        rows = weight.shape[0] // seqs
        return lax.dynamic_slice_in_dim(weight, own * rows, rows, 0)

    def gather_all(weight):
        return lax.all_gather(quarter(weight), ("fsdp", "seq"), axis=0, tiled=True)

    wo_full = gather_all(w_out)
    win_full = gather_all(w_in)
    wback_full = gather_all(w_back)
    order = own ^ jnp.arange(seqs, dtype=jnp.int32)
    wo_near = jnp.take(wo_full.reshape(seqs, local_cols, width), order, axis=0).reshape(width, width)

    longest = jnp.argmax(pack_sizes).astype(jnp.int32)
    start = jnp.sum(jnp.where(jnp.arange(3) < longest, pack_sizes, 0))
    near = jnp.sum(jnp.where(jnp.arange(3) == (longest + 1) % 3, pack_sizes, 0))
    place = jnp.stack([own, start, near]).astype(jnp.int32)
    row_index = jnp.arange(pack_rows, dtype=jnp.int32)
    position = jnp.where(
        row_index < LONGEST,
        row_index,
        jnp.where(row_index < LONGEST + near, row_index - LONGEST, row_index - LONGEST - near),
    )
    sine, cosine = angles_of(position, width)
    key_pos = jnp.concatenate([cosine, sine], axis=-1).astype(BF)
    key_pos_t = key_pos.T
    turned_types = lax.dynamic_slice_in_dim(
        jnp.concatenate([pack_types, pack_types]), start, pack_rows, 0
    )[:, None]
    wrel = qkvr[:, 3 * local_cols :].reshape(width, local_heads, DH)
    wrel_rows = jnp.pad(jnp.transpose(wrel, (1, 0, 2)), ((0, 0), (0, 0), (0, 64)))
    wrel_cols = jnp.pad(jnp.transpose(wrel, (1, 2, 0)), ((0, 0), (0, 64), (0, 0)))
    w_qkv = qkvr[:, :640]

    pieces = [mine] + [to_seq(mine, k) for k in range(1, 4)]
    qx, pq, kx, kxt, vx, vxt = project(place, pieces, w_qkv, head, turned_types)
    big, small, ox, *head_out = attend(place, qx, pq, kxt, vx, key_pos_t, wrel_cols, sine, cosine)
    attn_rows = jnp.concatenate(
        [head_out[0]] + [to_seq(head_out[k], k) for k in range(1, 4)], axis=1
    )
    branch = jnp.dot(attn_rows, wo_near, preferred_element_type=F32) + bo_full
    first_sum = mine.astype(F32) + branch
    hidden_one, normed_one, inverse_one = norm_rows(first_sum, gain_one, shift_one)
    hidden_low = hidden_one.astype(BF)
    pre_act = jnp.dot(hidden_low, win_full, preferred_element_type=F32) + bin_full
    act_low = jax.nn.gelu(pre_act).astype(BF)
    ffn_out = jnp.dot(act_low, wback_full, preferred_element_type=F32) + bback_full
    second_sum = hidden_one + ffn_out
    result, normed_two, inverse_two = norm_rows(second_sum, gain_two, shift_two)
    activations = result.astype(BF).reshape(1, row_count, width)
    out_grad = grad_output[0].astype(F32)
    sum_two_grad, gain_two_grad, shift_two_grad = norm_back(
        out_grad, normed_two, inverse_two, gain_two
    )
    ffn_grad = sum_two_grad.astype(BF)
    back_bias_grad = jnp.sum(ffn_grad.astype(F32), axis=0)
    act_grad = contract_cols(ffn_grad, wback_full)
    pre_grad = jax.vjp(jax.nn.gelu, pre_act)[1](act_grad)[0].astype(BF)
    in_bias_grad = jnp.sum(pre_grad.astype(F32), axis=0)
    hidden_grad = sum_two_grad + contract_cols(pre_grad, win_full)
    sum_one_grad, gain_one_grad, shift_one_grad = norm_back(
        hidden_grad, normed_one, inverse_one, gain_one
    )
    branch_grad = sum_one_grad.astype(BF)
    out_bias_grad = jnp.sum(branch_grad.astype(F32), axis=0)
    attn_grad = contract_cols(branch_grad, wo_near).astype(BF)
    douts = [attn_grad[:, k * local_cols : (k + 1) * local_cols] for k in range(4)]
    douts = [douts[0]] + [to_seq(douts[k], k) for k in range(1, 4)]
    short = (gain_one_grad, shift_one_grad, gain_two_grad, shift_two_grad, out_bias_grad, back_bias_grad)
    devices = seqs * fsdps
    if direct:
        relative = jnp.arange(32, dtype=jnp.int32) ^ (own * 8 + rank)
        bit = lambda n: (relative >> n) & 1
        flip = (bit(0) ^ (rank & 1)) == 1
        slots = jnp.where(flip, bit(4), bit(3)) * 8 + jnp.where(flip, bit(3), bit(4)) * 4 + bit(1) * 2 + bit(2)
        table = jnp.concatenate([(own * 8 + rank)[None], slots]).astype(jnp.int32)
        hops = (to_first, to_second, to_near, to_far)
        kept, sent = back_blocks(table, act_low, ffn_grad)
        back_total = halve(kept, to_core(sent), hops)
        vec = jnp.concatenate(
            [v.reshape(32, -1) for v in short] + [in_bias_grad.reshape(32, -1)], axis=1
        )
        vec = jnp.pad(vec.astype(BF)[:, None, :], ((0, 0), (0, 7), (0, width - vec.shape[1])))
        kept, sent = in_blocks(table, hidden_low, pre_grad, attn_rows, branch_grad, vec)
        in_total = halve(kept, to_core(sent), hops)
        w_back_grad = back_total
        w_in_grad = jnp.concatenate([in_total[c * 24 : (c + 1) * 24] for c in range(4)], axis=1)
        w_out_grad = in_total[96:120]
        row = in_total[120]
        short_grads = [row[n * 24 : (n + 1) * 24] for n in range(6)]
        in_bias_grad = row[144:240]
    else:
        scatter = lambda v: lax.psum_scatter(v, ("seq", "fsdp"), scatter_dimension=0, tiled=True)
        w_back_grad = scatter(contract_rows(act_low, ffn_grad))
        w_in_grad = scatter(contract_rows(hidden_low, pre_grad))
        turned = contract_rows(attn_rows, branch_grad).reshape(seqs, local_cols, width)
        w_out_grad = scatter(jnp.take(turned, order, axis=0).reshape(width, width))
        short_grads = [scatter(v) for v in short]
        in_bias_grad = scatter(in_bias_grad)

    *turned, rel_grad, sums = attend_back(
        place, douts, big, small, ox, qx, pq, kx, vxt, key_pos, wrel_rows, sine, cosine, turned_types, head
    )
    dx = [contract_cols(t, w_qkv) for t in turned]
    input_rows = sum_one_grad + dx[0]
    for k in range(1, 4):
        input_rows = input_rows + to_seq(dx[k].astype(BF), k).astype(F32)
    input_rows = input_rows.astype(BF)
    returned = lax.all_to_all(
        input_rows.reshape(1, row_count, width), "fsdp", split_axis=1, concat_axis=0, tiled=True
    )
    input_grad = contract_rows(owner_low, returned.reshape(pack_count, sliver_rows * width))
    input_grad = input_grad.astype(BF).reshape(pack_count, sliver_rows, width)

    qkv_grad = contract_rows(jnp.concatenate(pieces, axis=0), jnp.concatenate(turned, axis=0))
    fine = width // devices
    qkv_grad = qkv_grad[:, : 3 * local_cols].reshape(seqs, fsdps, fine, 3 * local_cols)
    qkv_grad = jnp.transpose(qkv_grad, (1, 0, 2, 3)).reshape(fsdps, local_rows, 3 * local_cols)
    rel_grad = jnp.transpose(rel_grad, (2, 0, 1)).reshape(fsdps, local_rows, local_cols)
    sums = sums[:, :, :DH]
    eighth = DH // fsdps
    spread = lambda v, n: jnp.moveaxis(v.reshape(v.shape[:-1] + (fsdps, n)), -2, 0).reshape(fsdps, -1)
    vec = jnp.concatenate(
        [
            sums[:, 5].reshape(fsdps, fine),
            spread(sums[:, 0], eighth),
            spread(sums[:, 1], eighth),
            spread(sums[:, 2], eighth),
            spread(jnp.stack([sums[:, 3], sums[:, 4]]), eighth),
        ],
        axis=1,
    )
    vec = jnp.pad(vec[:, None, :], ((0, 0), (0, 7), (0, width - vec.shape[1])))
    bundle = jnp.concatenate([jnp.concatenate([qkv_grad, rel_grad], axis=2), vec], axis=1)
    if direct:
        count = jnp.arange(8, dtype=jnp.int32)
        wanted = rank ^ (((count >> 2) & 1) | (((count >> 1) & 1) << 1) | ((count & 1) << 2))
        bundle = jnp.take(bundle.astype(BF), wanted, axis=0)
        total = halve(bundle[:4], to_core(bundle[4:]), (to_near, to_far))
    else:
        total = lax.psum_scatter(bundle, "fsdp", scatter_dimension=0, tiled=True)[0]
    own_qkv = total[:local_rows, : 3 * local_cols].reshape(seqs, fine, 3 * local_cols).astype(BF)
    swapped = lax.all_to_all(own_qkv, "seq", split_axis=0, concat_axis=0, tiled=True).astype(F32)
    both = swapped[:, :, : 2 * local_cols].reshape(seqs, fine, local_heads, 2, DH)
    both = jnp.transpose(both, (3, 1, 0, 2, 4)).reshape(2, fine, width)
    w_value_grad = jnp.transpose(swapped[:, :, 2 * local_cols :], (1, 0, 2)).reshape(fine, width)
    rel_total = total[:local_rows, 3 * local_cols :].reshape(local_rows, local_heads, DH)
    row = total[local_rows]
    cut = local_heads * eighth
    value_bias_grad = row[:fine]
    bias_grads = [row[fine + n * cut : fine + (n + 1) * cut].reshape(local_heads, eighth) for n in range(3)]
    embed_grad = row[fine + 3 * cut : fine + 5 * cut].reshape(2, local_heads, eighth)
    return (
        activations,
        input_grad,
        both[0],
        both[1],
        w_value_grad,
        value_bias_grad,
        w_out_grad,
        short_grads[4],
        short_grads[0],
        short_grads[1],
        w_in_grad,
        in_bias_grad,
        w_back_grad,
        short_grads[5],
        short_grads[2],
        short_grads[3],
        rel_total,
        bias_grads[0],
        bias_grads[1],
        bias_grads[2],
        embed_grad,
    )


def solution(mesh):
    placed = (
        P(None, ("seq", "fsdp"), None),
        P("fsdp", None),
        P("fsdp", None),
        P("fsdp", None),
        P("fsdp"),
        P("fsdp", None),
        P("fsdp"),
        P("fsdp"),
        P("fsdp"),
        P("fsdp", None),
        P("fsdp"),
        P("fsdp", None),
        P("fsdp"),
        P("fsdp"),
        P("fsdp"),
        P("fsdp", "seq", None),
        P("seq", "fsdp"),
        P("seq", "fsdp"),
        P("seq", "fsdp"),
        P(None, "seq", "fsdp"),
        P(),
        P(),
        P(),
        P("fsdp", "seq", None),
    )
    return jax.shard_map(
        shards,
        mesh=mesh,
        in_specs=placed,
        out_specs=(
            P("fsdp", "seq", None),
            P(None, ("seq", "fsdp"), None),
            P(("seq", "fsdp"), None),
            P(("seq", "fsdp"), None),
            P(("seq", "fsdp"), None),
            P(("seq", "fsdp")),
            P(("seq", "fsdp"), None),
            P(("seq", "fsdp")),
            P(("seq", "fsdp")),
            P(("seq", "fsdp")),
            P(("seq", "fsdp"), None),
            P(("seq", "fsdp")),
            P(("seq", "fsdp"), None),
            P(("seq", "fsdp")),
            P(("seq", "fsdp")),
            P(("seq", "fsdp")),
            P("fsdp", "seq", None),
            P("seq", "fsdp"),
            P("seq", "fsdp"),
            P("seq", "fsdp"),
            P(None, "seq", "fsdp"),
        ),
        check_vma=False,
    )
```

```python
import jax
import jax.numpy as jnp
from jax import lax
from jax.experimental import pallas as pl
from jax.experimental.pallas import tpu as pltpu
from jax.sharding import PartitionSpec as P

DH = 64
LONGEST = 1024
QB = 256
BLOCKED = -1e30
BF = jnp.bfloat16
F32 = jnp.float32
VM = pl.BlockSpec(memory_space=pltpu.VMEM)
SM = pl.BlockSpec(memory_space=pltpu.SMEM)
VMEM_LIMIT = 60 * 1024 * 1024


def lanes_of(rows, width=128):
    return lax.broadcasted_iota(jnp.int32, (rows, width), 1)


def split3(value):
    high = value.astype(BF).astype(F32)
    rest = value - high
    middle = rest.astype(BF).astype(F32)
    return high, middle, rest - middle


def pick(lane, first, columns, base):
    for number, column in enumerate(columns):
        base = jnp.where(lane == first + number, column, base)
    return base


def project_body(place, x0, x1, x2, x3, w_ref, head_ref, tcol_ref, qx_ref, pq_ref, kx_ref, kxt_ref, vx_ref, vxt_ref, rolled):
    own, start, near = place[0], place[1], place[2]
    scale = DH ** -0.5
    rows = qx_ref.shape[1]
    part = x0.shape[0]
    for number, piece in enumerate((x0, x1, x2, x3)):
        y = jnp.dot(piece[...], w_ref[...], preferred_element_type=F32)
        base = pl.multiple_of((own ^ number) * part, 8)
        for c in range(5):
            column = y[:, c * 128 : (c + 1) * 128]
            rolled[c, pl.ds(base, part), :] = column
            rolled[c, pl.ds(pl.multiple_of(base + rows, 8), part), :] = column

    def block(r, carry):
        row = pl.multiple_of(r * QB, QB)
        lane = lanes_of(QB)
        kind = tcol_ref[pl.ds(row, QB), :]
        index = row + lax.broadcasted_iota(jnp.int32, (QB, 1), 0)
        small = index >= LONGEST
        first = jnp.where(small & (index < LONGEST + near), 1.0, 0.0)
        second = jnp.where(small & (index >= LONGEST + near), 1.0, 0.0)
        one = jnp.where(kind == 1, 1.0, 0.0)
        zero = 1.0 - one
        for h in range(3):
            both = rolled[h, pl.ds(start + row, QB), :].astype(BF).astype(F32)
            if h < 2:
                v = rolled[3, pl.ds(start + row, QB), :]
                v = v if h == 0 else pltpu.roll(v, 64, 1)
            else:
                v = rolled[4, pl.ds(start + row, QB), :]
            head = head_ref[h]
            content = (both + head[0:1]) * scale
            position = ((both + head[1:2]) * scale).astype(BF)
            typed = (both + head[2:3]) * scale
            differ = jnp.sum(typed * head[3:4], axis=1, keepdims=True)
            same = jnp.sum(typed * head[4:5], axis=1, keepdims=True)
            for_zero = jnp.where(kind == 1, differ, same)
            for_one = jnp.where(kind == 1, same, differ)
            columns = [*split3(for_zero), *split3(for_one), second * BLOCKED, first * BLOCKED]
            qx = pick(lane, 64, columns, jnp.where(lane < 64, content, 0.0)).astype(BF)
            qx_ref[h, pl.ds(row, QB), :] = qx
            raw = pltpu.roll(both, 64, 1)
            pq_ref[h, pl.ds(row, QB), :] = jnp.where(lane < 64, position.astype(F32), raw).astype(BF)
            kx = pick(lane, 64, [zero, zero, zero, one, one, one, first, second], jnp.where(lane < 64, raw, 0.0))
            kx_ref[h, pl.ds(row, QB), :] = kx.astype(BF)
            kxt_ref[h, :, pl.ds(row, QB)] = jnp.transpose(kx, (1, 0)).astype(BF)
            vx = jnp.where(lane < 64, v + head[5:6], jnp.where(lane < 67, 1.0, 0.0)).astype(BF)
            vx_ref[h, pl.ds(row, QB), :] = vx
            vxt_ref[h, :, pl.ds(row, QB)] = jnp.transpose(vx.astype(F32), (1, 0)).astype(BF)
        return carry

    lax.fori_loop(0, rows // QB, block, 0)


def project(place, pieces, w_qkv, head, tcol):
    rows = 4 * pieces[0].shape[0]
    tall = jax.ShapeDtypeStruct((3, rows, 128), BF)
    wide = jax.ShapeDtypeStruct((3, 128, rows), BF)
    return pl.pallas_call(
        project_body,
        in_specs=[SM] + [VM] * 7,
        out_specs=[VM] * 6,
        out_shape=[tall, tall, tall, wide, tall, wide],
        scratch_shapes=[pltpu.VMEM((5, 2 * rows, 128), F32)],
        compiler_params=pltpu.CompilerParams(vmem_limit_bytes=VMEM_LIMIT),
        cost_estimate=pl.CostEstimate(flops=2 * rows * 768 * 640, bytes_accessed=10_000_000, transcendentals=0),
        name="project",
    )(place, *pieces, w_qkv, head, tcol)


def attend_body(place, qx_ref, pq_ref, kxt_ref, vx_ref, kpt_ref, wrt_ref, sn_ref, cs_ref, big_ref, small_ref, ox_ref, o0, o1, o2, o3, keys, left, outs):
    h, i = pl.program_id(0), pl.program_id(1)
    own, start = place[0], place[1]
    width = kpt_ref.shape[0]
    half = width // 2
    rows = kpt_ref.shape[1]

    @pl.when((h == 0) & (i == 0))
    def _():
        keys[0:width, :] = kpt_ref[...]

    @pl.when(i == 0)
    def _():
        keys[width:, :] = kxt_ref[0]

    rel = jnp.dot(pq_ref[0], wrt_ref[0], preferred_element_type=F32)
    r1, r2 = rel[:, :half], rel[:, half:]
    sn, cs = sn_ref[...], cs_ref[...]
    left[:, 0:half] = (r1 * sn + r2 * cs).astype(BF)
    left[:, half:width] = (r2 * sn - r1 * cs).astype(BF)
    left[:, width:] = qx_ref[0]

    def attend(low, high, store):
        score = jnp.dot(left[...], keys[:, low:high], preferred_element_type=F32)
        top = jnp.max(score, axis=1, keepdims=True)
        raised = jnp.exp(score - top).astype(BF)
        store[0] = raised
        mixed = jnp.dot(raised, vx_ref[0, low:high, :], preferred_element_type=F32)
        inverse = 1.0 / mixed[:, 64:65]
        lane = lanes_of(QB)
        ox = jnp.where(lane < 64, mixed * inverse, jnp.where(lane == 64, inverse, 0.0))
        ox_ref[0] = ox
        row = pl.multiple_of(i * QB, QB)
        outs[h, pl.ds(row, QB), :] = ox
        outs[h, pl.ds(pl.multiple_of(row + rows, QB), QB), :] = ox

    @pl.when(i < LONGEST // QB)
    def _():
        attend(0, LONGEST, big_ref)

    @pl.when(i >= LONGEST // QB)
    def _():
        attend(LONGEST, rows, small_ref)

    @pl.when((h == 2) & (i == pl.num_programs(1) - 1))
    def _():
        part = o0.shape[0]
        for number, out in enumerate((o0, o1, o2, o3)):
            at = lax.rem((own ^ number) * part + rows - start, rows)
            out[...] = jnp.concatenate([outs[g, pl.ds(at, part), :][:, 0:64] for g in range(3)], axis=1).astype(BF)


def attend(place, qx, pq, kxt, vx, kpt, wrt, sn, cs):
    rows = qx.shape[1]
    width = kpt.shape[0]
    blocks = rows // QB
    bigs = LONGEST // QB
    rest = rows - LONGEST
    per_block = lambda h, i: (h, i, 0)
    per_head = lambda h, i: (h, 0, 0)
    whole2 = lambda h, i: (0, 0)
    part = rows // 4
    out_piece = jax.ShapeDtypeStruct((part, 192), BF)
    return pl.pallas_call(
        attend_body,
        grid=(3, blocks),
        in_specs=[
            SM,
            pl.BlockSpec((1, QB, 128), per_block),
            pl.BlockSpec((1, QB, 128), per_block),
            pl.BlockSpec((1, 128, rows), per_head),
            pl.BlockSpec((1, rows, 128), per_head),
            pl.BlockSpec((width, rows), whole2, pipeline_mode=pl.Buffered(1)),
            pl.BlockSpec((1, 128, width), per_head),
            pl.BlockSpec((QB, width // 2), lambda h, i: (i, 0)),
            pl.BlockSpec((QB, width // 2), lambda h, i: (i, 0)),
        ],
        out_specs=[
            pl.BlockSpec((1, QB, LONGEST), lambda h, i: (h, jnp.minimum(i, bigs - 1), 0)),
            pl.BlockSpec((1, QB, rest), lambda h, i: (h, jnp.maximum(i - bigs, 0), 0)),
            pl.BlockSpec((1, QB, 128), per_block),
        ]
        + [pl.BlockSpec((part, 192), whole2)] * 4,
        out_shape=[
            jax.ShapeDtypeStruct((3, LONGEST, LONGEST), BF),
            jax.ShapeDtypeStruct((3, rest, rest), BF),
            jax.ShapeDtypeStruct((3, rows, 128), F32),
        ]
        + [out_piece] * 4,
        scratch_shapes=[
            pltpu.VMEM((width + 128, rows), BF),
            pltpu.VMEM((QB, width + 128), BF),
            pltpu.VMEM((3, 2 * rows, 128), F32),
        ],
        compiler_params=pltpu.CompilerParams(vmem_limit_bytes=VMEM_LIMIT, dimension_semantics=("arbitrary", "arbitrary")),
        cost_estimate=pl.CostEstimate(flops=12_000_000_000, bytes_accessed=20_000_000, transcendentals=4_000_000),
        name="attend",
    )(place, qx, pq, kxt, vx, kpt, wrt, sn, cs)


def back_body(place, d0, d1, d2, d3, big_ref, small_ref, ox_ref, qx_ref, pq_ref, kx_ref, vxt_ref, kp_ref, wr_ref, sn_ref, cs_ref, tcol_ref, head_ref, g0, g1, g2, g3, gw_ref, sum_ref, keys, douts, dkt, dvt, grads):
    h, i = pl.program_id(0), pl.program_id(1)
    own, start = place[0], place[1]
    rows, width = kp_ref.shape
    half = width // 2
    scale = DH ** -0.5
    part = d0.shape[0]
    last = pl.num_programs(1) - 1
    row = pl.multiple_of(i * QB, QB)
    again = pl.multiple_of(row + rows, QB)

    @pl.when((h == 0) & (i == 0))
    def _():
        keys[:, 0:width] = kp_ref[...]
        blank = jnp.zeros((part, 64), F32)
        for number, piece in enumerate((d0, d1, d2, d3)):
            values = piece[...].astype(F32)
            base = pl.multiple_of((own ^ number) * part, 8)
            for g in range(3):
                padded = jnp.concatenate([values[:, g * 64 : (g + 1) * 64], blank], axis=1)
                douts[g, pl.ds(base, part), :] = padded
                douts[g, pl.ds(pl.multiple_of(base + rows, 8), part), :] = padded

    @pl.when(i == 0)
    def _():
        keys[:, width:] = kx_ref[0]
        dkt[...] = jnp.zeros_like(dkt)
        dvt[...] = jnp.zeros_like(dvt)
        gw_ref[...] = jnp.zeros_like(gw_ref)
        sum_ref[...] = jnp.zeros_like(sum_ref)

    lane = lanes_of(QB)
    dout = douts[h, pl.ds(start + row, QB), :]
    ox = ox_ref[0]
    inverse = ox[:, 64:65]
    dot_row = jnp.sum(dout * ox, axis=1, keepdims=True)
    dox = pick(lane, 64, [-x for x in split3(dot_row)], dout).astype(BF)
    dout_t = jnp.transpose(dout * inverse, (1, 0))[0:64].astype(BF)
    qx = qx_ref[0]
    qc_t = jnp.transpose(qx.astype(F32), (1, 0))[0:64].astype(BF)
    pq = pq_ref[0].astype(F32)
    qp_t = jnp.transpose(pq, (1, 0))[0:64].astype(BF)
    sn, cs = sn_ref[...], cs_ref[...]

    def back(low, high, saved):
        raised = saved[0]
        dprob = jnp.dot(dox, vxt_ref[0, :, low:high], preferred_element_type=F32)
        dscore = (raised.astype(F32) * (dprob * inverse)).astype(BF)
        dvt[:, low:high] += jnp.dot(dout_t, raised, preferred_element_type=F32)
        dkt[:, low:high] += jnp.dot(qc_t, dscore, preferred_element_type=F32)
        dleft = jnp.dot(dscore, keys[low:high, :], preferred_element_type=F32)
        da1, da2 = dleft[:, 0:half], dleft[:, half:width]
        drel = jnp.concatenate([(da1 * sn - da2 * cs).astype(BF), (da1 * cs + da2 * sn).astype(BF)], axis=1)
        dqp = jnp.dot(drel, wr_ref[0], preferred_element_type=F32)
        gw_ref[0] += jnp.dot(qp_t, drel, preferred_element_type=F32)
        dqx = dleft[:, width:]
        kind = tcol_ref[...]
        over_zero, over_one = dqx[:, 64:65], dqx[:, 67:68]
        same = jnp.where(kind == 1, over_one, over_zero)
        differ = jnp.where(kind == 1, over_zero, over_one)
        head = head_ref[0]
        dqt = differ * head[3:4] + same * head[4:5]
        dqc = jnp.where(lane < 64, dqx, 0.0)
        dq = (dqc + dqp + dqt) * scale
        grads[h, pl.ds(row, QB), :] = dq
        typed = (pltpu.roll(pq, 64, 1) + head[2:3]) * scale
        sums = [dqc * scale, dqp * scale, dqt * scale, differ * typed, same * typed]
        for number, values in enumerate(sums):
            sum_ref[0, number : number + 1, :] += jnp.sum(values, axis=0, keepdims=True)

    @pl.when(i < LONGEST // QB)
    def _():
        back(0, LONGEST, big_ref)

    @pl.when(i >= LONGEST // QB)
    def _():
        back(LONGEST, rows, small_ref)

    @pl.when(i == last)
    def _():
        dk = jnp.transpose(dkt[...], (1, 0))
        dq = grads[h, 0:rows, :]
        pair = jnp.concatenate([dq[:, 0:64], dk], axis=1)
        grads[h, 0:rows, :] = pair
        grads[h, rows : 2 * rows, :] = pair
        dv = jnp.transpose(dvt[...], (1, 0)).astype(BF).astype(F32)
        sum_ref[0, 5:6, 0:64] = jnp.sum(dv, axis=0, keepdims=True)
        blank = jnp.zeros_like(dv)

        @pl.when(h == 0)
        def _():
            padded = jnp.concatenate([dv, blank], axis=1)
            grads[3, 0:rows, :] = padded
            grads[3, rows : 2 * rows, :] = padded

        @pl.when(h == 1)
        def _():
            padded = grads[3, 0:rows, :] + jnp.concatenate([blank, dv], axis=1)
            grads[3, 0:rows, :] = padded
            grads[3, rows : 2 * rows, :] = padded

        @pl.when(h == 2)
        def _():
            padded = jnp.concatenate([dv, blank], axis=1)
            grads[4, 0:rows, :] = padded
            grads[4, rows : 2 * rows, :] = padded
            for number, out in enumerate((g0, g1, g2, g3)):
                at = lax.rem((own ^ number) * part + rows - start, rows)
                for c in range(5):
                    out[:, c * 128 : (c + 1) * 128] = grads[c, pl.ds(at, part), :].astype(BF)


def attend_back(place, douts, big, small, ox, qx, pq, kx, vxt, kp, wr, sn, cs, tcol, head):
    rows, width = kp.shape
    blocks = rows // QB
    bigs = LONGEST // QB
    rest = rows - LONGEST
    part = rows // 4
    per_block = lambda h, i: (h, i, 0)
    per_head = lambda h, i: (h, 0, 0)
    whole2 = lambda h, i: (0, 0)
    return pl.pallas_call(
        back_body,
        grid=(3, blocks),
        in_specs=[SM]
        + [pl.BlockSpec((part, 192), whole2)] * 4
        + [
            pl.BlockSpec((1, QB, LONGEST), lambda h, i: (h, jnp.minimum(i, bigs - 1), 0)),
            pl.BlockSpec((1, QB, rest), lambda h, i: (h, jnp.maximum(i - bigs, 0), 0)),
            pl.BlockSpec((1, QB, 128), per_block),
            pl.BlockSpec((1, QB, 128), per_block),
            pl.BlockSpec((1, QB, 128), per_block),
            pl.BlockSpec((1, rows, 128), per_head),
            pl.BlockSpec((1, 128, rows), per_head),
            pl.BlockSpec((rows, width), whole2, pipeline_mode=pl.Buffered(1)),
            pl.BlockSpec((1, width, 128), per_head),
            pl.BlockSpec((QB, width // 2), lambda h, i: (i, 0)),
            pl.BlockSpec((QB, width // 2), lambda h, i: (i, 0)),
            pl.BlockSpec((QB, 1), lambda h, i: (i, 0)),
            pl.BlockSpec((1, 8, 128), per_head),
        ],
        out_specs=[pl.BlockSpec((part, 640), whole2)] * 4
        + [pl.BlockSpec((1, 64, width), per_head), pl.BlockSpec((1, 8, 128), per_head)],
        out_shape=[jax.ShapeDtypeStruct((part, 640), BF)] * 4
        + [jax.ShapeDtypeStruct((3, 64, width), F32), jax.ShapeDtypeStruct((3, 8, 128), F32)],
        scratch_shapes=[
            pltpu.VMEM((rows, width + 128), BF),
            pltpu.VMEM((3, 2 * rows, 128), F32),
            pltpu.VMEM((64, rows), F32),
            pltpu.VMEM((64, rows), F32),
            pltpu.VMEM((5, 2 * rows, 128), F32),
        ],
        compiler_params=pltpu.CompilerParams(vmem_limit_bytes=VMEM_LIMIT, dimension_semantics=("arbitrary", "arbitrary")),
        cost_estimate=pl.CostEstimate(flops=20_000_000_000, bytes_accessed=25_000_000, transcendentals=0),
        name="attend_back",
    )(place, *douts, big, small, ox, qx, pq, kx, vxt, kp, wr, sn, cs, tcol, head)


EPS = 1e-09
GELU_A = (2.0 / 3.141592653589793) ** 0.5
GELU_B = 0.044715

def spread_norm(values):
    center = values - jnp.mean(values, axis=1, keepdims=True)
    inverse = lax.rsqrt(jnp.mean(center * center, axis=1, keepdims=True) + EPS)
    return center * inverse, inverse


def middle_body(
    place, a0, a1, a2, a3, x_ref, go_ref, w_ref, vec_ref, bin_ref,
    act_ref, h_ref, u_ref, dz_ref, df_ref, dbr_ref, dr_ref, d0, d1, d2, d3, sum_ref, dbin_ref,
    wout, slope, high, normed, acc,
):
    own = place[0]
    width = x_ref.shape[1]
    cols = a0.shape[1]
    vector = lambda n: vec_ref[n : n + 1, :]
    for s in range(4):
        piece = w_ref[:, s, :, 2 * width : 2 * width + cols]
        wout[:, s * cols : (s + 1) * cols] = piece.reshape(width, cols)
    part = lambda k: wout[pl.ds(pl.multiple_of((own ^ k) * cols, 64), cols), :]
    total = x_ref[...].astype(F32) + vector(0)
    for k, piece in enumerate((a0, a1, a2, a3)):
        total = total + jnp.dot(piece[...], part(k), preferred_element_type=F32)
    unit, inverse_one = spread_norm(total)
    normed[...] = unit
    first = unit * vector(1) + vector(2)
    high[...] = first
    h_ref[...] = first.astype(BF)
    acc[...] = first + vector(3)

    def w_in_at(w):
        return w_ref[:, w, :, 0:width].reshape(width, width)

    def w_back_at(w):
        return w_ref[pl.ds(2 * w, 2), :, :, width : 2 * width].reshape(width, width)

    def forward(w, carry):
        at = pl.multiple_of(w * width, 128)
        z = jnp.dot(h_ref[...], w_in_at(w), preferred_element_type=F32) + bin_ref[:, pl.ds(at, width)]
        square = z * z
        bend = jnp.tanh(GELU_A * z * (1.0 + GELU_B * square))
        half = 0.5 + 0.5 * bend
        u = (z * half).astype(BF)
        u_ref[:, pl.ds(at, width)] = u
        slope[:, pl.ds(at, width)] = half + 0.5 * z * (1.0 - bend * bend) * (GELU_A * (1.0 + 3.0 * GELU_B * square))
        acc[...] += jnp.dot(u, w_back_at(w), preferred_element_type=F32)
        return carry

    lax.fori_loop(0, 4, forward, 0)
    unit, inverse_two = spread_norm(acc[...])
    act_ref[...] = (unit * vector(4) + vector(5)).astype(BF)

    def back(gradient, unit, inverse, gain):
        scaled = gradient * gain
        inner = scaled - jnp.mean(scaled, axis=1, keepdims=True)
        return (inner - unit * jnp.mean(scaled * unit, axis=1, keepdims=True)) * inverse

    def note(row, values):
        sum_ref[row : row + 1, :] = jnp.sum(values, axis=0, keepdims=True)

    gradient = go_ref[...].astype(F32)
    note(2, gradient * unit)
    note(3, gradient)
    second = back(gradient, unit, inverse_two, vector(4))
    df = second.astype(BF)
    df_ref[...] = df
    note(5, df.astype(F32))
    acc[...] = second

    def backward(w, carry):
        at = pl.multiple_of(w * width, 128)
        du = lax.dot_general(df_ref[...], w_back_at(w), (((1,), (1,)), ((), ())), preferred_element_type=F32)
        dz = (slope[:, pl.ds(at, width)] * du).astype(BF)
        dz_ref[:, pl.ds(at, width)] = dz
        dbin_ref[0:1, pl.ds(at, width)] = jnp.sum(dz.astype(F32), axis=0, keepdims=True)
        acc[...] += lax.dot_general(dz, w_in_at(w), (((1,), (1,)), ((), ())), preferred_element_type=F32)
        return carry

    lax.fori_loop(0, 4, backward, 0)
    gradient = acc[...]
    unit = normed[...]
    note(0, gradient * unit)
    note(1, gradient)
    dr = back(gradient, unit, inverse_one, vector(1))
    dr_ref[...] = dr
    dbr = dr.astype(BF)
    dbr_ref[...] = dbr
    note(4, dbr.astype(F32))
    sum_ref[6:8, :] = jnp.zeros((2, width), F32)
    for k, out in enumerate((d0, d1, d2, d3)):
        value = lax.dot_general(dbr, part(k), (((1,), (1,)), ((), ())), preferred_element_type=F32)
        out[...] = value.astype(BF)


def middle(place, pieces, x, out_grad, weights, vectors, bin_full):
    rows, width = x.shape
    cols = pieces[0].shape[1]
    hidden = bin_full.shape[1]
    low = lambda n: jax.ShapeDtypeStruct((rows, n), BF)
    full = lambda r, n: jax.ShapeDtypeStruct((r, n), F32)
    return pl.pallas_call(
        middle_body,
        in_specs=[SM] + [VM] * 9,
        out_specs=[VM] * 13,
        out_shape=[low(width), low(width), low(hidden), low(hidden), low(width), low(width), full(rows, width)]
        + [low(cols)] * 4
        + [full(8, width), full(1, hidden)],
        scratch_shapes=[
            pltpu.VMEM((width, width), BF),
            pltpu.VMEM((rows, hidden), F32),
            pltpu.VMEM((rows, width), F32),
            pltpu.VMEM((rows, width), F32),
            pltpu.VMEM((rows, width), F32),
        ],
        compiler_params=pltpu.CompilerParams(vmem_limit_bytes=VMEM_LIMIT),
        cost_estimate=pl.CostEstimate(flops=8_000_000_000, bytes_accessed=20_000_000, transcendentals=1_000_000),
        name="middle",
    )(place, *pieces, x, out_grad, weights, vectors, bin_full)


def angles_of(position, width):
    half_width = width // 2
    rate_table = 10000.0 ** (-(jnp.arange(half_width, dtype=jnp.float32) / half_width))
    turned = position.astype(jnp.float32)[:, None] * rate_table[None, :]
    return (jnp.sin(turned), jnp.cos(turned))


def contract_rows(left, right):
    return lax.dot_general(
        left, right, (((0,), (0,)), ((), ())), preferred_element_type=jnp.float32
    )


def contract_cols(left, right):
    return lax.dot_general(
        left, right, (((1,), (1,)), ((), ())), preferred_element_type=jnp.float32
    )


def across(values, other):
    seqs, fsdps = lax.axis_size("seq"), lax.axis_size("fsdp")
    pairs = []
    for s in range(seqs):
        for f in range(fsdps):
            to_s, to_f = other(s, f)
            pairs.append((s * fsdps + f, to_s * fsdps + to_f))
    return lax.ppermute(values, ("seq", "fsdp"), pairs)


def to_core(values):
    return across(values, lambda s, f: (s, f ^ 1))


def to_first(values):
    return across(values, lambda s, f: (s ^ (2 if f & 1 else 1), f))


def to_second(values):
    return across(values, lambda s, f: (s ^ (1 if f & 1 else 2), f))


def to_near(values):
    return across(values, lambda s, f: (s, f ^ 2))


def to_far(values):
    return across(values, lambda s, f: (s, f ^ 4))


def to_seq(values, k):
    return across(values, lambda s, f: (s ^ k, f))


def add_parts(parts, low, high):
    total = parts[0][low:high].astype(F32)
    for part in parts[1:]:
        total = total + part[low:high].astype(F32)
    return total


def halve(parts, count, hops):
    for hop in hops:
        count //= 2
        parts = parts + [hop(add_parts(parts, count, 2 * count).astype(BF))]
    return add_parts(parts, 0, 1)[0]


def back_blocks_body(place, u_ref, df_ref, keep_ref, send_ref):
    core = lax.rem(place[0], 2)
    group = u_ref.shape[1] // 4
    for g in range(1):
        acc = lax.dot_general(u_ref[...], df_ref[...], (((0,), (0,)), ((), ())), preferred_element_type=F32)
        at = pl.program_id(0) * 4
        for j in range(4):
            slot = place[1 + at + j]
            value = acc[j * group : (j + 1) * group].astype(BF)

            @pl.when(core == j % 2)
            def _():
                keep_ref[slot] = value

            @pl.when(core != j % 2)
            def _():
                send_ref[slot] = value


def back_blocks(place, u, df):
    rows, hidden = u.shape
    width = df.shape[1]
    out = jax.ShapeDtypeStruct((16, hidden // 32, width), BF)
    return pl.pallas_call(
        back_blocks_body,
        grid=(8,),
        in_specs=[SM, pl.BlockSpec((rows, hidden // 8), lambda g: (0, g)), pl.BlockSpec((rows, width), lambda g: (0, 0))],
        out_specs=[pl.BlockSpec((16, hidden // 32, width), lambda g: (0, 0, 0))] * 2,
        out_shape=[out, out],
        compiler_params=pltpu.CompilerParams(vmem_limit_bytes=VMEM_LIMIT, dimension_semantics=("arbitrary",)),
        cost_estimate=pl.CostEstimate(flops=2 * rows * hidden * width, bytes_accessed=8_000_000, transcendentals=0),
        name="back_blocks",
    )(place, u, df)


def in_blocks_body(place, h_ref, dz_ref, a_ref, db_ref, vec_ref, keep_ref, send_ref):
    core = lax.rem(place[0], 2)
    own = lax.div(place[0], 8)
    step = pl.program_id(0)

    def put(block, odd, low, value):
        slot = place[1 + block]
        high = low + value.shape[0]

        @pl.when(core == odd)
        def _():
            keep_ref[slot, low:high, :] = value

        @pl.when(core != odd)
        def _():
            send_ref[slot, low:high, :] = value

    def chunk(which):
        for g in range(2):
            acc = lax.dot_general(
                h_ref[:, g * 384 : (g + 1) * 384], dz_ref[...], (((0,), (0,)), ((), ())), preferred_element_type=F32
            )
            for j in range(16):
                put(g * 16 + j, j % 2, which * 24, acc[j * 24 : (j + 1) * 24].astype(BF))

    for which in range(4):
        pl.when(step == which)(lambda which=which: chunk(which))

    @pl.when(step == 4)
    def _():
        for g in range(2):
            acc = lax.dot_general(
                a_ref[:, g * 384 : (g + 1) * 384], db_ref[...], (((0,), (0,)), ((), ())), preferred_element_type=F32
            )
            for j in range(16):
                block = (own ^ (2 * g + j // 8)) * 8 + j % 8
                put(block, j % 2, 96, acc[j * 24 : (j + 1) * 24].astype(BF))
        for j in range(32):
            put(j, j % 2, 120, vec_ref[j])


def in_blocks(place, hidden_low, dz, attn, dbr, vec):
    rows, width = hidden_low.shape
    chunks = dz.shape[1] // width
    out = jax.ShapeDtypeStruct((16, 128, width), BF)
    whole = pl.BlockSpec((rows, width), lambda g: (0, 0))
    return pl.pallas_call(
        in_blocks_body,
        grid=(chunks + 1,),
        in_specs=[
            SM,
            whole,
            pl.BlockSpec((rows, width), lambda g: (0, jnp.minimum(g, chunks - 1))),
            whole,
            whole,
            pl.BlockSpec((32, 8, width), lambda g: (0, 0, 0)),
        ],
        out_specs=[pl.BlockSpec((16, 128, width), lambda g: (0, 0, 0))] * 2,
        out_shape=[out, out],
        compiler_params=pltpu.CompilerParams(vmem_limit_bytes=VMEM_LIMIT, dimension_semantics=("arbitrary",)),
        cost_estimate=pl.CostEstimate(flops=2 * rows * width * (dz.shape[1] + width), bytes_accessed=12_000_000, transcendentals=0),
        name="in_blocks",
    )(place, hidden_low, dz, attn, dbr, vec)


def shards(
    inputs,
    w_query,
    w_key,
    w_value,
    b_value,
    w_out,
    b_out,
    norm1_gain,
    norm1_bias,
    w_in,
    b_in,
    w_back,
    b_back,
    norm2_gain,
    norm2_bias,
    w_relative,
    bias_content,
    bias_position,
    bias_type,
    type_embed,
    lengths,
    token_types,
    owners,
    grad_output,
):
    seqs, fsdps = lax.axis_size("seq"), lax.axis_size("fsdp")
    direct = seqs == 4 and fsdps == 8
    own, rank = lax.axis_index("seq"), lax.axis_index("fsdp")
    pack_count = owners.shape[0]
    sliver_rows = inputs.shape[1]
    width = inputs.shape[2]
    local_rows = w_query.shape[0]
    local_cols = width // seqs
    local_heads = w_relative.shape[1]
    scale = DH ** -0.5
    owner_table = owners[None, :] == jnp.arange(pack_count, dtype=jnp.int32)[:, None]
    owner_low = owner_table.astype(BF)
    dealt = jnp.dot(
        owner_low, inputs.reshape(pack_count, sliver_rows * width), preferred_element_type=F32
    )
    dealt = dealt.astype(BF).reshape(pack_count, sliver_rows, width)
    mine = lax.all_to_all(dealt, "fsdp", split_axis=0, concat_axis=1, tiled=True)[0]
    row_count = mine.shape[0]
    chosen = (owners == rank).astype(jnp.int32)
    pack_types = jnp.sum(chosen[:, None] * token_types, axis=0)
    pack_sizes = jnp.sum(chosen[:, None] * lengths, axis=0)
    pack_rows = pack_types.shape[0]

    def head_columns(weight):
        return lax.dynamic_slice_in_dim(weight, own * local_cols, local_cols, 1)

    block = jnp.concatenate(
        [head_columns(w) for w in (w_query, w_key, w_value)] + [w_relative.reshape(local_rows, local_cols)], axis=1
    )
    long_vectors = (b_value, b_out, norm1_gain, norm1_bias, b_back, norm2_gain, norm2_bias, b_in)
    head_vectors = (bias_content, bias_position, bias_type, type_embed[0], type_embed[1])

    def placed_at(value, row, lane):
        value = value.reshape(-1, value.shape[-1])
        return jnp.pad(value, ((row, 8 - row - value.shape[0]), (lane, width - lane - value.shape[1])))

    corner = placed_at(b_value, 0, 0)
    for number, value in enumerate(long_vectors[1:]):
        corner = corner + placed_at(value, number + 1, 0)
    for number, value in enumerate(head_vectors[:3]):
        corner = corner + placed_at(value, 0, (number + 3) * 128)
    for number, value in enumerate(head_vectors[3:]):
        corner = corner + placed_at(value, 3, (number + 3) * 128)
    early = lax.all_gather(jnp.concatenate([block, corner], axis=0), "fsdp", axis=0)
    qkvr = early[:, :local_rows].reshape(width, width)
    corners = early[:, local_rows:].astype(F32)
    full = [corners[:, n, : v.shape[0]].reshape(-1) for n, v in enumerate(long_vectors)]
    bv_full, bo_full, gain_one, shift_one, bback_full, gain_two, shift_two, bin_full = full
    heads = []
    for number, value in enumerate(head_vectors):
        row = 0 if number < 3 else 3
        lane = (number % 3 + 3) * 128
        each = corners[:, row : row + local_heads, lane : lane + value.shape[1]]
        heads.append(jnp.moveaxis(each, 0, 1).reshape(local_heads, DH))
    content_full, position_full, typebias_full, embed_zero, embed_one = heads
    bv_own = lax.dynamic_slice_in_dim(bv_full, own * local_cols, local_cols, 0)
    head = jnp.stack(
        [
            content_full,
            position_full,
            typebias_full,
            embed_zero,
            embed_one,
            bv_own.reshape(local_heads, DH),
        ],
        axis=1,
    )
    head = jnp.pad(head, ((0, 0), (0, 2), (0, 64)))

    deep = w_back.shape[0] // seqs
    late = jnp.concatenate(
        [
            lax.dynamic_slice_in_dim(w_in, own * width, width, 1),
            lax.dynamic_slice_in_dim(w_back, own * deep, deep, 0),
            head_columns(w_out),
            jnp.zeros((local_rows, 64), BF),
        ],
        axis=1,
    )
    late = lax.all_gather(late, ("fsdp", "seq"), axis=0).reshape(fsdps, seqs, local_rows, -1)
    if not direct:
        eighth_rows = width // 8
        turned_in = jnp.swapaxes(late, 1, 2).reshape(8, eighth_rows, seqs, -1)
        natural = late[..., width : 2 * width].reshape(8, seqs, eighth_rows, width)
        turned_in = jnp.swapaxes(turned_in, 1, 2)
        late = jnp.concatenate([turned_in[..., :width], natural, turned_in[..., 2 * width :]], axis=-1)

    longest = jnp.argmax(pack_sizes).astype(jnp.int32)
    start = jnp.sum(jnp.where(jnp.arange(3) < longest, pack_sizes, 0))
    near = jnp.sum(jnp.where(jnp.arange(3) == (longest + 1) % 3, pack_sizes, 0))
    place = jnp.stack([own, start, near]).astype(jnp.int32)
    row_index = jnp.arange(pack_rows, dtype=jnp.int32)
    position = jnp.where(
        row_index < LONGEST,
        row_index,
        jnp.where(row_index < LONGEST + near, row_index - LONGEST, row_index - LONGEST - near),
    )
    sine, cosine = angles_of(position, width)
    key_pos = jnp.concatenate([cosine, sine], axis=-1).astype(BF)
    key_pos_t = key_pos.T
    turned_types = lax.dynamic_slice_in_dim(
        jnp.concatenate([pack_types, pack_types]), start, pack_rows, 0
    )[:, None]
    wrel = qkvr[:, 3 * local_cols :].reshape(width, local_heads, DH)
    wrel_rows = jnp.pad(jnp.transpose(wrel, (1, 0, 2)), ((0, 0), (0, 0), (0, 64)))
    wrel_cols = jnp.pad(jnp.transpose(wrel, (1, 2, 0)), ((0, 0), (0, 64), (0, 0)))
    together = lambda n: qkvr[:, n * local_cols : (n + 1) * local_cols].reshape(width, local_heads, DH)
    paired = jnp.concatenate([together(0), together(1)], axis=2).reshape(width, 2 * local_cols)
    w_qkv = jnp.concatenate([paired, qkvr[:, 2 * local_cols : 3 * local_cols], jnp.zeros((width, 64), BF)], axis=1)

    pieces = [mine] + [to_seq(mine, k) for k in range(1, 4)]
    qx, pq, kx, kxt, vx, vxt = project(place, pieces, w_qkv, head, turned_types)
    big, small, ox, *head_out = attend(place, qx, pq, kxt, vx, key_pos_t, wrel_cols, sine, cosine)
    order = own ^ jnp.arange(seqs, dtype=jnp.int32)
    attn = [head_out[0]] + [to_seq(head_out[k], k) for k in range(1, 4)]
    mid_vectors = jnp.stack([bo_full, gain_one, shift_one, bback_full, gain_two, shift_two, gain_two, gain_two])
    result, hidden_low, act_low, pre_grad, ffn_grad, branch_grad, sum_one_grad, *rest = middle(
        place, attn, mine, grad_output[0], late, mid_vectors, bin_full[None]
    )
    douts, short_sums, in_bias_grad = rest[:4], rest[4], rest[5]
    activations = result.reshape(1, row_count, width)
    douts = [douts[0]] + [to_seq(douts[k], k) for k in range(1, 4)]
    attn_rows = jnp.concatenate(attn, axis=1)
    short = [short_sums[n] for n in range(6)]
    in_bias_grad = in_bias_grad[0]
    devices = seqs * fsdps
    if direct:
        relative = jnp.arange(32, dtype=jnp.int32) ^ (own * 8 + rank)
        bit = lambda n: (relative >> n) & 1
        flip = (bit(0) ^ (rank & 1)) == 1
        slots = jnp.where(flip, bit(4), bit(3)) * 8 + jnp.where(flip, bit(3), bit(4)) * 4 + bit(1) * 2 + bit(2)
        table = jnp.concatenate([(own * 8 + rank)[None], slots]).astype(jnp.int32)
        hops = (to_first, to_second, to_near, to_far)
        kept, sent = back_blocks(table, act_low, ffn_grad)
        back_total = halve([kept, to_core(sent)], 16, hops)
        vec = jnp.concatenate(
            [v.reshape(32, -1) for v in short] + [in_bias_grad.reshape(32, -1)], axis=1
        )
        vec = jnp.pad(vec.astype(BF)[:, None, :], ((0, 0), (0, 7), (0, width - vec.shape[1])))
        kept, sent = in_blocks(table, hidden_low, pre_grad, attn_rows, branch_grad, vec)
        in_total = halve([kept, to_core(sent)], 16, hops)
        w_back_grad = back_total
        w_in_grad = jnp.concatenate([in_total[c * 24 : (c + 1) * 24] for c in range(4)], axis=1)
        w_out_grad = in_total[96:120]
        row = in_total[120]
        short_grads = [row[n * 24 : (n + 1) * 24] for n in range(6)]
        in_bias_grad = row[144:240]
    else:
        scatter = lambda v: lax.psum_scatter(v, ("seq", "fsdp"), scatter_dimension=0, tiled=True)
        w_back_grad = scatter(contract_rows(act_low, ffn_grad))
        w_in_grad = scatter(contract_rows(hidden_low, pre_grad))
        turned = contract_rows(attn_rows, branch_grad).reshape(seqs, local_cols, width)
        w_out_grad = scatter(jnp.take(turned, order, axis=0).reshape(width, width))
        short_grads = [scatter(v) for v in short]
        in_bias_grad = scatter(in_bias_grad)

    *turned, rel_grad, sums = attend_back(
        place, douts, big, small, ox, qx, pq, kx, vxt, key_pos, wrel_rows, sine, cosine, turned_types, head
    )
    dx = [contract_cols(t, w_qkv) for t in turned]
    dx = [dx[0]] + [v.astype(BF) for v in dx[1:]]
    turned, dx = lax.optimization_barrier((turned, dx))
    input_rows = sum_one_grad + dx[0]
    for k in range(1, 4):
        input_rows = input_rows + to_seq(dx[k], k).astype(F32)
    input_rows = input_rows.astype(BF)
    returned = lax.all_to_all(
        input_rows.reshape(1, row_count, width), "fsdp", split_axis=1, concat_axis=0, tiled=True
    )
    input_grad = contract_rows(owner_low, returned.reshape(pack_count, sliver_rows * width))
    input_grad = input_grad.astype(BF).reshape(pack_count, sliver_rows, width)

    qkv_grad = contract_rows(jnp.concatenate(pieces, axis=0), jnp.concatenate(turned, axis=0))
    fine = width // devices
    qkv_grad = qkv_grad[:, : 3 * local_cols].reshape(seqs, fsdps, fine, 3 * local_cols)
    qkv_grad = jnp.transpose(qkv_grad, (1, 0, 2, 3)).reshape(fsdps, local_rows, 3 * local_cols)
    rel_grad = jnp.transpose(rel_grad, (2, 0, 1)).reshape(fsdps, local_rows, local_cols)
    sums = sums[:, :, :DH]
    eighth = DH // fsdps
    spread = lambda v, n: jnp.moveaxis(v.reshape(v.shape[:-1] + (fsdps, n)), -2, 0).reshape(fsdps, -1)
    vec = jnp.concatenate(
        [
            sums[:, 5].reshape(fsdps, fine),
            spread(sums[:, 0], eighth),
            spread(sums[:, 1], eighth),
            spread(sums[:, 2], eighth),
            spread(jnp.stack([sums[:, 3], sums[:, 4]]), eighth),
        ],
        axis=1,
    )
    vec = jnp.pad(vec[:, None, :], ((0, 0), (0, 7), (0, width - vec.shape[1])))
    bundle = jnp.concatenate([jnp.concatenate([qkv_grad, rel_grad], axis=2), vec], axis=1)
    if direct:
        count = jnp.arange(8, dtype=jnp.int32)
        wanted = rank ^ (((count >> 2) & 1) | (((count >> 1) & 1) << 1) | ((count & 1) << 2))
        bundle = jnp.take(bundle.astype(BF), wanted, axis=0)
        total = halve([bundle[:4], to_core(bundle[4:])], 4, (to_near, to_far))
    else:
        total = lax.psum_scatter(bundle, "fsdp", scatter_dimension=0, tiled=True)[0]
    own_qkv = total[:local_rows, : 3 * local_cols].reshape(seqs, fine, 3 * local_cols).astype(BF)
    swapped = lax.all_to_all(own_qkv, "seq", split_axis=0, concat_axis=0, tiled=True).astype(F32)
    both = swapped[:, :, : 2 * local_cols].reshape(seqs, fine, local_heads, 2, DH)
    both = jnp.transpose(both, (3, 1, 0, 2, 4)).reshape(2, fine, width)
    w_value_grad = jnp.transpose(swapped[:, :, 2 * local_cols :], (1, 0, 2)).reshape(fine, width)
    rel_total = total[:local_rows, 3 * local_cols :].reshape(local_rows, local_heads, DH)
    row = total[local_rows]
    cut = local_heads * eighth
    value_bias_grad = row[:fine]
    bias_grads = [row[fine + n * cut : fine + (n + 1) * cut].reshape(local_heads, eighth) for n in range(3)]
    embed_grad = row[fine + 3 * cut : fine + 5 * cut].reshape(2, local_heads, eighth)
    return (
        activations,
        input_grad,
        both[0],
        both[1],
        w_value_grad,
        value_bias_grad,
        w_out_grad,
        short_grads[4],
        short_grads[0],
        short_grads[1],
        w_in_grad,
        in_bias_grad,
        w_back_grad,
        short_grads[5],
        short_grads[2],
        short_grads[3],
        rel_total,
        bias_grads[0],
        bias_grads[1],
        bias_grads[2],
        embed_grad,
    )


def solution(mesh):
    placed = (
        P(None, ("seq", "fsdp"), None),
        P("fsdp", None),
        P("fsdp", None),
        P("fsdp", None),
        P("fsdp"),
        P("fsdp", None),
        P("fsdp"),
        P("fsdp"),
        P("fsdp"),
        P("fsdp", None),
        P("fsdp"),
        P("fsdp", None),
        P("fsdp"),
        P("fsdp"),
        P("fsdp"),
        P("fsdp", "seq", None),
        P("seq", "fsdp"),
        P("seq", "fsdp"),
        P("seq", "fsdp"),
        P(None, "seq", "fsdp"),
        P(),
        P(),
        P(),
        P("fsdp", "seq", None),
    )
    return jax.shard_map(
        shards,
        mesh=mesh,
        in_specs=placed,
        out_specs=(
            P("fsdp", "seq", None),
            P(None, ("seq", "fsdp"), None),
            P(("seq", "fsdp"), None),
            P(("seq", "fsdp"), None),
            P(("seq", "fsdp"), None),
            P(("seq", "fsdp")),
            P(("seq", "fsdp"), None),
            P(("seq", "fsdp")),
            P(("seq", "fsdp")),
            P(("seq", "fsdp")),
            P(("seq", "fsdp"), None),
            P(("seq", "fsdp")),
            P(("seq", "fsdp"), None),
            P(("seq", "fsdp")),
            P(("seq", "fsdp")),
            P(("seq", "fsdp")),
            P("fsdp", "seq", None),
            P("seq", "fsdp"),
            P("seq", "fsdp"),
            P("seq", "fsdp"),
            P(None, "seq", "fsdp"),
        ),
        check_vma=False,
    )
```

```python
import jax
import jax.numpy as jnp
from jax import lax
from jax.experimental import pallas as pl
from jax.experimental.pallas import tpu as pltpu
from jax.sharding import PartitionSpec as P

DH = 64
LONGEST = 1024
QB = 256
BLOCKED = -1e30
BF = jnp.bfloat16
F32 = jnp.float32
VM = pl.BlockSpec(memory_space=pltpu.VMEM)
SM = pl.BlockSpec(memory_space=pltpu.SMEM)
VMEM_LIMIT = 60 * 1024 * 1024


def lanes_of(rows, width=128):
    return lax.broadcasted_iota(jnp.int32, (rows, width), 1)


def split3(value):
    high = value.astype(BF).astype(F32)
    rest = value - high
    middle = rest.astype(BF).astype(F32)
    return high, middle, rest - middle


def masks_of(place):
    return 0, place[3], place[4], 3


def pick(lane, first, columns, base):
    for number, column in enumerate(columns):
        base = jnp.where(lane == first + number, column, base)
    return base


def project_body(place, x0, x1, x2, x3, w_ref, head_ref, tcol_ref, qx_ref, pq_ref, kx_ref, kxt_ref, vx_ref, vxt_ref, rolled):
    own, start, near = place[0], place[1], place[2]
    scale = DH ** -0.5
    rows = qx_ref.shape[1]
    part = x0.shape[0]
    for mask, piece in zip(masks_of(place), (x0, x1, x2, x3)):
        y = jnp.dot(piece[...], w_ref[...], preferred_element_type=F32)
        base = pl.multiple_of((own ^ mask) * part, 8)
        for c in range(5):
            column = y[:, c * 128 : (c + 1) * 128]
            rolled[c, pl.ds(base, part), :] = column
            rolled[c, pl.ds(pl.multiple_of(base + rows, 8), part), :] = column

    def block(r, carry):
        row = pl.multiple_of(r * QB, QB)
        lane = lanes_of(QB)
        kind = tcol_ref[pl.ds(row, QB), :]
        index = row + lax.broadcasted_iota(jnp.int32, (QB, 1), 0)
        small = index >= LONGEST
        first = jnp.where(small & (index < LONGEST + near), 1.0, 0.0)
        second = jnp.where(small & (index >= LONGEST + near), 1.0, 0.0)
        one = jnp.where(kind == 1, 1.0, 0.0)
        zero = 1.0 - one
        for h in range(3):
            both = rolled[h, pl.ds(start + row, QB), :].astype(BF).astype(F32)
            if h < 2:
                v = rolled[3, pl.ds(start + row, QB), :]
                v = v if h == 0 else pltpu.roll(v, 64, 1)
            else:
                v = rolled[4, pl.ds(start + row, QB), :]
            head = head_ref[h]
            content = (both + head[0:1]) * scale
            position = ((both + head[1:2]) * scale).astype(BF)
            typed = (both + head[2:3]) * scale
            differ = jnp.sum(typed * head[3:4], axis=1, keepdims=True)
            same = jnp.sum(typed * head[4:5], axis=1, keepdims=True)
            for_zero = jnp.where(kind == 1, differ, same)
            for_one = jnp.where(kind == 1, same, differ)
            columns = [*split3(for_zero), *split3(for_one), second * BLOCKED, first * BLOCKED]
            qx = pick(lane, 64, columns, jnp.where(lane < 64, content, 0.0)).astype(BF)
            qx_ref[h, pl.ds(row, QB), :] = qx
            raw = pltpu.roll(both, 64, 1)
            pq_ref[h, pl.ds(row, QB), :] = jnp.where(lane < 64, position.astype(F32), raw).astype(BF)
            kx = pick(lane, 64, [zero, zero, zero, one, one, one, first, second], jnp.where(lane < 64, raw, 0.0))
            kx_ref[h, pl.ds(row, QB), :] = kx.astype(BF)
            kxt_ref[h, :, pl.ds(row, QB)] = jnp.transpose(kx, (1, 0)).astype(BF)
            vx = jnp.where(lane < 64, v + head[5:6], jnp.where(lane < 67, 1.0, 0.0)).astype(BF)
            vx_ref[h, pl.ds(row, QB), :] = vx
            vxt_ref[h, :, pl.ds(row, QB)] = jnp.transpose(vx.astype(F32), (1, 0)).astype(BF)
        return carry

    lax.fori_loop(0, rows // QB, block, 0)


def project(place, pieces, w_qkv, head, tcol):
    rows = 4 * pieces[0].shape[0]
    tall = jax.ShapeDtypeStruct((3, rows, 128), BF)
    wide = jax.ShapeDtypeStruct((3, 128, rows), BF)
    return pl.pallas_call(
        project_body,
        in_specs=[SM] + [VM] * 7,
        out_specs=[VM] * 6,
        out_shape=[tall, tall, tall, wide, tall, wide],
        scratch_shapes=[pltpu.VMEM((5, 2 * rows, 128), F32)],
        compiler_params=pltpu.CompilerParams(vmem_limit_bytes=VMEM_LIMIT),
        cost_estimate=pl.CostEstimate(flops=2 * rows * 768 * 640, bytes_accessed=10_000_000, transcendentals=0),
        name="project",
    )(place, *pieces, w_qkv, head, tcol)


def attend_body(place, qx_ref, pq_ref, kxt_ref, vx_ref, kpt_ref, wrt_ref, sn_ref, cs_ref, big_ref, small_ref, ox_ref, o0, o1, o2, o3, keys, left, outs):
    h, i = pl.program_id(0), pl.program_id(1)
    own, start = place[0], place[1]
    width = kpt_ref.shape[0]
    half = width // 2
    rows = kpt_ref.shape[1]

    @pl.when((h == 0) & (i == 0))
    def _():
        keys[0:width, :] = kpt_ref[...]

    @pl.when(i == 0)
    def _():
        keys[width:, :] = kxt_ref[0]

    rel = jnp.dot(pq_ref[0], wrt_ref[0], preferred_element_type=F32)
    r1, r2 = rel[:, :half], rel[:, half:]
    sn, cs = sn_ref[...], cs_ref[...]
    left[:, 0:half] = (r1 * sn + r2 * cs).astype(BF)
    left[:, half:width] = (r2 * sn - r1 * cs).astype(BF)
    left[:, width:] = qx_ref[0]

    def attend(low, high, store):
        score = jnp.dot(left[...], keys[:, low:high], preferred_element_type=F32)
        top = jnp.max(score, axis=1, keepdims=True)
        raised = jnp.exp(score - top).astype(BF)
        store[0] = raised
        mixed = jnp.dot(raised, vx_ref[0, low:high, :], preferred_element_type=F32)
        inverse = 1.0 / mixed[:, 64:65]
        lane = lanes_of(QB)
        ox = jnp.where(lane < 64, mixed * inverse, jnp.where(lane == 64, inverse, 0.0))
        ox_ref[0] = ox
        row = pl.multiple_of(i * QB, QB)
        outs[h, pl.ds(row, QB), :] = ox
        outs[h, pl.ds(pl.multiple_of(row + rows, QB), QB), :] = ox

    @pl.when(i < LONGEST // QB)
    def _():
        attend(0, LONGEST, big_ref)

    @pl.when(i >= LONGEST // QB)
    def _():
        attend(LONGEST, rows, small_ref)

    @pl.when((h == 2) & (i == pl.num_programs(1) - 1))
    def _():
        part = o0.shape[0]
        for mask, out in zip(masks_of(place), (o0, o1, o2, o3)):
            at = lax.rem((own ^ mask) * part + rows - start, rows)
            out[...] = jnp.concatenate([outs[g, pl.ds(at, part), :][:, 0:64] for g in range(3)], axis=1).astype(BF)


def attend(place, qx, pq, kxt, vx, kpt, wrt, sn, cs):
    rows = qx.shape[1]
    width = kpt.shape[0]
    blocks = rows // QB
    bigs = LONGEST // QB
    rest = rows - LONGEST
    per_block = lambda h, i: (h, i, 0)
    per_head = lambda h, i: (h, 0, 0)
    whole2 = lambda h, i: (0, 0)
    part = rows // 4
    out_piece = jax.ShapeDtypeStruct((part, 192), BF)
    return pl.pallas_call(
        attend_body,
        grid=(3, blocks),
        in_specs=[
            SM,
            pl.BlockSpec((1, QB, 128), per_block),
            pl.BlockSpec((1, QB, 128), per_block),
            pl.BlockSpec((1, 128, rows), per_head),
            pl.BlockSpec((1, rows, 128), per_head),
            pl.BlockSpec((width, rows), whole2, pipeline_mode=pl.Buffered(1)),
            pl.BlockSpec((1, 128, width), per_head),
            pl.BlockSpec((QB, width // 2), lambda h, i: (i, 0)),
            pl.BlockSpec((QB, width // 2), lambda h, i: (i, 0)),
        ],
        out_specs=[
            pl.BlockSpec((1, QB, LONGEST), lambda h, i: (h, jnp.minimum(i, bigs - 1), 0)),
            pl.BlockSpec((1, QB, rest), lambda h, i: (h, jnp.maximum(i - bigs, 0), 0)),
            pl.BlockSpec((1, QB, 128), per_block),
        ]
        + [pl.BlockSpec((part, 192), whole2)] * 4,
        out_shape=[
            jax.ShapeDtypeStruct((3, LONGEST, LONGEST), BF),
            jax.ShapeDtypeStruct((3, rest, rest), BF),
            jax.ShapeDtypeStruct((3, rows, 128), F32),
        ]
        + [out_piece] * 4,
        scratch_shapes=[
            pltpu.VMEM((width + 128, rows), BF),
            pltpu.VMEM((QB, width + 128), BF),
            pltpu.VMEM((3, 2 * rows, 128), F32),
        ],
        compiler_params=pltpu.CompilerParams(vmem_limit_bytes=VMEM_LIMIT, dimension_semantics=("arbitrary", "arbitrary")),
        cost_estimate=pl.CostEstimate(flops=12_000_000_000, bytes_accessed=20_000_000, transcendentals=4_000_000),
        name="attend",
    )(place, qx, pq, kxt, vx, kpt, wrt, sn, cs)


def back_body(place, d0, d1, d2, d3, big_ref, small_ref, ox_ref, qx_ref, pq_ref, kx_ref, vxt_ref, kp_ref, wr_ref, sn_ref, cs_ref, tcol_ref, head_ref, gkeep_ref, gsend_ref, rel_ref, sum_ref, douts, dkt, dvt, gwt, grads):
    h, i = pl.program_id(0), pl.program_id(1)
    own, start = place[0], place[1]
    rows, width = kp_ref.shape
    half = width // 2
    scale = DH ** -0.5
    part = d0.shape[0]
    last = pl.num_programs(1) - 1
    row = pl.multiple_of(i * QB, QB)
    again = pl.multiple_of(row + rows, QB)

    @pl.when((h == 0) & (i == 0))
    def _():
        blank = jnp.zeros((part, 64), F32)
        for mask, piece in zip(masks_of(place), (d0, d1, d2, d3)):
            values = piece[...].astype(F32)
            base = pl.multiple_of((own ^ mask) * part, 8)
            for g in range(3):
                padded = jnp.concatenate([values[:, g * 64 : (g + 1) * 64], blank], axis=1)
                douts[g, pl.ds(base, part), :] = padded
                douts[g, pl.ds(pl.multiple_of(base + rows, 8), part), :] = padded

    @pl.when(i == 0)
    def _():
        dkt[...] = jnp.zeros_like(dkt)
        dvt[...] = jnp.zeros_like(dvt)
        gwt[...] = jnp.zeros_like(gwt)
        sum_ref[...] = jnp.zeros_like(sum_ref)

    lane = lanes_of(QB)
    dout = douts[h, pl.ds(start + row, QB), :]
    ox = ox_ref[0]
    inverse = ox[:, 64:65]
    dot_row = jnp.sum(dout * ox, axis=1, keepdims=True)
    dox = pick(lane, 64, [-x for x in split3(dot_row)], dout).astype(BF)
    dout_t = jnp.transpose(dout * inverse, (1, 0))[0:64].astype(BF)
    qx = qx_ref[0]
    qc_t = jnp.transpose(qx.astype(F32), (1, 0))[0:64].astype(BF)
    pq = pq_ref[0].astype(F32)
    qp_t = jnp.transpose(pq, (1, 0))[0:64].astype(BF)
    sn, cs = sn_ref[...], cs_ref[...]

    def back(low, high, saved):
        raised = saved[0]
        dprob = jnp.dot(dox, vxt_ref[0, :, low:high], preferred_element_type=F32)
        dscore = (raised.astype(F32) * (dprob * inverse)).astype(BF)
        dvt[:, low:high] += jnp.dot(dout_t, raised, preferred_element_type=F32)
        dkt[:, low:high] += jnp.dot(qc_t, dscore, preferred_element_type=F32)
        da = jnp.dot(dscore, kp_ref[low:high, :], preferred_element_type=F32)
        dqx = jnp.dot(dscore, kx_ref[0, low:high, :], preferred_element_type=F32)
        da1, da2 = da[:, 0:half], da[:, half:width]
        drel = jnp.concatenate([(da1 * sn - da2 * cs).astype(BF), (da1 * cs + da2 * sn).astype(BF)], axis=1)
        dqp = jnp.dot(drel, wr_ref[0], preferred_element_type=F32)
        gwt[...] += jnp.dot(qp_t, drel, preferred_element_type=F32)
        kind = tcol_ref[...]
        over_zero, over_one = dqx[:, 64:65], dqx[:, 67:68]
        same = jnp.where(kind == 1, over_one, over_zero)
        differ = jnp.where(kind == 1, over_zero, over_one)
        head = head_ref[0]
        dqt = differ * head[3:4] + same * head[4:5]
        dqc = jnp.where(lane < 64, dqx, 0.0)
        dq = (dqc + dqp + dqt) * scale
        grads[h, pl.ds(row, QB), :] = dq
        typed = (pltpu.roll(pq, 64, 1) + head[2:3]) * scale
        sums = [dqc * scale, dqp * scale, dqt * scale, differ * typed, same * typed]
        for number, values in enumerate(sums):
            sum_ref[0, number : number + 1, :] += jnp.sum(values, axis=0, keepdims=True)

    @pl.when(i < LONGEST // QB)
    def _():
        back(0, LONGEST, big_ref)

    @pl.when(i >= LONGEST // QB)
    def _():
        back(LONGEST, rows, small_ref)

    @pl.when(i == last)
    def _():
        dk = jnp.transpose(dkt[...], (1, 0))
        dq = grads[h, 0:rows, :]
        pair = jnp.concatenate([dq[:, 0:64], dk], axis=1)
        grads[h, 0:rows, :] = pair
        grads[h, rows : 2 * rows, :] = pair
        dv = jnp.transpose(dvt[...], (1, 0)).astype(BF).astype(F32)
        sum_ref[0, 5:6, 0:64] = jnp.sum(dv, axis=0, keepdims=True)
        blank = jnp.zeros_like(dv)
        rel = jnp.transpose(gwt[...], (1, 0))
        empty = jnp.zeros_like(rel)

        @pl.when(h == 0)
        def _():
            padded = jnp.concatenate([dv, blank], axis=1)
            grads[3, 0:rows, :] = padded
            grads[3, rows : 2 * rows, :] = padded
            rel_ref[:, 0:128] = jnp.concatenate([empty, rel], axis=1)

        @pl.when(h == 1)
        def _():
            rel_ref[:, 128:256] = jnp.concatenate([rel, empty], axis=1)
            padded = grads[3, 0:rows, :] + jnp.concatenate([blank, dv], axis=1)
            grads[3, 0:rows, :] = padded
            grads[3, rows : 2 * rows, :] = padded

        @pl.when(h == 2)
        def _():
            padded = jnp.concatenate([dv, blank], axis=1)
            grads[4, 0:rows, :] = padded
            grads[4, rows : 2 * rows, :] = padded
            rel_ref[:, 128:256] += jnp.concatenate([empty, rel], axis=1)
            spots = ((gkeep_ref, 0), (gsend_ref, 0), (gkeep_ref, part), (gsend_ref, part))
            for mask, (out, low) in zip(masks_of(place), spots):
                at = lax.rem((own ^ mask) * part + rows - start, rows)
                for c in range(5):
                    out[low : low + part, c * 128 : (c + 1) * 128] = grads[c, pl.ds(at, part), :].astype(BF)


def attend_back(place, douts, big, small, ox, qx, pq, kx, vxt, kp, wr, sn, cs, tcol, head):
    rows, width = kp.shape
    blocks = rows // QB
    bigs = LONGEST // QB
    rest = rows - LONGEST
    part = rows // 4
    per_block = lambda h, i: (h, i, 0)
    per_head = lambda h, i: (h, 0, 0)
    whole2 = lambda h, i: (0, 0)
    return pl.pallas_call(
        back_body,
        grid=(3, blocks),
        in_specs=[SM]
        + [pl.BlockSpec((part, 192), whole2)] * 4
        + [
            pl.BlockSpec((1, QB, LONGEST), lambda h, i: (h, jnp.minimum(i, bigs - 1), 0)),
            pl.BlockSpec((1, QB, rest), lambda h, i: (h, jnp.maximum(i - bigs, 0), 0)),
            pl.BlockSpec((1, QB, 128), per_block),
            pl.BlockSpec((1, QB, 128), per_block),
            pl.BlockSpec((1, QB, 128), per_block),
            pl.BlockSpec((1, rows, 128), per_head),
            pl.BlockSpec((1, 128, rows), per_head),
            pl.BlockSpec((rows, width), whole2, pipeline_mode=pl.Buffered(1)),
            pl.BlockSpec((1, width, 128), per_head),
            pl.BlockSpec((QB, width // 2), lambda h, i: (i, 0)),
            pl.BlockSpec((QB, width // 2), lambda h, i: (i, 0)),
            pl.BlockSpec((QB, 1), lambda h, i: (i, 0)),
            pl.BlockSpec((1, 8, 128), per_head),
        ],
        out_specs=[pl.BlockSpec((2 * part, 640), whole2)] * 2
        + [pl.BlockSpec((width, 256), whole2), pl.BlockSpec((1, 8, 128), per_head)],
        out_shape=[jax.ShapeDtypeStruct((2 * part, 640), BF)] * 2
        + [jax.ShapeDtypeStruct((width, 256), F32), jax.ShapeDtypeStruct((3, 8, 128), F32)],
        scratch_shapes=[
            pltpu.VMEM((3, 2 * rows, 128), F32),
            pltpu.VMEM((64, rows), F32),
            pltpu.VMEM((64, rows), F32),
            pltpu.VMEM((64, width), F32),
            pltpu.VMEM((5, 2 * rows, 128), F32),
        ],
        compiler_params=pltpu.CompilerParams(vmem_limit_bytes=VMEM_LIMIT, dimension_semantics=("arbitrary", "arbitrary")),
        cost_estimate=pl.CostEstimate(flops=20_000_000_000, bytes_accessed=25_000_000, transcendentals=0),
        name="attend_back",
    )(place, *douts, big, small, ox, qx, pq, kx, vxt, kp, wr, sn, cs, tcol, head)


def reload_body(owners, in_ref, out_ref):
    def move(j, carry):
        out_ref[j] = in_ref[owners[j]]
        return carry

    lax.fori_loop(0, out_ref.shape[0], move, 0)


def reload(owners, returned):
    return pl.pallas_call(
        reload_body,
        in_specs=[SM, VM],
        out_specs=VM,
        out_shape=jax.ShapeDtypeStruct(returned.shape, returned.dtype),
        compiler_params=pltpu.CompilerParams(vmem_limit_bytes=VMEM_LIMIT),
        name="reload",
    )(owners, returned)


def qkv_blocks_body(place, x0, x1, x2, x3, tkeep_ref, tsend_ref, rel_ref, sums_ref, keep_ref, send_ref, acc):
    even = lax.rem(place[0], 2) == 0
    part = x0.shape[0]
    parts = ((x0, tkeep_ref, 0), (x2, tkeep_ref, part), (x1, tsend_ref, 0), (x3, tsend_ref, part))
    for number, (x, t, low) in enumerate(parts):
        value = lax.dot_general(x[...], t[low : low + part, :], (((0,), (0,)), ((), ())), preferred_element_type=F32)
        acc[...] = value if number == 0 else acc[...] + value
    notes = jnp.concatenate([sums_ref[0], sums_ref[1], sums_ref[2], jnp.zeros((8, 384), F32)], axis=1).astype(BF)

    def piece(f, s):
        value = acc[(8 * s + f) * 24 : (8 * s + f + 1) * 24, :]
        rel = rel_ref[96 * f + 24 * s : 96 * f + 24 * s + 24, :]
        return jnp.concatenate([value[:, 0:512], value[:, 512:640] + rel[:, 0:128], rel[:, 128:256]], axis=1)

    for g in range(4):
        slot = place[1 + g]
        for s in range(4):
            a, b = piece(2 * g, s), piece(2 * g + 1, s)
            keep_ref[slot, 24 * s : 24 * s + 24, :] = jnp.where(even, a, b).astype(BF)
            send_ref[slot, 24 * s : 24 * s + 24, :] = jnp.where(even, b, a).astype(BF)
        keep_ref[slot, 96:104, :] = notes
        send_ref[slot, 96:104, :] = notes


def qkv_blocks(place, pieces, tkeep, tsend, rel, sums):
    width = pieces[0].shape[1]
    out = jax.ShapeDtypeStruct((4, 104, width), BF)
    return pl.pallas_call(
        qkv_blocks_body,
        in_specs=[SM] + [VM] * 8,
        out_specs=[VM] * 2,
        out_shape=[out, out],
        scratch_shapes=[pltpu.VMEM((width, 640), F32)],
        compiler_params=pltpu.CompilerParams(vmem_limit_bytes=VMEM_LIMIT),
        cost_estimate=pl.CostEstimate(flops=2_000_000_000, bytes_accessed=8_000_000, transcendentals=0),
        name="qkv_blocks",
    )(place, *pieces, tkeep, tsend, rel, sums)


def merge_body(*refs):
    kb, cb, ki, ci, *more, out_ref = refs
    cut = kb.shape[1]
    back = kb[...].astype(F32) + cb[...].astype(F32)
    ins = ki[...].astype(F32) + ci[...].astype(F32)
    for m in more:
        back = back + m[:, :cut, :].astype(F32)
        ins = ins + m[:, cut:, :].astype(F32)
    out_ref[:, :cut, :] = back.astype(BF)
    out_ref[:, cut:, :] = ins.astype(BF)


def merge(parts, half):
    step = min(half, 2)
    first = half // step
    rows = parts[0].shape[1] + parts[2].shape[1]
    width = parts[0].shape[2]
    block = lambda p: pl.BlockSpec((step,) + p.shape[1:], lambda g: (first + g, 0, 0))
    return pl.pallas_call(
        merge_body,
        grid=(first,),
        in_specs=[block(p) for p in parts],
        out_specs=pl.BlockSpec((step, rows, width), lambda g: (g, 0, 0)),
        out_shape=jax.ShapeDtypeStruct((half, rows, width), BF),
        compiler_params=pltpu.CompilerParams(vmem_limit_bytes=VMEM_LIMIT, dimension_semantics=("arbitrary",)),
        cost_estimate=pl.CostEstimate(flops=half * rows * width * 6, bytes_accessed=half * rows * width * 8, transcendentals=0),
        name="merge",
    )(*parts)


EPS = 1e-09
GELU_A = (2.0 / 3.141592653589793) ** 0.5
GELU_B = 0.044715

def spread_norm(values):
    center = values - jnp.mean(values, axis=1, keepdims=True)
    inverse = lax.rsqrt(jnp.mean(center * center, axis=1, keepdims=True) + EPS)
    return center * inverse, inverse


def middle_body(
    place, a0, a1, a2, a3, x_ref, go_ref, w_ref, vec_ref, bin_ref,
    act_ref, h_ref, u_ref, dz_ref, df_ref, dbr_ref, dr_ref, d0, d1, d2, d3, sum_ref,
    wout, slope, high, normed, acc,
):
    own = place[0]
    width = x_ref.shape[1]
    cols = a0.shape[1]
    vector = lambda n: vec_ref[n : n + 1, :]
    for s in range(4):
        piece = w_ref[:, s, :, 2 * width : 2 * width + cols]
        wout[:, s * cols : (s + 1) * cols] = piece.reshape(width, cols)
    part = lambda mask: wout[pl.ds(pl.multiple_of((own ^ mask) * cols, 64), cols), :]
    masks = masks_of(place)
    total = x_ref[...].astype(F32) + vector(0)
    for mask, piece in zip(masks, (a0, a1, a2, a3)):
        total = total + jnp.dot(piece[...], part(mask), preferred_element_type=F32)
    unit, inverse_one = spread_norm(total)
    normed[...] = unit
    first = unit * vector(1) + vector(2)
    high[...] = first
    h_ref[...] = first.astype(BF)
    acc[...] = first + vector(3)

    def w_in_at(w):
        return w_ref[:, w, :, 0:width].reshape(width, width)

    def w_back_at(w):
        return w_ref[pl.ds(2 * w, 2), :, :, width : 2 * width].reshape(width, width)

    def forward(w, carry):
        at = pl.multiple_of(w * width, 128)
        z = jnp.dot(h_ref[...], w_in_at(w), preferred_element_type=F32) + bin_ref[:, pl.ds(at, width)]
        square = z * z
        bend = jnp.tanh(GELU_A * z * (1.0 + GELU_B * square))
        half = 0.5 + 0.5 * bend
        u = (z * half).astype(BF)
        u_ref[:, pl.ds(at, width)] = u
        slope[:, pl.ds(at, width)] = half + 0.5 * z * (1.0 - bend * bend) * (GELU_A * (1.0 + 3.0 * GELU_B * square))
        acc[...] += jnp.dot(u, w_back_at(w), preferred_element_type=F32)
        return carry

    lax.fori_loop(0, 4, forward, 0)
    unit, inverse_two = spread_norm(acc[...])
    act_ref[...] = (unit * vector(4) + vector(5)).astype(BF)

    def back(gradient, unit, inverse, gain):
        scaled = gradient * gain
        inner = scaled - jnp.mean(scaled, axis=1, keepdims=True)
        return (inner - unit * jnp.mean(scaled * unit, axis=1, keepdims=True)) * inverse

    def note(row, values):
        sum_ref[row : row + 1, :] = jnp.sum(values, axis=0, keepdims=True)

    gradient = go_ref[...].astype(F32)
    note(2, gradient * unit)
    note(3, gradient)
    second = back(gradient, unit, inverse_two, vector(4))
    df = second.astype(BF)
    df_ref[...] = df
    note(5, df.astype(F32))
    acc[...] = second

    def backward(w, carry):
        at = pl.multiple_of(w * width, 128)
        du = lax.dot_general(df_ref[...], w_back_at(w), (((1,), (1,)), ((), ())), preferred_element_type=F32)
        dz = (slope[:, pl.ds(at, width)] * du).astype(BF)
        dz_ref[:, pl.ds(at, width)] = dz
        sum_ref[pl.ds(8 + w, 1), :] = jnp.sum(dz.astype(F32), axis=0, keepdims=True)
        acc[...] += lax.dot_general(dz, w_in_at(w), (((1,), (1,)), ((), ())), preferred_element_type=F32)
        return carry

    lax.fori_loop(0, 4, backward, 0)
    gradient = acc[...]
    unit = normed[...]
    note(0, gradient * unit)
    note(1, gradient)
    dr = back(gradient, unit, inverse_one, vector(1))
    dr_ref[...] = dr
    dbr = dr.astype(BF)
    dbr_ref[...] = dbr
    note(4, dbr.astype(F32))
    sum_ref[6:8, :] = jnp.zeros((2, width), F32)
    sum_ref[12:16, :] = jnp.zeros((4, width), F32)
    for mask, out in zip(masks, (d0, d1, d2, d3)):
        value = lax.dot_general(dbr, part(mask), (((1,), (1,)), ((), ())), preferred_element_type=F32)
        out[...] = value.astype(BF)


def middle(place, pieces, x, out_grad, weights, vectors, bin_full):
    rows, width = x.shape
    cols = pieces[0].shape[1]
    hidden = bin_full.shape[1]
    low = lambda n: jax.ShapeDtypeStruct((rows, n), BF)
    full = lambda r, n: jax.ShapeDtypeStruct((r, n), F32)
    return pl.pallas_call(
        middle_body,
        in_specs=[SM] + [VM] * 9,
        out_specs=[VM] * 12,
        out_shape=[low(width), low(width), low(hidden), low(hidden), low(width), low(width), full(rows, width)]
        + [low(cols)] * 4
        + [full(16, width)],
        scratch_shapes=[
            pltpu.VMEM((width, width), BF),
            pltpu.VMEM((rows, hidden), F32),
            pltpu.VMEM((rows, width), F32),
            pltpu.VMEM((rows, width), F32),
            pltpu.VMEM((rows, width), F32),
        ],
        compiler_params=pltpu.CompilerParams(vmem_limit_bytes=VMEM_LIMIT),
        cost_estimate=pl.CostEstimate(flops=8_000_000_000, bytes_accessed=20_000_000, transcendentals=1_000_000),
        name="middle",
    )(place, *pieces, x, out_grad, weights, vectors, bin_full)


def angles_of(position, width):
    half_width = width // 2
    rate_table = 10000.0 ** (-(jnp.arange(half_width, dtype=jnp.float32) / half_width))
    turned = position.astype(jnp.float32)[:, None] * rate_table[None, :]
    return (jnp.sin(turned), jnp.cos(turned))


def contract_rows(left, right):
    return lax.dot_general(
        left, right, (((0,), (0,)), ((), ())), preferred_element_type=jnp.float32
    )


def contract_cols(left, right):
    return lax.dot_general(
        left, right, (((1,), (1,)), ((), ())), preferred_element_type=jnp.float32
    )


def across(values, other):
    seqs, fsdps = lax.axis_size("seq"), lax.axis_size("fsdp")
    pairs = []
    for s in range(seqs):
        for f in range(fsdps):
            to_s, to_f = other(s, f)
            pairs.append((s * fsdps + f, to_s * fsdps + to_f))
    return lax.ppermute(values, ("seq", "fsdp"), pairs)


def to_core(values):
    return across(values, lambda s, f: (s, f ^ 1))


def to_first(values):
    return across(values, lambda s, f: (s ^ (2 if f & 1 else 1), f))


def to_second(values):
    return across(values, lambda s, f: (s ^ (1 if f & 1 else 2), f))


def to_near(values):
    return across(values, lambda s, f: (s, f ^ 2))


def to_far(values):
    return across(values, lambda s, f: (s, f ^ 4))


def to_seq(values, k):
    return across(values, lambda s, f: (s ^ k, f))


def add_parts(parts, low, high):
    total = parts[0][low:high].astype(F32)
    for part in parts[1:]:
        total = total + part[low:high].astype(F32)
    return total


def outgoing(parts, count):
    return add_parts(parts, count // 2, count).astype(BF)


def back_blocks_body(place, u_ref, df_ref, keep_ref, send_ref):
    core = lax.rem(place[0], 2)
    group = u_ref.shape[1] // 4
    for g in range(1):
        acc = lax.dot_general(u_ref[...], df_ref[...], (((0,), (0,)), ((), ())), preferred_element_type=F32)
        at = pl.program_id(0) * 4
        for j in range(4):
            slot = place[1 + at + j]
            value = acc[j * group : (j + 1) * group].astype(BF)

            @pl.when(core == j % 2)
            def _():
                keep_ref[slot] = value

            @pl.when(core != j % 2)
            def _():
                send_ref[slot] = value


def back_blocks(place, u, df):
    rows, hidden = u.shape
    width = df.shape[1]
    out = jax.ShapeDtypeStruct((16, hidden // 32, width), BF)
    return pl.pallas_call(
        back_blocks_body,
        grid=(8,),
        in_specs=[SM, pl.BlockSpec((rows, hidden // 8), lambda g: (0, g)), pl.BlockSpec((rows, width), lambda g: (0, 0))],
        out_specs=[pl.BlockSpec((16, hidden // 32, width), lambda g: (0, 0, 0))] * 2,
        out_shape=[out, out],
        compiler_params=pltpu.CompilerParams(vmem_limit_bytes=VMEM_LIMIT, dimension_semantics=("arbitrary",)),
        cost_estimate=pl.CostEstimate(flops=2 * rows * hidden * width, bytes_accessed=8_000_000, transcendentals=0),
        name="back_blocks",
    )(place, u, df)


def in_blocks_body(place, h_ref, dz_ref, a_ref, db_ref, sum_ref, keep_ref, send_ref):
    even = lax.rem(place[0], 2) == 0
    core = lax.rem(place[0], 2)
    own = lax.div(place[0], 8)
    step = pl.program_id(0)

    def store(block, low, a, b):
        count = a.shape[0]
        keep_ref[place[1 + block + core], pl.ds(low, count), :] = jnp.where(even, a, b).astype(BF)
        send_ref[place[2 + block - core], pl.ds(low, count), :] = jnp.where(even, b, a).astype(BF)

    def put(block, low, acc):
        store(block, low, acc[0:24], acc[24:48])

    def chunk(which):
        for g in range(2):
            acc = lax.dot_general(
                h_ref[:, g * 384 : (g + 1) * 384], dz_ref[...], (((0,), (0,)), ((), ())), preferred_element_type=F32
            )
            for j in range(0, 16, 2):
                put(g * 16 + j, which * 24, acc[j * 24 : (j + 2) * 24])

    for which in range(4):
        pl.when(step == which)(lambda which=which: chunk(which))

    @pl.when(step == 4)
    def _():
        for g in range(2):
            acc = lax.dot_general(
                a_ref[:, g * 384 : (g + 1) * 384], db_ref[...], (((0,), (0,)), ((), ())), preferred_element_type=F32
            )
            for j in range(0, 16, 2):
                row = 2 * g + j // 8
                source = jnp.where(row == 0, 0, jnp.where(row == 3, 3, place[32 + row]))
                put((own ^ source) * 8 + j % 8, 96, acc[j * 24 : (j + 2) * 24])
        width = sum_ref.shape[1]
        line = lax.broadcasted_iota(jnp.int32, (8, width), 0)

        def note(j):
            wide = sum_ref[8 + j // 8 : 9 + j // 8, :] + jnp.zeros((8, width), F32)
            short, wide = (
                pltpu.roll(v, shift, 1) if shift % width else v
                for v, shift in ((sum_ref[0:8, :], width - 24 * j), (wide, width - 96 * (j % 8)))
            )
            return jnp.where(line == 6, wide, short)

        for j in range(0, 32, 2):
            store(j, 120, note(j), note(j + 1))


def in_blocks(place, hidden_low, dz, attn, dbr, sums):
    rows, width = hidden_low.shape
    chunks = dz.shape[1] // width
    out = jax.ShapeDtypeStruct((16, 128, width), BF)
    whole = pl.BlockSpec((rows, width), lambda g: (0, 0))
    return pl.pallas_call(
        in_blocks_body,
        grid=(chunks + 1,),
        in_specs=[SM, whole, pl.BlockSpec((rows, width), lambda g: (0, jnp.minimum(g, chunks - 1))), whole, whole]
        + [pl.BlockSpec(sums.shape, lambda g: (0, 0))],
        out_specs=[pl.BlockSpec((16, 128, width), lambda g: (0, 0, 0))] * 2,
        out_shape=[out, out],
        compiler_params=pltpu.CompilerParams(vmem_limit_bytes=VMEM_LIMIT, dimension_semantics=("arbitrary",)),
        cost_estimate=pl.CostEstimate(flops=2 * rows * width * (dz.shape[1] + width), bytes_accessed=12_000_000, transcendentals=0),
        name="in_blocks",
    )(place, hidden_low, dz, attn, dbr, sums)


def shards(
    inputs,
    w_query,
    w_key,
    w_value,
    b_value,
    w_out,
    b_out,
    norm1_gain,
    norm1_bias,
    w_in,
    b_in,
    w_back,
    b_back,
    norm2_gain,
    norm2_bias,
    w_relative,
    bias_content,
    bias_position,
    bias_type,
    type_embed,
    lengths,
    token_types,
    owners,
    grad_output,
):
    seqs, fsdps = lax.axis_size("seq"), lax.axis_size("fsdp")
    direct = seqs == 4 and fsdps == 8
    own, rank = lax.axis_index("seq"), lax.axis_index("fsdp")
    pack_count = owners.shape[0]
    sliver_rows = inputs.shape[1]
    width = inputs.shape[2]
    local_rows = w_query.shape[0]
    local_cols = width // seqs
    local_heads = w_relative.shape[1]
    scale = DH ** -0.5
    owner_table = owners[None, :] == jnp.arange(pack_count, dtype=jnp.int32)[:, None]
    owner_low = owner_table.astype(BF)
    dealt = jnp.dot(
        owner_low, inputs.reshape(pack_count, sliver_rows * width), preferred_element_type=F32
    )
    dealt = dealt.astype(BF).reshape(pack_count, sliver_rows, width)
    mine = lax.all_to_all(dealt, "fsdp", split_axis=0, concat_axis=1, tiled=True)[0]
    row_count = mine.shape[0]
    chosen = (owners == rank).astype(jnp.int32)
    pack_types = jnp.sum(chosen[:, None] * token_types, axis=0)
    pack_sizes = jnp.sum(chosen[:, None] * lengths, axis=0)
    pack_rows = pack_types.shape[0]

    def head_columns(weight):
        return lax.dynamic_slice_in_dim(weight, own * local_cols, local_cols, 1)

    block = jnp.concatenate(
        [head_columns(w) for w in (w_query, w_key, w_value)] + [w_relative.reshape(local_rows, local_cols)], axis=1
    )
    long_vectors = (b_value, b_out, norm1_gain, norm1_bias, b_back, norm2_gain, norm2_bias, b_in)
    head_vectors = (bias_content, bias_position, bias_type, type_embed[0], type_embed[1])

    def placed_at(value, row, lane):
        value = value.reshape(-1, value.shape[-1])
        return jnp.pad(value, ((row, 8 - row - value.shape[0]), (lane, width - lane - value.shape[1])))

    corner = placed_at(b_value, 0, 0)
    for number, value in enumerate(long_vectors[1:]):
        corner = corner + placed_at(value, number + 1, 0)
    for number, value in enumerate(head_vectors[:3]):
        corner = corner + placed_at(value, 0, (number + 3) * 128)
    for number, value in enumerate(head_vectors[3:]):
        corner = corner + placed_at(value, 3, (number + 3) * 128)
    early = lax.all_gather(jnp.concatenate([block, corner], axis=0), "fsdp", axis=0)
    qkvr = early[:, :local_rows].reshape(width, width)
    corners = early[:, local_rows:].astype(F32)
    full = [corners[:, n, : v.shape[0]].reshape(-1) for n, v in enumerate(long_vectors)]
    bv_full, bo_full, gain_one, shift_one, bback_full, gain_two, shift_two, bin_full = full
    heads = []
    for number, value in enumerate(head_vectors):
        row = 0 if number < 3 else 3
        lane = (number % 3 + 3) * 128
        each = corners[:, row : row + local_heads, lane : lane + value.shape[1]]
        heads.append(jnp.moveaxis(each, 0, 1).reshape(local_heads, DH))
    content_full, position_full, typebias_full, embed_zero, embed_one = heads
    bv_own = lax.dynamic_slice_in_dim(bv_full, own * local_cols, local_cols, 0)
    head = jnp.stack(
        [
            content_full,
            position_full,
            typebias_full,
            embed_zero,
            embed_one,
            bv_own.reshape(local_heads, DH),
        ],
        axis=1,
    )
    head = jnp.pad(head, ((0, 0), (0, 2), (0, 64)))

    deep = w_back.shape[0] // seqs
    late = jnp.concatenate(
        [
            lax.dynamic_slice_in_dim(w_in, own * width, width, 1),
            lax.dynamic_slice_in_dim(w_back, own * deep, deep, 0),
            head_columns(w_out),
            jnp.zeros((local_rows, 64), BF),
        ],
        axis=1,
    )
    late = lax.all_gather(late, ("fsdp", "seq"), axis=0).reshape(fsdps, seqs, local_rows, -1)
    if not direct:
        eighth_rows = width // 8
        turned_in = jnp.swapaxes(late, 1, 2).reshape(8, eighth_rows, seqs, -1)
        natural = late[..., width : 2 * width].reshape(8, seqs, eighth_rows, width)
        turned_in = jnp.swapaxes(turned_in, 1, 2)
        late = jnp.concatenate([turned_in[..., :width], natural, turned_in[..., 2 * width :]], axis=-1)

    longest = jnp.argmax(pack_sizes).astype(jnp.int32)
    start = jnp.sum(jnp.where(jnp.arange(3) < longest, pack_sizes, 0))
    near = jnp.sum(jnp.where(jnp.arange(3) == (longest + 1) % 3, pack_sizes, 0))
    parity = rank & 1
    place = jnp.stack([own, start, near, 1 + parity, 2 - parity]).astype(jnp.int32)
    row_index = jnp.arange(pack_rows, dtype=jnp.int32)
    position = jnp.where(
        row_index < LONGEST,
        row_index,
        jnp.where(row_index < LONGEST + near, row_index - LONGEST, row_index - LONGEST - near),
    )
    sine, cosine = angles_of(position, width)
    key_pos = jnp.concatenate([cosine, sine], axis=-1).astype(BF)
    key_pos_t = key_pos.T
    turned_types = lax.dynamic_slice_in_dim(
        jnp.concatenate([pack_types, pack_types]), start, pack_rows, 0
    )[:, None]
    wrel = qkvr[:, 3 * local_cols :].reshape(width, local_heads, DH)
    wrel_rows = jnp.pad(jnp.transpose(wrel, (1, 0, 2)), ((0, 0), (0, 0), (0, 64)))
    wrel_cols = jnp.pad(jnp.transpose(wrel, (1, 2, 0)), ((0, 0), (0, 64), (0, 0)))
    together = lambda n: qkvr[:, n * local_cols : (n + 1) * local_cols].reshape(width, local_heads, DH)
    paired = jnp.concatenate([together(0), together(1)], axis=2).reshape(width, 2 * local_cols)
    w_qkv = jnp.concatenate([paired, qkvr[:, 2 * local_cols : 3 * local_cols], jnp.zeros((width, 64), BF)], axis=1)

    pieces = [mine, to_first(mine), to_second(mine)]
    pieces.append(to_second(pieces[1]))
    qx, pq, kx, kxt, vx, vxt = project(place, pieces, w_qkv, head, turned_types)
    big, small, ox, *head_out = attend(place, qx, pq, kxt, vx, key_pos_t, wrel_cols, sine, cosine)
    order = own ^ jnp.arange(seqs, dtype=jnp.int32)
    deal = lambda v: [v[0], to_first(v[1]), to_second(v[2]), to_seq(v[3], 3)]
    attn = deal(head_out)
    mid_vectors = jnp.stack([bo_full, gain_one, shift_one, bback_full, gain_two, shift_two, gain_two, gain_two])
    result, hidden_low, act_low, pre_grad, ffn_grad, branch_grad, sum_one_grad, *douts, short_sums = middle(
        place, attn, mine, grad_output[0], late, mid_vectors, bin_full[None]
    )
    activations = result.reshape(1, row_count, width)
    douts = deal(douts)
    attn_rows = jnp.concatenate(attn, axis=1)
    devices = seqs * fsdps
    device = own * fsdps + rank
    fine = width // devices
    deep = act_low.shape[1] // devices
    kept_place = jnp.where((order == 1) | (order == 2), jnp.where(parity == 1, 3 - order, order), order)
    if direct:
        relative = jnp.arange(32, dtype=jnp.int32) ^ device
        bit = lambda n: (relative >> n) & 1
        flip = (bit(0) ^ parity) == 1
        one, two = jnp.where(flip, bit(4), bit(3)), jnp.where(flip, bit(3), bit(4))
        slots = one * 8 + two * 4 + bit(1) * 2 + bit(2)
        table = jnp.concatenate([device[None], slots, place[3:5]]).astype(jnp.int32)
        kept_in, sent_in = in_blocks(table, hidden_low, pre_grad, attn_rows, branch_grad, short_sums)
        core_in = to_core(sent_in)
        kept_back, sent_back = back_blocks(table, act_low, ffn_grad)
        parts = [kept_back, to_core(sent_back), kept_in, core_in]
        out = merge(parts, 8)
        douts, out = lax.optimization_barrier((douts, out))
        parts.append(to_first(out))
    else:
        scatter = lambda v: lax.psum_scatter(v, ("seq", "fsdp"), scatter_dimension=0, tiled=True)
        w_back_grad = scatter(contract_rows(act_low, ffn_grad))
        w_in_grad = scatter(contract_rows(hidden_low, pre_grad))
        spun = contract_rows(attn_rows, branch_grad).reshape(seqs, local_cols, width)
        w_out_grad = scatter(jnp.take(spun, kept_place, axis=0).reshape(width, width))

    tkeep, tsend, rel, sums = attend_back(
        place, douts, big, small, ox, qx, pq, kx, vxt, key_pos, wrel_rows, sine, cosine, turned_types, head
    )
    if direct:
        out = merge(parts, 4)
        tkeep, tsend, out = lax.optimization_barrier((tkeep, tsend, out))
        parts.append(to_second(out))
    dx_send = contract_cols(tsend, w_qkv).astype(BF)
    tkeep, tsend, dx_send = lax.optimization_barrier((tkeep, tsend, dx_send))
    dx_first = to_first(dx_send)
    dx_keep = contract_cols(tkeep, w_qkv)
    dx_out = (dx_keep[row_count:] + dx_first[row_count:].astype(F32)).astype(BF)
    if direct:
        spots = ((rank >> 1) ^ jnp.arange(4, dtype=jnp.int32)) & 3
        spots = (spots & 1) * 2 + (spots >> 1)
        qkv_table = jnp.concatenate([rank[None], spots]).astype(jnp.int32)
        kept, sent = qkv_blocks(qkv_table, pieces, tkeep, tsend, rel, sums)
        qkv_parts = [kept, to_core(sent)]
        dx_out, qkv_parts = lax.optimization_barrier((dx_out, qkv_parts))
    dx_second = to_second(dx_out)
    if direct:
        qkv_parts.append(to_near(outgoing(qkv_parts, 4)))
        parts.append(to_near(merge(parts, 2)))
    input_rows = sum_one_grad + dx_keep[:row_count] + dx_first[:row_count].astype(F32) + dx_second.astype(F32)
    input_rows = input_rows.astype(BF).reshape(fsdps, sliver_rows, width)
    if direct:
        input_rows, qkv_parts, parts = lax.optimization_barrier((input_rows, qkv_parts, parts))
    returned = lax.all_to_all(input_rows, "fsdp", split_axis=0, concat_axis=0, tiled=True)
    input_grad = reload(owners, returned)
    if direct:
        qkv_parts.append(to_far(outgoing(qkv_parts, 2)))
        parts.append(to_far(merge(parts, 1)))
        total = add_parts(qkv_parts, 0, 1)[0]
        cut = kept_back.shape[1]
        tails = [p[:, :cut] for p in parts[4:]]
        w_back_grad = add_parts(parts[:2] + tails, 0, 1)[0]
        tails = [p[:, cut:] for p in parts[4:]]
        in_total = add_parts(parts[2:4] + tails, 0, 1)[0]
        w_in_grad = jnp.concatenate([in_total[c * 24 : (c + 1) * 24] for c in range(4)], axis=1)
        w_out_grad = in_total[96:120]
        short_grads, in_bias_grad = in_total[120:128, :fine], in_total[126, :deep]
    else:
        short_sums = lax.psum(short_sums, ("seq", "fsdp"))
        short_grads = lax.dynamic_slice(short_sums, (0, device * fine), (8, fine))
        in_bias_grad = lax.dynamic_slice(short_sums, (8 + device * deep // width, device * deep % width), (1, deep))[0]
        grad = contract_rows(pieces[0], tkeep[:row_count]) + contract_rows(pieces[2], tkeep[row_count:])
        grad = grad + contract_rows(pieces[1], tsend[:row_count]) + contract_rows(pieces[3], tsend[row_count:])
        grad = jnp.swapaxes(grad.reshape(seqs, fsdps, fine, 640), 0, 1).reshape(fsdps, local_rows, 640)
        tall = rel.reshape(fsdps, local_rows, 256)
        bundle = jnp.concatenate([grad[..., :512], grad[..., 512:] + tall[..., :128], tall[..., 128:]], axis=2)
        notes = jnp.concatenate([sums[0], sums[1], sums[2], jnp.zeros((8, 384), F32)], axis=1)
        bundle = jnp.concatenate([bundle, jnp.broadcast_to(notes[None], (fsdps,) + notes.shape)], axis=1)
        total = lax.psum_scatter(bundle, "fsdp", scatter_dimension=0, tiled=True)[0]
    own_qkv = total[:local_rows].astype(BF).reshape(seqs, fine, width)
    block_for = lambda mask: lax.dynamic_index_in_dim(own_qkv, own ^ mask, 0, keepdims=True)
    swapped = jnp.concatenate(deal([block_for(m) for m in (0, place[3], place[4], 3)]), axis=0)
    swapped = jnp.take(swapped, kept_place, axis=0).astype(F32)
    both = swapped[:, :, : 2 * local_cols].reshape(seqs, fine, local_heads, 2, DH)
    both = jnp.transpose(both, (3, 1, 0, 2, 4)).reshape(2, fine, width)
    w_value_grad = jnp.transpose(swapped[:, :, 2 * local_cols : 3 * local_cols], (1, 0, 2)).reshape(fine, width)
    rel_total = total[:local_rows, 3 * local_cols :].reshape(local_rows, local_heads, DH)
    notes = total[local_rows:, :384].reshape(8, 3, 128)
    eighth = DH // fsdps
    mine_sums = lax.dynamic_slice(notes, (0, 0, rank * eighth), (8, 3, eighth))
    value_bias_grad = lax.dynamic_slice(notes[5, :, :DH].reshape(-1), (rank * fine,), (fine,))
    return (
        activations,
        input_grad,
        both[0],
        both[1],
        w_value_grad,
        value_bias_grad,
        w_out_grad,
        short_grads[4],
        short_grads[0],
        short_grads[1],
        w_in_grad,
        in_bias_grad,
        w_back_grad,
        short_grads[5],
        short_grads[2],
        short_grads[3],
        rel_total,
        mine_sums[0],
        mine_sums[1],
        mine_sums[2],
        mine_sums[3:5],
    )


def solution(mesh):
    placed = (
        P(None, ("seq", "fsdp"), None),
        P("fsdp", None),
        P("fsdp", None),
        P("fsdp", None),
        P("fsdp"),
        P("fsdp", None),
        P("fsdp"),
        P("fsdp"),
        P("fsdp"),
        P("fsdp", None),
        P("fsdp"),
        P("fsdp", None),
        P("fsdp"),
        P("fsdp"),
        P("fsdp"),
        P("fsdp", "seq", None),
        P("seq", "fsdp"),
        P("seq", "fsdp"),
        P("seq", "fsdp"),
        P(None, "seq", "fsdp"),
        P(),
        P(),
        P(),
        P("fsdp", "seq", None),
    )
    return jax.shard_map(
        shards,
        mesh=mesh,
        in_specs=placed,
        out_specs=(
            P("fsdp", "seq", None),
            P(None, ("seq", "fsdp"), None),
            P(("seq", "fsdp"), None),
            P(("seq", "fsdp"), None),
            P(("seq", "fsdp"), None),
            P(("seq", "fsdp")),
            P(("seq", "fsdp"), None),
            P(("seq", "fsdp")),
            P(("seq", "fsdp")),
            P(("seq", "fsdp")),
            P(("seq", "fsdp"), None),
            P(("seq", "fsdp")),
            P(("seq", "fsdp"), None),
            P(("seq", "fsdp")),
            P(("seq", "fsdp")),
            P(("seq", "fsdp")),
            P("fsdp", "seq", None),
            P("seq", "fsdp"),
            P("seq", "fsdp"),
            P("seq", "fsdp"),
            P(None, "seq", "fsdp"),
        ),
        check_vma=False,
    )
```

```python
import functools

import jax
import jax.numpy as jnp
from jax import lax
from jax.experimental import pallas as pl
from jax.experimental.pallas import tpu as pltpu
from jax.sharding import PartitionSpec as P

DH = 64
LONGEST = 1024
QB = 256
BLOCKED = -1e30
BF = jnp.bfloat16
F32 = jnp.float32
VM = pl.BlockSpec(memory_space=pltpu.VMEM)
SM = pl.BlockSpec(memory_space=pltpu.SMEM)
VMEM_LIMIT = 60 * 1024 * 1024


def lanes_of(rows, width=128):
    return lax.broadcasted_iota(jnp.int32, (rows, width), 1)


def split3(value):
    high = value.astype(BF).astype(F32)
    rest = value - high
    middle = rest.astype(BF).astype(F32)
    return high, middle, rest - middle


def masks_of(place):
    return 0, place[3], place[4], 3


def pick(lane, first, columns, base):
    for number, column in enumerate(columns):
        base = jnp.where(lane == first + number, column, base)
    return base


def project_body(place, x0, x1, x2, x3, w_ref, head_ref, tcol_ref, qx_ref, pq_ref, kx_ref, kxt_ref, vx_ref, vxt_ref, rolled):
    own, start, near = place[0], place[1], place[2]
    scale = DH ** -0.5
    rows = qx_ref.shape[1]
    part = x0.shape[0]
    for mask, piece in zip(masks_of(place), (x0, x1, x2, x3)):
        y = jnp.dot(piece[...], w_ref[...], preferred_element_type=F32)
        base = pl.multiple_of((own ^ mask) * part, 8)
        for c in range(5):
            column = y[:, c * 128 : (c + 1) * 128]
            rolled[c, pl.ds(base, part), :] = column
            rolled[c, pl.ds(pl.multiple_of(base + rows, 8), part), :] = column

    def block(r, carry):
        row = pl.multiple_of(r * QB, QB)
        lane = lanes_of(QB)
        kind = tcol_ref[pl.ds(row, QB), :]
        index = row + lax.broadcasted_iota(jnp.int32, (QB, 1), 0)
        small = index >= LONGEST
        first = jnp.where(small & (index < LONGEST + near), 1.0, 0.0)
        second = jnp.where(small & (index >= LONGEST + near), 1.0, 0.0)
        one = jnp.where(kind == 1, 1.0, 0.0)
        zero = 1.0 - one
        for h in range(3):
            both = rolled[h, pl.ds(start + row, QB), :].astype(BF).astype(F32)
            if h < 2:
                v = rolled[3, pl.ds(start + row, QB), :]
                v = v if h == 0 else pltpu.roll(v, 64, 1)
            else:
                v = rolled[4, pl.ds(start + row, QB), :]
            head = head_ref[h]
            content = (both + head[0:1]) * scale
            position = ((both + head[1:2]) * scale).astype(BF)
            typed = (both + head[2:3]) * scale
            differ = jnp.sum(typed * head[3:4], axis=1, keepdims=True)
            same = jnp.sum(typed * head[4:5], axis=1, keepdims=True)
            for_zero = jnp.where(kind == 1, differ, same)
            for_one = jnp.where(kind == 1, same, differ)
            columns = [*split3(for_zero), *split3(for_one), second * BLOCKED, first * BLOCKED]
            qx = pick(lane, 64, columns, jnp.where(lane < 64, content, 0.0)).astype(BF)
            qx_ref[h, pl.ds(row, QB), :] = qx
            raw = pltpu.roll(both, 64, 1)
            pq_ref[h, pl.ds(row, QB), :] = jnp.where(lane < 64, position.astype(F32), raw).astype(BF)
            kx = pick(lane, 64, [zero, zero, zero, one, one, one, first, second], jnp.where(lane < 64, raw, 0.0))
            kx_ref[h, pl.ds(row, QB), :] = kx.astype(BF)
            kxt_ref[h, :, pl.ds(row, QB)] = jnp.transpose(kx, (1, 0)).astype(BF)
            vx = jnp.where(lane < 64, v + head[5:6], jnp.where(lane < 67, 1.0, 0.0)).astype(BF)
            vx_ref[h, pl.ds(row, QB), :] = vx
            vxt_ref[h, :, pl.ds(row, QB)] = jnp.transpose(vx.astype(F32), (1, 0)).astype(BF)
        return carry

    lax.fori_loop(0, rows // QB, block, 0)


def project(place, pieces, w_qkv, head, tcol):
    rows = 4 * pieces[0].shape[0]
    tall = jax.ShapeDtypeStruct((3, rows, 128), BF)
    wide = jax.ShapeDtypeStruct((3, 128, rows), BF)
    return pl.pallas_call(
        project_body,
        in_specs=[SM] + [VM] * 7,
        out_specs=[VM] * 6,
        out_shape=[tall, tall, tall, wide, tall, wide],
        scratch_shapes=[pltpu.VMEM((5, 2 * rows, 128), F32)],
        compiler_params=pltpu.CompilerParams(vmem_limit_bytes=VMEM_LIMIT),
        cost_estimate=pl.CostEstimate(flops=2 * rows * 768 * 640, bytes_accessed=10_000_000, transcendentals=0),
        name="project",
    )(place, *pieces, w_qkv, head, tcol)


def attend_body(place, qx_ref, pq_ref, kxt_ref, vx_ref, kpt_ref, wrt_ref, sn_ref, cs_ref, big_ref, small_ref, ox_ref, o0, o1, o2, o3, keys, left, outs):
    h, i = pl.program_id(0), pl.program_id(1)
    own, start = place[0], place[1]
    width = kpt_ref.shape[0]
    half = width // 2
    rows = kpt_ref.shape[1]

    @pl.when((h == 0) & (i == 0))
    def _():
        keys[0:width, :] = kpt_ref[...]

    @pl.when(i == 0)
    def _():
        keys[width:, :] = kxt_ref[0]

    rel = jnp.dot(pq_ref[0], wrt_ref[0], preferred_element_type=F32)
    r1, r2 = rel[:, :half], rel[:, half:]
    sn, cs = sn_ref[...], cs_ref[...]
    left[:, 0:half] = (r1 * sn + r2 * cs).astype(BF)
    left[:, half:width] = (r2 * sn - r1 * cs).astype(BF)
    left[:, width:] = qx_ref[0]

    def attend(low, high, store):
        score = jnp.dot(left[...], keys[:, low:high], preferred_element_type=F32)
        top = jnp.max(score, axis=1, keepdims=True)
        raised = jnp.exp(score - top).astype(BF)
        store[0] = raised
        mixed = jnp.dot(raised, vx_ref[0, low:high, :], preferred_element_type=F32)
        inverse = 1.0 / mixed[:, 64:65]
        lane = lanes_of(QB)
        ox = jnp.where(lane < 64, mixed * inverse, jnp.where(lane == 64, inverse, 0.0))
        ox_ref[0] = ox
        row = pl.multiple_of(i * QB, QB)
        outs[h, pl.ds(row, QB), :] = ox
        outs[h, pl.ds(pl.multiple_of(row + rows, QB), QB), :] = ox

    @pl.when(i < LONGEST // QB)
    def _():
        attend(0, LONGEST, big_ref)

    @pl.when(i >= LONGEST // QB)
    def _():
        attend(LONGEST, rows, small_ref)

    @pl.when((h == 2) & (i == pl.num_programs(1) - 1))
    def _():
        part = o0.shape[0]
        for mask, out in zip(masks_of(place), (o0, o1, o2, o3)):
            at = lax.rem((own ^ mask) * part + rows - start, rows)
            out[...] = jnp.concatenate([outs[g, pl.ds(at, part), :][:, 0:64] for g in range(3)], axis=1).astype(BF)


def attend(place, qx, pq, kxt, vx, kpt, wrt, sn, cs):
    rows = qx.shape[1]
    width = kpt.shape[0]
    blocks = rows // QB
    bigs = LONGEST // QB
    rest = rows - LONGEST
    per_block = lambda h, i: (h, i, 0)
    per_head = lambda h, i: (h, 0, 0)
    whole2 = lambda h, i: (0, 0)
    part = rows // 4
    out_piece = jax.ShapeDtypeStruct((part, 192), BF)
    return pl.pallas_call(
        attend_body,
        grid=(3, blocks),
        in_specs=[
            SM,
            pl.BlockSpec((1, QB, 128), per_block),
            pl.BlockSpec((1, QB, 128), per_block),
            pl.BlockSpec((1, 128, rows), per_head),
            pl.BlockSpec((1, rows, 128), per_head),
            pl.BlockSpec((width, rows), whole2, pipeline_mode=pl.Buffered(1)),
            pl.BlockSpec((1, 128, width), per_head),
            pl.BlockSpec((QB, width // 2), lambda h, i: (i, 0)),
            pl.BlockSpec((QB, width // 2), lambda h, i: (i, 0)),
        ],
        out_specs=[
            pl.BlockSpec((1, QB, LONGEST), lambda h, i: (h, jnp.minimum(i, bigs - 1), 0)),
            pl.BlockSpec((1, QB, rest), lambda h, i: (h, jnp.maximum(i - bigs, 0), 0)),
            pl.BlockSpec((1, QB, 128), per_block),
        ]
        + [pl.BlockSpec((part, 192), whole2)] * 4,
        out_shape=[
            jax.ShapeDtypeStruct((3, LONGEST, LONGEST), BF),
            jax.ShapeDtypeStruct((3, rest, rest), BF),
            jax.ShapeDtypeStruct((3, rows, 128), F32),
        ]
        + [out_piece] * 4,
        scratch_shapes=[
            pltpu.VMEM((width + 128, rows), BF),
            pltpu.VMEM((QB, width + 128), BF),
            pltpu.VMEM((3, 2 * rows, 128), F32),
        ],
        compiler_params=pltpu.CompilerParams(vmem_limit_bytes=VMEM_LIMIT, dimension_semantics=("arbitrary", "arbitrary")),
        cost_estimate=pl.CostEstimate(flops=12_000_000_000, bytes_accessed=20_000_000, transcendentals=4_000_000),
        name="attend",
    )(place, qx, pq, kxt, vx, kpt, wrt, sn, cs)


def back_body(place, d0, d1, d2, d3, big_ref, small_ref, ox_ref, qx_ref, pq_ref, kx_ref, vxt_ref, kp_ref, wr_ref, sn_ref, cs_ref, tcol_ref, head_ref, gkeep_ref, gsend_ref, rel_ref, sum_ref, douts, dkt, dvt, gwt, grads):
    h, i = pl.program_id(0), pl.program_id(1)
    own, start = place[0], place[1]
    rows, width = kp_ref.shape
    half = width // 2
    scale = DH ** -0.5
    part = d0.shape[0]
    last = pl.num_programs(1) - 1
    row = pl.multiple_of(i * QB, QB)
    again = pl.multiple_of(row + rows, QB)

    @pl.when((h == 0) & (i == 0))
    def _():
        blank = jnp.zeros((part, 64), F32)
        for mask, piece in zip(masks_of(place), (d0, d1, d2, d3)):
            values = piece[...].astype(F32)
            base = pl.multiple_of((own ^ mask) * part, 8)
            for g in range(3):
                padded = jnp.concatenate([values[:, g * 64 : (g + 1) * 64], blank], axis=1)
                douts[g, pl.ds(base, part), :] = padded
                douts[g, pl.ds(pl.multiple_of(base + rows, 8), part), :] = padded

    @pl.when(i == 0)
    def _():
        dkt[...] = jnp.zeros_like(dkt)
        dvt[...] = jnp.zeros_like(dvt)
        gwt[...] = jnp.zeros_like(gwt)
        sum_ref[...] = jnp.zeros_like(sum_ref)

    lane = lanes_of(QB)
    dout = douts[h, pl.ds(start + row, QB), :]
    ox = ox_ref[0]
    inverse = ox[:, 64:65]
    dot_row = jnp.sum(dout * ox, axis=1, keepdims=True)
    dox = pick(lane, 64, [-x for x in split3(dot_row)], dout).astype(BF)
    dout_t = jnp.transpose(dout * inverse, (1, 0))[0:64].astype(BF)
    qx = qx_ref[0]
    qc_t = jnp.transpose(qx.astype(F32), (1, 0))[0:64].astype(BF)
    pq = pq_ref[0].astype(F32)
    qp_t = jnp.transpose(pq, (1, 0))[0:64].astype(BF)
    sn, cs = sn_ref[...], cs_ref[...]

    def back(low, high, saved):
        raised = saved[0]
        dprob = jnp.dot(dox, vxt_ref[0, :, low:high], preferred_element_type=F32)
        dscore = (raised.astype(F32) * (dprob * inverse)).astype(BF)
        dvt[:, low:high] += jnp.dot(dout_t, raised, preferred_element_type=F32)
        dkt[:, low:high] += jnp.dot(qc_t, dscore, preferred_element_type=F32)
        da = jnp.dot(dscore, kp_ref[low:high, :], preferred_element_type=F32)
        dqx = jnp.dot(dscore, kx_ref[0, low:high, :], preferred_element_type=F32)
        da1, da2 = da[:, 0:half], da[:, half:width]
        drel = jnp.concatenate([(da1 * sn - da2 * cs).astype(BF), (da1 * cs + da2 * sn).astype(BF)], axis=1)
        dqp = jnp.dot(drel, wr_ref[0], preferred_element_type=F32)
        gwt[...] += jnp.dot(qp_t, drel, preferred_element_type=F32)
        kind = tcol_ref[...]
        over_zero, over_one = dqx[:, 64:65], dqx[:, 67:68]
        same = jnp.where(kind == 1, over_one, over_zero)
        differ = jnp.where(kind == 1, over_zero, over_one)
        head = head_ref[0]
        dqt = differ * head[3:4] + same * head[4:5]
        dqc = jnp.where(lane < 64, dqx, 0.0)
        dq = (dqc + dqp + dqt) * scale
        grads[h, pl.ds(row, QB), :] = dq
        typed = (pltpu.roll(pq, 64, 1) + head[2:3]) * scale
        sums = [dqc * scale, dqp * scale, dqt * scale, differ * typed, same * typed]
        for number, values in enumerate(sums):
            sum_ref[0, number : number + 1, :] += jnp.sum(values, axis=0, keepdims=True)

    @pl.when(i < LONGEST // QB)
    def _():
        back(0, LONGEST, big_ref)

    @pl.when(i >= LONGEST // QB)
    def _():
        back(LONGEST, rows, small_ref)

    @pl.when(i == last)
    def _():
        dk = jnp.transpose(dkt[...], (1, 0))
        dq = grads[h, 0:rows, :]
        pair = jnp.concatenate([dq[:, 0:64], dk], axis=1)
        grads[h, 0:rows, :] = pair
        grads[h, rows : 2 * rows, :] = pair
        dv = jnp.transpose(dvt[...], (1, 0)).astype(BF).astype(F32)
        sum_ref[0, 5:6, 0:64] = jnp.sum(dv, axis=0, keepdims=True)
        blank = jnp.zeros_like(dv)
        rel = jnp.transpose(gwt[...], (1, 0))
        empty = jnp.zeros_like(rel)

        @pl.when(h == 0)
        def _():
            padded = jnp.concatenate([dv, blank], axis=1)
            grads[3, 0:rows, :] = padded
            grads[3, rows : 2 * rows, :] = padded
            rel_ref[:, 0:128] = jnp.concatenate([empty, rel], axis=1)

        @pl.when(h == 1)
        def _():
            rel_ref[:, 128:256] = jnp.concatenate([rel, empty], axis=1)
            padded = grads[3, 0:rows, :] + jnp.concatenate([blank, dv], axis=1)
            grads[3, 0:rows, :] = padded
            grads[3, rows : 2 * rows, :] = padded

        @pl.when(h == 2)
        def _():
            padded = jnp.concatenate([dv, blank], axis=1)
            grads[4, 0:rows, :] = padded
            grads[4, rows : 2 * rows, :] = padded
            rel_ref[:, 128:256] += jnp.concatenate([empty, rel], axis=1)
            spots = ((gkeep_ref, 0), (gsend_ref, 0), (gkeep_ref, part), (gsend_ref, part))
            for mask, (out, low) in zip(masks_of(place), spots):
                at = lax.rem((own ^ mask) * part + rows - start, rows)
                for c in range(5):
                    out[low : low + part, c * 128 : (c + 1) * 128] = grads[c, pl.ds(at, part), :].astype(BF)


def attend_back(place, douts, big, small, ox, qx, pq, kx, vxt, kp, wr, sn, cs, tcol, head):
    rows, width = kp.shape
    blocks = rows // QB
    bigs = LONGEST // QB
    rest = rows - LONGEST
    part = rows // 4
    per_block = lambda h, i: (h, i, 0)
    per_head = lambda h, i: (h, 0, 0)
    whole2 = lambda h, i: (0, 0)
    return pl.pallas_call(
        back_body,
        grid=(3, blocks),
        in_specs=[SM]
        + [pl.BlockSpec((part, 192), whole2)] * 4
        + [
            pl.BlockSpec((1, QB, LONGEST), lambda h, i: (h, jnp.minimum(i, bigs - 1), 0)),
            pl.BlockSpec((1, QB, rest), lambda h, i: (h, jnp.maximum(i - bigs, 0), 0)),
            pl.BlockSpec((1, QB, 128), per_block),
            pl.BlockSpec((1, QB, 128), per_block),
            pl.BlockSpec((1, QB, 128), per_block),
            pl.BlockSpec((1, rows, 128), per_head),
            pl.BlockSpec((1, 128, rows), per_head),
            pl.BlockSpec((rows, width), whole2, pipeline_mode=pl.Buffered(1)),
            pl.BlockSpec((1, width, 128), per_head),
            pl.BlockSpec((QB, width // 2), lambda h, i: (i, 0)),
            pl.BlockSpec((QB, width // 2), lambda h, i: (i, 0)),
            pl.BlockSpec((QB, 1), lambda h, i: (i, 0)),
            pl.BlockSpec((1, 8, 128), per_head),
        ],
        out_specs=[pl.BlockSpec((2 * part, 640), whole2)] * 2
        + [pl.BlockSpec((width, 256), whole2), pl.BlockSpec((1, 8, 128), per_head)],
        out_shape=[jax.ShapeDtypeStruct((2 * part, 640), BF)] * 2
        + [jax.ShapeDtypeStruct((width, 256), F32), jax.ShapeDtypeStruct((3, 8, 128), F32)],
        scratch_shapes=[
            pltpu.VMEM((3, 2 * rows, 128), F32),
            pltpu.VMEM((64, rows), F32),
            pltpu.VMEM((64, rows), F32),
            pltpu.VMEM((64, width), F32),
            pltpu.VMEM((5, 2 * rows, 128), F32),
        ],
        compiler_params=pltpu.CompilerParams(vmem_limit_bytes=VMEM_LIMIT, dimension_semantics=("arbitrary", "arbitrary")),
        cost_estimate=pl.CostEstimate(flops=20_000_000_000, bytes_accessed=25_000_000, transcendentals=0),
        name="attend_back",
    )(place, *douts, big, small, ox, qx, pq, kx, vxt, kp, wr, sn, cs, tcol, head)


def reload_body(outward, owners, in_ref, out_ref):
    def move(j, carry):
        if outward:
            out_ref[owners[j]] = in_ref[j]
        else:
            out_ref[j] = in_ref[owners[j]]
        return carry

    lax.fori_loop(0, out_ref.shape[0], move, 0)


def reload(owners, rows, outward):
    return pl.pallas_call(
        functools.partial(reload_body, outward),
        in_specs=[SM, VM],
        out_specs=VM,
        out_shape=jax.ShapeDtypeStruct(rows.shape, rows.dtype),
        compiler_params=pltpu.CompilerParams(vmem_limit_bytes=VMEM_LIMIT),
        name="deal" if outward else "reload",
    )(owners, rows)


def qkv_blocks_body(x0, x1, x2, x3, tkeep_ref, tsend_ref, rel_ref, sums_ref, out_ref, acc):
    part = x0.shape[0]
    count, high, _ = out_ref.shape
    rows = high - 8
    fine = rows // 4
    parts = ((x0, tkeep_ref, 0), (x2, tkeep_ref, part), (x1, tsend_ref, 0), (x3, tsend_ref, part))
    for number, (x, t, low) in enumerate(parts):
        value = lax.dot_general(x[...], t[low : low + part, :], (((0,), (0,)), ((), ())), preferred_element_type=F32)
        acc[...] = value if number == 0 else acc[...] + value
    notes = jnp.concatenate([sums_ref[0], sums_ref[1], sums_ref[2], jnp.zeros((8, 384), F32)], axis=1).astype(BF)
    for f in range(count):
        for s in range(4):
            value = acc[(count * s + f) * fine : (count * s + f + 1) * fine, :]
            rel = rel_ref[rows * f + fine * s : rows * f + fine * (s + 1), :]
            low, high = fine * s, fine * (s + 1)
            out_ref[f, low:high, 0:512] = value[:, 0:512].astype(BF)
            out_ref[f, low:high, 512:640] = (value[:, 512:640] + rel[:, 0:128]).astype(BF)
            out_ref[f, low:high, 640:768] = rel[:, 128:256].astype(BF)
        out_ref[f, rows : rows + 8, :] = notes


def qkv_blocks(count, pieces, tkeep, tsend, rel, sums):
    width = pieces[0].shape[1]
    return pl.pallas_call(
        qkv_blocks_body,
        in_specs=[VM] * 8,
        out_specs=VM,
        out_shape=jax.ShapeDtypeStruct((count, width // count + 8, width), BF),
        scratch_shapes=[pltpu.VMEM((width, 640), F32)],
        compiler_params=pltpu.CompilerParams(vmem_limit_bytes=VMEM_LIMIT),
        cost_estimate=pl.CostEstimate(flops=2_000_000_000, bytes_accessed=8_000_000, transcendentals=0),
        name="qkv_blocks",
    )(*pieces, tkeep, tsend, rel, sums)


def merge_body(split, *refs):
    count = len(refs) - (2 if split else 1)
    sums = []
    for group in (refs[: count // 2], refs[count // 2 : count]):
        total = group[0][...].astype(F32)
        for ref in group[1:]:
            total = total + ref[...].astype(F32)
        sums.append(total.astype(BF))
    if split:
        refs[count][...], refs[count + 1][...] = sums
    else:
        cut = sums[0].shape[1]
        refs[count][:, :cut, :] = sums[0]
        refs[count][:, cut:, :] = sums[1]


def merge(backs, ins, half, split=True):
    step = min(half, 2)
    first = half // step
    width = backs[0].shape[2]
    heights = [backs[0].shape[1], ins[0].shape[1]]
    heights = heights if split else [sum(heights)]
    block = lambda p: pl.BlockSpec((step,) + p.shape[1:], lambda g: (first + g, 0, 0))
    parts = backs + ins
    return pl.pallas_call(
        functools.partial(merge_body, split),
        grid=(first,),
        in_specs=[block(p) for p in parts],
        out_specs=[pl.BlockSpec((step, h, width), lambda g: (g, 0, 0)) for h in heights],
        out_shape=[jax.ShapeDtypeStruct((half, h, width), BF) for h in heights],
        compiler_params=pltpu.CompilerParams(vmem_limit_bytes=VMEM_LIMIT, dimension_semantics=("arbitrary",)),
        cost_estimate=pl.CostEstimate(flops=half * 224 * width * 6, bytes_accessed=half * 224 * width * 8, transcendentals=0),
        name="merge",
    )(*parts)


EPS = 1e-09
GELU_A = (2.0 / 3.141592653589793) ** 0.5
GELU_B = 0.044715

def spread_norm(values):
    center = values - jnp.mean(values, axis=1, keepdims=True)
    inverse = lax.rsqrt(jnp.mean(center * center, axis=1, keepdims=True) + EPS)
    return center * inverse, inverse


def middle_body(
    place, a0, a1, a2, a3, x_ref, go_ref, w_ref, vec_ref, bin_ref,
    act_ref, h_ref, u_ref, dz_ref, df_ref, dbr_ref, dr_ref, d0, d1, d2, d3, sum_ref,
    wout, slope, high, normed, acc,
):
    own = place[0]
    width = x_ref.shape[1]
    cols = a0.shape[1]
    vector = lambda n: vec_ref[n : n + 1, :]
    for s in range(4):
        piece = w_ref[:, s, :, 2 * width : 2 * width + cols]
        wout[:, s * cols : (s + 1) * cols] = piece.reshape(width, cols)
    part = lambda mask: wout[pl.ds(pl.multiple_of((own ^ mask) * cols, 64), cols), :]
    masks = masks_of(place)
    total = x_ref[...].astype(F32) + vector(0)
    for mask, piece in zip(masks, (a0, a1, a2, a3)):
        total = total + jnp.dot(piece[...], part(mask), preferred_element_type=F32)
    unit, inverse_one = spread_norm(total)
    normed[...] = unit
    first = unit * vector(1) + vector(2)
    high[...] = first
    h_ref[...] = first.astype(BF)
    acc[...] = first + vector(3)

    def w_in_at(w):
        return w_ref[:, w, :, 0:width].reshape(width, width)

    def w_back_at(w):
        return w_ref[pl.ds(2 * w, 2), :, :, width : 2 * width].reshape(width, width)

    def forward(w, carry):
        at = pl.multiple_of(w * width, 128)
        z = jnp.dot(h_ref[...], w_in_at(w), preferred_element_type=F32) + bin_ref[:, pl.ds(at, width)]
        square = z * z
        bend = jnp.tanh(GELU_A * z * (1.0 + GELU_B * square))
        half = 0.5 + 0.5 * bend
        u = (z * half).astype(BF)
        u_ref[:, pl.ds(at, width)] = u
        slope[:, pl.ds(at, width)] = half + 0.5 * z * (1.0 - bend * bend) * (GELU_A * (1.0 + 3.0 * GELU_B * square))
        acc[...] += jnp.dot(u, w_back_at(w), preferred_element_type=F32)
        return carry

    lax.fori_loop(0, 4, forward, 0)
    unit, inverse_two = spread_norm(acc[...])
    act_ref[...] = (unit * vector(4) + vector(5)).astype(BF)

    def back(gradient, unit, inverse, gain):
        scaled = gradient * gain
        inner = scaled - jnp.mean(scaled, axis=1, keepdims=True)
        return (inner - unit * jnp.mean(scaled * unit, axis=1, keepdims=True)) * inverse

    def note(row, values):
        sum_ref[row : row + 1, :] = jnp.sum(values, axis=0, keepdims=True)

    gradient = go_ref[...].astype(F32)
    note(2, gradient * unit)
    note(3, gradient)
    second = back(gradient, unit, inverse_two, vector(4))
    df = second.astype(BF)
    df_ref[...] = df
    note(5, df.astype(F32))
    acc[...] = second

    def backward(w, carry):
        at = pl.multiple_of(w * width, 128)
        du = lax.dot_general(df_ref[...], w_back_at(w), (((1,), (1,)), ((), ())), preferred_element_type=F32)
        dz = (slope[:, pl.ds(at, width)] * du).astype(BF)
        dz_ref[:, pl.ds(at, width)] = dz
        sum_ref[pl.ds(8 + w, 1), :] = jnp.sum(dz.astype(F32), axis=0, keepdims=True)
        acc[...] += lax.dot_general(dz, w_in_at(w), (((1,), (1,)), ((), ())), preferred_element_type=F32)
        return carry

    lax.fori_loop(0, 4, backward, 0)
    gradient = acc[...]
    unit = normed[...]
    note(0, gradient * unit)
    note(1, gradient)
    dr = back(gradient, unit, inverse_one, vector(1))
    dr_ref[...] = dr
    dbr = dr.astype(BF)
    dbr_ref[...] = dbr
    note(4, dbr.astype(F32))
    sum_ref[6:8, :] = jnp.zeros((2, width), F32)
    sum_ref[12:16, :] = jnp.zeros((4, width), F32)
    for mask, out in zip(masks, (d0, d1, d2, d3)):
        value = lax.dot_general(dbr, part(mask), (((1,), (1,)), ((), ())), preferred_element_type=F32)
        out[...] = value.astype(BF)


def middle(place, pieces, x, out_grad, weights, vectors, bin_full):
    rows, width = x.shape
    cols = pieces[0].shape[1]
    hidden = bin_full.shape[1]
    low = lambda n: jax.ShapeDtypeStruct((rows, n), BF)
    full = lambda r, n: jax.ShapeDtypeStruct((r, n), F32)
    return pl.pallas_call(
        middle_body,
        in_specs=[SM] + [VM] * 9,
        out_specs=[VM] * 12,
        out_shape=[low(width), low(width), low(hidden), low(hidden), low(width), low(width), full(rows, width)]
        + [low(cols)] * 4
        + [full(16, width)],
        scratch_shapes=[
            pltpu.VMEM((width, width), BF),
            pltpu.VMEM((rows, hidden), F32),
            pltpu.VMEM((rows, width), F32),
            pltpu.VMEM((rows, width), F32),
            pltpu.VMEM((rows, width), F32),
        ],
        compiler_params=pltpu.CompilerParams(vmem_limit_bytes=VMEM_LIMIT),
        cost_estimate=pl.CostEstimate(flops=8_000_000_000, bytes_accessed=20_000_000, transcendentals=1_000_000),
        name="middle",
    )(place, *pieces, x, out_grad, weights, vectors, bin_full)


def angles_of(position, width):
    half_width = width // 2
    rate_table = 10000.0 ** (-(jnp.arange(half_width, dtype=jnp.float32) / half_width))
    turned = position.astype(jnp.float32)[:, None] * rate_table[None, :]
    return (jnp.sin(turned), jnp.cos(turned))


def contract_rows(left, right):
    return lax.dot_general(
        left, right, (((0,), (0,)), ((), ())), preferred_element_type=jnp.float32
    )


def contract_cols(left, right):
    return lax.dot_general(
        left, right, (((1,), (1,)), ((), ())), preferred_element_type=jnp.float32
    )


def across(values, other):
    seqs, fsdps = lax.axis_size("seq"), lax.axis_size("fsdp")
    pairs = []
    for s in range(seqs):
        for f in range(fsdps):
            to_s, to_f = other(s, f)
            pairs.append((s * fsdps + f, to_s * fsdps + to_f))
    return lax.ppermute(values, ("seq", "fsdp"), pairs)


def to_core(values):
    return across(values, lambda s, f: (s, f ^ 1))


def to_first(values):
    return across(values, lambda s, f: (s ^ (2 if f & 1 else 1), f))


def to_second(values):
    return across(values, lambda s, f: (s ^ (1 if f & 1 else 2), f))


def to_near(values):
    return across(values, lambda s, f: (s, f ^ 2))


def to_far(values):
    return across(values, lambda s, f: (s, f ^ 4))


def to_seq(values, k):
    return across(values, lambda s, f: (s ^ k, f))


def add_parts(parts, low, high):
    total = parts[0][low:high].astype(F32)
    for part in parts[1:]:
        total = total + part[low:high].astype(F32)
    return total


def back_blocks_body(place, u_ref, df_ref, keep_ref, send_ref):
    core = lax.rem(place[0], 2)
    group = u_ref.shape[1] // 4
    for g in range(1):
        acc = lax.dot_general(u_ref[...], df_ref[...], (((0,), (0,)), ((), ())), preferred_element_type=F32)
        at = pl.program_id(0) * 4
        for j in range(4):
            slot = place[1 + at + j]
            value = acc[j * group : (j + 1) * group].astype(BF)

            @pl.when(core == j % 2)
            def _():
                keep_ref[slot] = value

            @pl.when(core != j % 2)
            def _():
                send_ref[slot] = value


def back_blocks(place, u, df):
    rows, hidden = u.shape
    width = df.shape[1]
    out = jax.ShapeDtypeStruct((16, hidden // 32, width), BF)
    return pl.pallas_call(
        back_blocks_body,
        grid=(8,),
        in_specs=[SM, pl.BlockSpec((rows, hidden // 8), lambda g: (0, g)), pl.BlockSpec((rows, width), lambda g: (0, 0))],
        out_specs=[pl.BlockSpec((16, hidden // 32, width), lambda g: (0, 0, 0))] * 2,
        out_shape=[out, out],
        compiler_params=pltpu.CompilerParams(vmem_limit_bytes=VMEM_LIMIT, dimension_semantics=("arbitrary",)),
        cost_estimate=pl.CostEstimate(flops=2 * rows * hidden * width, bytes_accessed=8_000_000, transcendentals=0),
        name="back_blocks",
    )(place, u, df)


def in_blocks_body(place, h_ref, dz_ref, a0, a1, a2, a3, db_ref, sum_ref, keep_ref, send_ref):
    even = lax.rem(place[0], 2) == 0
    core = lax.rem(place[0], 2)
    own = lax.div(place[0], 8)
    step = pl.program_id(0)

    def store(block, low, a, b):
        count = a.shape[0]
        keep_ref[place[1 + block + core], pl.ds(low, count), :] = jnp.where(even, a, b).astype(BF)
        send_ref[place[2 + block - core], pl.ds(low, count), :] = jnp.where(even, b, a).astype(BF)

    def put(block, low, acc):
        store(block, low, acc[0:24], acc[24:48])

    def chunk(which):
        for g in range(2):
            acc = lax.dot_general(
                h_ref[:, g * 384 : (g + 1) * 384], dz_ref[...], (((0,), (0,)), ((), ())), preferred_element_type=F32
            )
            for j in range(0, 16, 2):
                put(g * 16 + j, which * 24, acc[j * 24 : (j + 2) * 24])

    for which in range(4):
        pl.when(step == which)(lambda which=which: chunk(which))

    @pl.when(step == 4)
    def _():
        for mask, piece in zip((0, place[33], place[34], 3), (a0, a1, a2, a3)):
            acc = lax.dot_general(piece[...], db_ref[...], (((0,), (0,)), ((), ())), preferred_element_type=F32)
            for j in range(0, 8, 2):
                put((own ^ mask) * 8 + j, 96, acc[j * 24 : (j + 2) * 24])
        width = sum_ref.shape[1]
        line = lax.broadcasted_iota(jnp.int32, (8, width), 0)

        def note(j):
            wide = sum_ref[8 + j // 8 : 9 + j // 8, :] + jnp.zeros((8, width), F32)
            short, wide = (
                pltpu.roll(v, shift, 1) if shift % width else v
                for v, shift in ((sum_ref[0:8, :], width - 24 * j), (wide, width - 96 * (j % 8)))
            )
            return jnp.where(line == 6, wide, short)

        for j in range(0, 32, 2):
            store(j, 120, note(j), note(j + 1))


def in_blocks(place, hidden_low, dz, attn, dbr, sums):
    rows, width = hidden_low.shape
    chunks = dz.shape[1] // width
    out = jax.ShapeDtypeStruct((16, 128, width), BF)
    whole = pl.BlockSpec((rows, width), lambda g: (0, 0))
    return pl.pallas_call(
        in_blocks_body,
        grid=(chunks + 1,),
        in_specs=[SM, whole, pl.BlockSpec((rows, width), lambda g: (0, jnp.minimum(g, chunks - 1)))]
        + [pl.BlockSpec(attn[0].shape, lambda g: (0, 0))] * 4
        + [whole]
        + [pl.BlockSpec(sums.shape, lambda g: (0, 0))],
        out_specs=[pl.BlockSpec((16, 128, width), lambda g: (0, 0, 0))] * 2,
        out_shape=[out, out],
        compiler_params=pltpu.CompilerParams(vmem_limit_bytes=VMEM_LIMIT, dimension_semantics=("arbitrary",)),
        cost_estimate=pl.CostEstimate(flops=2 * rows * width * (dz.shape[1] + width), bytes_accessed=12_000_000, transcendentals=0),
        name="in_blocks",
    )(place, hidden_low, dz, *attn, dbr, sums)


def shards(
    inputs,
    w_query,
    w_key,
    w_value,
    b_value,
    w_out,
    b_out,
    norm1_gain,
    norm1_bias,
    w_in,
    b_in,
    w_back,
    b_back,
    norm2_gain,
    norm2_bias,
    w_relative,
    bias_content,
    bias_position,
    bias_type,
    type_embed,
    lengths,
    token_types,
    owners,
    grad_output,
):
    seqs, fsdps = lax.axis_size("seq"), lax.axis_size("fsdp")
    direct = seqs == 4 and fsdps == 8
    own, rank = lax.axis_index("seq"), lax.axis_index("fsdp")
    pack_count = owners.shape[0]
    sliver_rows = inputs.shape[1]
    width = inputs.shape[2]
    local_rows = w_query.shape[0]
    local_cols = width // seqs
    local_heads = w_relative.shape[1]
    scale = DH ** -0.5
    dealt = reload(owners, inputs, True)
    mine = lax.all_to_all(dealt, "fsdp", split_axis=0, concat_axis=1, tiled=True)[0]
    row_count = mine.shape[0]
    chosen = (owners == rank).astype(jnp.int32)
    pack_types = jnp.sum(chosen[:, None] * token_types, axis=0)
    pack_sizes = jnp.sum(chosen[:, None] * lengths, axis=0)
    pack_rows = pack_types.shape[0]

    def head_columns(weight):
        return lax.dynamic_slice_in_dim(weight, own * local_cols, local_cols, 1)

    block = jnp.concatenate(
        [head_columns(w) for w in (w_query, w_key, w_value)] + [w_relative.reshape(local_rows, local_cols)], axis=1
    )
    long_vectors = (b_value, b_out, norm1_gain, norm1_bias, b_back, norm2_gain, norm2_bias, b_in)
    head_vectors = (bias_content, bias_position, bias_type, type_embed[0], type_embed[1])

    def placed_at(value, row, lane):
        value = value.reshape(-1, value.shape[-1])
        return jnp.pad(value, ((row, 8 - row - value.shape[0]), (lane, width - lane - value.shape[1])))

    corner = placed_at(b_value, 0, 0)
    for number, value in enumerate(long_vectors[1:]):
        corner = corner + placed_at(value, number + 1, 0)
    for number, value in enumerate(head_vectors[:3]):
        corner = corner + placed_at(value, 0, (number + 3) * 128)
    for number, value in enumerate(head_vectors[3:]):
        corner = corner + placed_at(value, 3, (number + 3) * 128)
    early = lax.all_gather(jnp.concatenate([block, corner], axis=0), "fsdp", axis=0)
    qkvr = early[:, :local_rows].reshape(width, width)
    corners = early[:, local_rows:].astype(F32)
    full = [corners[:, n, : v.shape[0]].reshape(-1) for n, v in enumerate(long_vectors)]
    bv_full, bo_full, gain_one, shift_one, bback_full, gain_two, shift_two, bin_full = full
    heads = []
    for number, value in enumerate(head_vectors):
        row = 0 if number < 3 else 3
        lane = (number % 3 + 3) * 128
        each = corners[:, row : row + local_heads, lane : lane + value.shape[1]]
        heads.append(jnp.moveaxis(each, 0, 1).reshape(local_heads, DH))
    content_full, position_full, typebias_full, embed_zero, embed_one = heads
    bv_own = lax.dynamic_slice_in_dim(bv_full, own * local_cols, local_cols, 0)
    head = jnp.stack(
        [
            content_full,
            position_full,
            typebias_full,
            embed_zero,
            embed_one,
            bv_own.reshape(local_heads, DH),
        ],
        axis=1,
    )
    head = jnp.pad(head, ((0, 0), (0, 2), (0, 64)))

    deep = w_back.shape[0] // seqs
    late = jnp.concatenate(
        [
            lax.dynamic_slice_in_dim(w_in, own * width, width, 1),
            lax.dynamic_slice_in_dim(w_back, own * deep, deep, 0),
            head_columns(w_out),
            jnp.zeros((local_rows, 64), BF),
        ],
        axis=1,
    )
    late = lax.all_gather(late, ("fsdp", "seq"), axis=0).reshape(fsdps, seqs, local_rows, -1)
    if not direct:
        eighth_rows = width // 8
        turned_in = jnp.swapaxes(late, 1, 2).reshape(8, eighth_rows, seqs, -1)
        natural = late[..., width : 2 * width].reshape(8, seqs, eighth_rows, width)
        turned_in = jnp.swapaxes(turned_in, 1, 2)
        late = jnp.concatenate([turned_in[..., :width], natural, turned_in[..., 2 * width :]], axis=-1)

    longest = jnp.argmax(pack_sizes).astype(jnp.int32)
    start = jnp.sum(jnp.where(jnp.arange(3) < longest, pack_sizes, 0))
    near = jnp.sum(jnp.where(jnp.arange(3) == (longest + 1) % 3, pack_sizes, 0))
    parity = rank & 1
    place = jnp.stack([own, start, near, 1 + parity, 2 - parity]).astype(jnp.int32)
    row_index = jnp.arange(pack_rows, dtype=jnp.int32)
    position = jnp.where(
        row_index < LONGEST,
        row_index,
        jnp.where(row_index < LONGEST + near, row_index - LONGEST, row_index - LONGEST - near),
    )
    sine, cosine = angles_of(position, width)
    key_pos = jnp.concatenate([cosine, sine], axis=-1).astype(BF)
    key_pos_t = key_pos.T
    turned_types = lax.dynamic_slice_in_dim(
        jnp.concatenate([pack_types, pack_types]), start, pack_rows, 0
    )[:, None]
    wrel = qkvr[:, 3 * local_cols :].reshape(width, local_heads, DH)
    wrel_rows = jnp.pad(jnp.transpose(wrel, (1, 0, 2)), ((0, 0), (0, 0), (0, 64)))
    wrel_cols = jnp.pad(jnp.transpose(wrel, (1, 2, 0)), ((0, 0), (0, 64), (0, 0)))
    together = lambda n: qkvr[:, n * local_cols : (n + 1) * local_cols].reshape(width, local_heads, DH)
    paired = jnp.concatenate([together(0), together(1)], axis=2).reshape(width, 2 * local_cols)
    w_qkv = jnp.concatenate([paired, qkvr[:, 2 * local_cols : 3 * local_cols], jnp.zeros((width, 64), BF)], axis=1)

    pieces = [mine, to_first(mine), to_second(mine)]
    pieces.append(to_second(pieces[1]))
    pieces, wrel_rows = lax.optimization_barrier((pieces, wrel_rows))
    qx, pq, kx, kxt, vx, vxt = project(place, pieces, w_qkv, head, turned_types)
    big, small, ox, *head_out = attend(place, qx, pq, kxt, vx, key_pos_t, wrel_cols, sine, cosine)
    order = own ^ jnp.arange(seqs, dtype=jnp.int32)
    deal = lambda v: [v[0], to_first(v[1]), to_second(v[2]), to_seq(v[3], 3)]
    attn = deal(head_out)
    mid_vectors = jnp.stack([bo_full, gain_one, shift_one, bback_full, gain_two, shift_two, gain_two, gain_two])
    result, hidden_low, act_low, pre_grad, ffn_grad, branch_grad, sum_one_grad, *douts, short_sums = middle(
        place, attn, mine, grad_output[0], late, mid_vectors, bin_full[None]
    )
    activations = result.reshape(1, row_count, width)
    douts = deal(douts)
    devices = seqs * fsdps
    device = own * fsdps + rank
    fine = width // devices
    deep = act_low.shape[1] // devices
    kept_place = jnp.where((order == 1) | (order == 2), jnp.where(parity == 1, 3 - order, order), order)
    if direct:
        relative = jnp.arange(32, dtype=jnp.int32) ^ device
        bit = lambda n: (relative >> n) & 1
        flip = (bit(0) ^ parity) == 1
        one, two = jnp.where(flip, bit(4), bit(3)), jnp.where(flip, bit(3), bit(4))
        me, masks = device[None], place[3:5]
        in_table = jnp.concatenate([me, one * 8 + two * 4 + bit(1) * 2 + bit(2), masks]).astype(jnp.int32)
        back_table = jnp.concatenate([me, bit(1) * 8 + one * 4 + two * 2 + bit(2), masks]).astype(jnp.int32)
        kept, sent = in_blocks(in_table, hidden_low, pre_grad, attn, branch_grad, short_sums)
        ins = [kept, to_core(sent)]
        kept, sent = back_blocks(back_table, act_low, ffn_grad)
        backs = [kept, to_core(sent)]
        back_out, in_out = merge(backs, ins, 8)
        douts, back_out, in_out = lax.optimization_barrier((douts, back_out, in_out))
        backs.append(to_near(back_out))
        ins.append(to_first(in_out))
    else:
        scatter = lambda v: lax.psum_scatter(v, ("seq", "fsdp"), scatter_dimension=0, tiled=True)
        w_back_grad = scatter(contract_rows(act_low, ffn_grad))
        w_in_grad = scatter(contract_rows(hidden_low, pre_grad))
        spun = contract_rows(jnp.concatenate(attn, axis=1), branch_grad).reshape(seqs, local_cols, width)
        w_out_grad = scatter(jnp.take(spun, kept_place, axis=0).reshape(width, width))

    tkeep, tsend, rel, sums = attend_back(
        place, douts, big, small, ox, qx, pq, kx, vxt, key_pos, wrel_rows, sine, cosine, turned_types, head
    )
    if direct:
        bundle = qkv_blocks(fsdps, pieces, tkeep, tsend, rel, sums)
    else:
        grad = contract_rows(pieces[0], tkeep[:row_count]) + contract_rows(pieces[2], tkeep[row_count:])
        grad = grad + contract_rows(pieces[1], tsend[:row_count]) + contract_rows(pieces[3], tsend[row_count:])
        grad = jnp.swapaxes(grad.reshape(seqs, fsdps, fine, 640), 0, 1).reshape(fsdps, local_rows, 640)
        tall = rel.reshape(fsdps, local_rows, 256)
        bundle = jnp.concatenate([grad[..., :512], grad[..., 512:] + tall[..., :128], tall[..., 128:]], axis=2)
        notes = jnp.concatenate([sums[0], sums[1], sums[2], jnp.zeros((8, 384), F32)], axis=1)
        bundle = jnp.concatenate([bundle, jnp.broadcast_to(notes[None], (fsdps,) + notes.shape)], axis=1).astype(BF)
    total = lax.psum_scatter(bundle, "fsdp", scatter_dimension=0, tiled=True)[0].astype(F32)
    dx_send = contract_cols(tsend, w_qkv).astype(BF)
    if direct:
        dx_send, backs, ins, bundle = lax.optimization_barrier((dx_send, backs, ins, bundle))
        back_out, in_out = merge(backs, ins, 4)
        backs.append(to_first(back_out))
        ins.append(to_second(in_out))
    dx_first = to_first(dx_send)
    dx_keep = contract_cols(tkeep, w_qkv)
    if direct:
        dx_first, backs, ins = lax.optimization_barrier((dx_first, backs, ins))
    dx_out = (dx_keep[row_count:] + dx_first[row_count:].astype(F32)).astype(BF)
    dx_second = to_second(dx_out)
    if direct:
        back_out, in_out = merge(backs, ins, 2)
        backs.append(to_second(back_out))
        ins.append(to_near(in_out))
        dx_second, backs, ins = lax.optimization_barrier((dx_second, backs, ins))
    input_rows = sum_one_grad + dx_keep[:row_count] + dx_first[:row_count].astype(F32) + dx_second.astype(F32)
    input_rows = input_rows.astype(BF).reshape(fsdps, sliver_rows, width)
    returned = lax.all_to_all(input_rows, "fsdp", split_axis=0, concat_axis=0, tiled=True)
    input_grad = reload(owners, returned, False)
    if direct:
        far_out, total = lax.optimization_barrier((merge(backs, ins, 1, False)[0], total))
        far = to_far(far_out)
        cut = kept.shape[1]
    if not direct:
        short_sums = lax.psum(short_sums, ("seq", "fsdp"))
        short_grads = lax.dynamic_slice(short_sums, (0, device * fine), (8, fine))
        in_bias_grad = lax.dynamic_slice(short_sums, (8 + device * deep // width, device * deep % width), (1, deep))[0]
    own_qkv = total[:local_rows].astype(BF).reshape(seqs, fine, width)
    block_for = lambda mask: lax.dynamic_index_in_dim(own_qkv, own ^ mask, 0, keepdims=True)
    swapped = jnp.concatenate(deal([block_for(m) for m in (0, place[3], place[4], 3)]), axis=0)
    swapped = jnp.take(swapped, kept_place, axis=0).astype(F32)
    both = swapped[:, :, : 2 * local_cols].reshape(seqs, fine, local_heads, 2, DH)
    both = jnp.transpose(both, (3, 1, 0, 2, 4)).reshape(2, fine, width)
    w_value_grad = jnp.transpose(swapped[:, :, 2 * local_cols : 3 * local_cols], (1, 0, 2)).reshape(fine, width)
    if direct:
        _, _, far, _ = lax.optimization_barrier((both, w_value_grad, far, input_grad))
        w_back_grad = add_parts(backs + [far[:, :cut]], 0, 1)[0]
        in_total = add_parts(ins + [far[:, cut:]], 0, 1)[0]
        w_in_grad = jnp.concatenate([in_total[c * 24 : (c + 1) * 24] for c in range(4)], axis=1)
        w_out_grad = in_total[96:120]
        short_grads, in_bias_grad = in_total[120:128, :fine], in_total[126, :deep]
    rel_total = total[:local_rows, 3 * local_cols :].reshape(local_rows, local_heads, DH)
    notes = total[local_rows:, :384].reshape(8, 3, 128)
    eighth = DH // fsdps
    mine_sums = lax.dynamic_slice(notes, (0, 0, rank * eighth), (8, 3, eighth))
    value_bias_grad = lax.dynamic_slice(notes[5, :, :DH].reshape(-1), (rank * fine,), (fine,))
    return (
        activations,
        input_grad,
        both[0],
        both[1],
        w_value_grad,
        value_bias_grad,
        w_out_grad,
        short_grads[4],
        short_grads[0],
        short_grads[1],
        w_in_grad,
        in_bias_grad,
        w_back_grad,
        short_grads[5],
        short_grads[2],
        short_grads[3],
        rel_total,
        mine_sums[0],
        mine_sums[1],
        mine_sums[2],
        mine_sums[3:5],
    )


def solution(mesh):
    placed = (
        P(None, ("seq", "fsdp"), None),
        P("fsdp", None),
        P("fsdp", None),
        P("fsdp", None),
        P("fsdp"),
        P("fsdp", None),
        P("fsdp"),
        P("fsdp"),
        P("fsdp"),
        P("fsdp", None),
        P("fsdp"),
        P("fsdp", None),
        P("fsdp"),
        P("fsdp"),
        P("fsdp"),
        P("fsdp", "seq", None),
        P("seq", "fsdp"),
        P("seq", "fsdp"),
        P("seq", "fsdp"),
        P(None, "seq", "fsdp"),
        P(),
        P(),
        P(),
        P("fsdp", "seq", None),
    )
    return jax.shard_map(
        shards,
        mesh=mesh,
        in_specs=placed,
        out_specs=(
            P("fsdp", "seq", None),
            P(None, ("seq", "fsdp"), None),
            P(("seq", "fsdp"), None),
            P(("seq", "fsdp"), None),
            P(("seq", "fsdp"), None),
            P(("seq", "fsdp")),
            P(("seq", "fsdp"), None),
            P(("seq", "fsdp")),
            P(("seq", "fsdp")),
            P(("seq", "fsdp")),
            P(("seq", "fsdp"), None),
            P(("seq", "fsdp")),
            P(("seq", "fsdp"), None),
            P(("seq", "fsdp")),
            P(("seq", "fsdp")),
            P(("seq", "fsdp")),
            P("fsdp", "seq", None),
            P("seq", "fsdp"),
            P("seq", "fsdp"),
            P("seq", "fsdp"),
            P(None, "seq", "fsdp"),
        ),
        check_vma=False,
    )
```

```python
import functools

import jax
import jax.numpy as jnp
from jax import lax
from jax.experimental import pallas as pl
from jax.experimental.pallas import tpu as pltpu
from jax.sharding import PartitionSpec as P

DH = 64
LONGEST = 1024
QB = 256
BLOCKED = -1e30
BF = jnp.bfloat16
F32 = jnp.float32
VM = pl.BlockSpec(memory_space=pltpu.VMEM)
SM = pl.BlockSpec(memory_space=pltpu.SMEM)
MIB = 1024 * 1024


def lanes_of(rows, width=128):
    return lax.broadcasted_iota(jnp.int32, (rows, width), 1)


def split3(value):
    high = value.astype(BF).astype(F32)
    rest = value - high
    middle = rest.astype(BF).astype(F32)
    return high, middle, rest - middle


def masks_of(place):
    return 0, place[3], place[4], 3


def pick(lane, first, columns, base):
    for number, column in enumerate(columns):
        base = jnp.where(lane == first + number, column, base)
    return base


def project_body(place, x0, x1, x2, x3, w_ref, head_ref, tcol_ref, qx_ref, pq_ref, kx_ref, kxt_ref, vx_ref, vxt_ref, rolled):
    own, start, near = place[0], place[1], place[2]
    scale = DH ** -0.5
    rows = qx_ref.shape[1]
    part = x0.shape[0]
    for mask, piece in zip(masks_of(place), (x0, x1, x2, x3)):
        y = jnp.dot(piece[...], w_ref[...], preferred_element_type=F32)
        base = pl.multiple_of((own ^ mask) * part, 8)
        for c in range(5):
            column = y[:, c * 128 : (c + 1) * 128]
            rolled[c, pl.ds(base, part), :] = column
            rolled[c, pl.ds(pl.multiple_of(base + rows, 8), part), :] = column

    def block(r, carry):
        row = pl.multiple_of(r * QB, QB)
        lane = lanes_of(QB)
        kind = tcol_ref[pl.ds(row, QB), :]
        index = row + lax.broadcasted_iota(jnp.int32, (QB, 1), 0)
        small = index >= LONGEST
        first = jnp.where(small & (index < LONGEST + near), 1.0, 0.0)
        second = jnp.where(small & (index >= LONGEST + near), 1.0, 0.0)
        one = jnp.where(kind == 1, 1.0, 0.0)
        zero = 1.0 - one
        for h in range(3):
            both = rolled[h, pl.ds(start + row, QB), :].astype(BF).astype(F32)
            if h < 2:
                v = rolled[3, pl.ds(start + row, QB), :]
                v = v if h == 0 else pltpu.roll(v, 64, 1)
            else:
                v = rolled[4, pl.ds(start + row, QB), :]
            head = head_ref[h]
            content = (both + head[0:1]) * scale
            position = ((both + head[1:2]) * scale).astype(BF)
            typed = (both + head[2:3]) * scale
            differ = jnp.sum(typed * head[3:4], axis=1, keepdims=True)
            same = jnp.sum(typed * head[4:5], axis=1, keepdims=True)
            for_zero = jnp.where(kind == 1, differ, same)
            for_one = jnp.where(kind == 1, same, differ)
            columns = [*split3(for_zero), *split3(for_one), second * BLOCKED, first * BLOCKED]
            qx = pick(lane, 64, columns, jnp.where(lane < 64, content, 0.0)).astype(BF)
            qx_ref[h, pl.ds(row, QB), :] = qx
            raw = pltpu.roll(both, 64, 1)
            pq_ref[h, pl.ds(row, QB), :] = jnp.where(lane < 64, position.astype(F32), raw).astype(BF)
            kx = pick(lane, 64, [zero, zero, zero, one, one, one, first, second], jnp.where(lane < 64, raw, 0.0))
            kx_ref[h, pl.ds(row, QB), :] = kx.astype(BF)
            kxt_ref[h, :, pl.ds(row, QB)] = jnp.transpose(kx, (1, 0)).astype(BF)
            vx = jnp.where(lane < 64, v + head[5:6], jnp.where(lane < 67, 1.0, 0.0)).astype(BF)
            vx_ref[h, pl.ds(row, QB), :] = vx
            vxt_ref[h, :, pl.ds(row, QB)] = jnp.transpose(vx.astype(F32), (1, 0)).astype(BF)
        return carry

    lax.fori_loop(0, rows // QB, block, 0)


def project(place, pieces, w_qkv, head, tcol):
    rows = 4 * pieces[0].shape[0]
    tall = jax.ShapeDtypeStruct((3, rows, 128), BF)
    wide = jax.ShapeDtypeStruct((3, 128, rows), BF)
    return pl.pallas_call(
        project_body,
        in_specs=[SM] + [VM] * 7,
        out_specs=[VM] * 6,
        out_shape=[tall, tall, tall, wide, tall, wide],
        scratch_shapes=[pltpu.VMEM((5, 2 * rows, 128), F32)],
        compiler_params=pltpu.CompilerParams(vmem_limit_bytes=32 * MIB),
        cost_estimate=pl.CostEstimate(flops=2 * rows * 768 * 640, bytes_accessed=10_000_000, transcendentals=0),
        name="project",
    )(place, *pieces, w_qkv, head, tcol)


def attend_body(place, qx_ref, pq_ref, kxt_ref, vx_ref, kpt_ref, wrt_ref, sn_ref, cs_ref, big_ref, small_ref, ox_ref, o0, o1, o2, o3, keys, left, outs):
    h, i = pl.program_id(0), pl.program_id(1)
    own, start = place[0], place[1]
    width = kpt_ref.shape[0]
    half = width // 2
    rows = kpt_ref.shape[1]

    @pl.when((h == 0) & (i == 0))
    def _():
        keys[0:width, :] = kpt_ref[...]

    @pl.when(i == 0)
    def _():
        keys[width:, :] = kxt_ref[0]

    rel = jnp.dot(pq_ref[0], wrt_ref[0], preferred_element_type=F32)
    r1, r2 = rel[:, :half], rel[:, half:]
    sn, cs = sn_ref[...], cs_ref[...]
    left[:, 0:half] = (r1 * sn + r2 * cs).astype(BF)
    left[:, half:width] = (r2 * sn - r1 * cs).astype(BF)
    left[:, width:] = qx_ref[0]

    def attend(low, high, store):
        score = jnp.dot(left[...], keys[:, low:high], preferred_element_type=F32)
        top = jnp.max(score, axis=1, keepdims=True)
        raised = jnp.exp(score - top).astype(BF)
        store[0] = raised
        mixed = jnp.dot(raised, vx_ref[0, low:high, :], preferred_element_type=F32)
        inverse = 1.0 / mixed[:, 64:65]
        lane = lanes_of(QB)
        ox = jnp.where(lane < 64, mixed * inverse, jnp.where(lane == 64, inverse, 0.0))
        ox_ref[0] = ox
        row = pl.multiple_of(i * QB, QB)
        outs[h, pl.ds(row, QB), :] = ox
        outs[h, pl.ds(pl.multiple_of(row + rows, QB), QB), :] = ox

    @pl.when(i < LONGEST // QB)
    def _():
        attend(0, LONGEST, big_ref)

    @pl.when(i >= LONGEST // QB)
    def _():
        attend(LONGEST, rows, small_ref)

    @pl.when((h == 2) & (i == pl.num_programs(1) - 1))
    def _():
        part = o0.shape[0]
        for mask, out in zip(masks_of(place), (o0, o1, o2, o3)):
            at = lax.rem((own ^ mask) * part + rows - start, rows)
            out[...] = jnp.concatenate([outs[g, pl.ds(at, part), :][:, 0:64] for g in range(3)], axis=1).astype(BF)


def attend(place, qx, pq, kxt, vx, kpt, wrt, sn, cs):
    rows = qx.shape[1]
    width = kpt.shape[0]
    blocks = rows // QB
    bigs = LONGEST // QB
    rest = rows - LONGEST
    per_block = lambda h, i: (h, i, 0)
    per_head = lambda h, i: (h, 0, 0)
    whole2 = lambda h, i: (0, 0)
    part = rows // 4
    out_piece = jax.ShapeDtypeStruct((part, 192), BF)
    return pl.pallas_call(
        attend_body,
        grid=(3, blocks),
        in_specs=[
            SM,
            pl.BlockSpec((1, QB, 128), per_block),
            pl.BlockSpec((1, QB, 128), per_block),
            pl.BlockSpec((1, 128, rows), per_head),
            pl.BlockSpec((1, rows, 128), per_head),
            pl.BlockSpec((width, rows), whole2, pipeline_mode=pl.Buffered(1)),
            pl.BlockSpec((1, 128, width), per_head),
            pl.BlockSpec((QB, width // 2), lambda h, i: (i, 0)),
            pl.BlockSpec((QB, width // 2), lambda h, i: (i, 0)),
        ],
        out_specs=[
            pl.BlockSpec((1, QB, LONGEST), lambda h, i: (h, jnp.minimum(i, bigs - 1), 0)),
            pl.BlockSpec((1, QB, rest), lambda h, i: (h, jnp.maximum(i - bigs, 0), 0)),
            pl.BlockSpec((1, QB, 128), per_block),
        ]
        + [pl.BlockSpec((part, 192), whole2)] * 4,
        out_shape=[
            jax.ShapeDtypeStruct((3, LONGEST, LONGEST), BF),
            jax.ShapeDtypeStruct((3, rest, rest), BF),
            jax.ShapeDtypeStruct((3, rows, 128), F32),
        ]
        + [out_piece] * 4,
        scratch_shapes=[
            pltpu.VMEM((width + 128, rows), BF),
            pltpu.VMEM((QB, width + 128), BF),
            pltpu.VMEM((3, 2 * rows, 128), F32),
        ],
        compiler_params=pltpu.CompilerParams(vmem_limit_bytes=32 * MIB, dimension_semantics=("arbitrary", "arbitrary")),
        cost_estimate=pl.CostEstimate(flops=12_000_000_000, bytes_accessed=20_000_000, transcendentals=4_000_000),
        name="attend",
    )(place, qx, pq, kxt, vx, kpt, wrt, sn, cs)


def back_body(place, d0, d1, d2, d3, big_ref, small_ref, ox_ref, qx_ref, pq_ref, kx_ref, vxt_ref, kp_ref, wr_ref, sn_ref, cs_ref, tcol_ref, head_ref, gkeep_ref, gsend_ref, rel_ref, sum_ref, douts, dkt, dvt, gwt, grads):
    h, i = pl.program_id(0), pl.program_id(1)
    own, start = place[0], place[1]
    rows, width = kp_ref.shape
    half = width // 2
    scale = DH ** -0.5
    part = d0.shape[0]
    last = pl.num_programs(1) - 1
    row = pl.multiple_of(i * QB, QB)
    again = pl.multiple_of(row + rows, QB)

    @pl.when((h == 0) & (i == 0))
    def _():
        blank = jnp.zeros((part, 64), F32)
        for mask, piece in zip(masks_of(place), (d0, d1, d2, d3)):
            values = piece[...].astype(F32)
            base = pl.multiple_of((own ^ mask) * part, 8)
            for g in range(3):
                padded = jnp.concatenate([values[:, g * 64 : (g + 1) * 64], blank], axis=1)
                douts[g, pl.ds(base, part), :] = padded
                douts[g, pl.ds(pl.multiple_of(base + rows, 8), part), :] = padded

    @pl.when(i == 0)
    def _():
        dkt[...] = jnp.zeros_like(dkt)
        dvt[...] = jnp.zeros_like(dvt)
        gwt[...] = jnp.zeros_like(gwt)
        sum_ref[...] = jnp.zeros_like(sum_ref)

    lane = lanes_of(QB)
    dout = douts[h, pl.ds(start + row, QB), :]
    ox = ox_ref[0]
    inverse = ox[:, 64:65]
    dot_row = jnp.sum(dout * ox, axis=1, keepdims=True)
    dox = pick(lane, 64, [-x for x in split3(dot_row)], dout).astype(BF)
    dout_t = jnp.transpose(dout * inverse, (1, 0))[0:64].astype(BF)
    qx = qx_ref[0]
    qc_t = jnp.transpose(qx.astype(F32), (1, 0))[0:64].astype(BF)
    pq = pq_ref[0].astype(F32)
    qp_t = jnp.transpose(pq, (1, 0))[0:64].astype(BF)
    sn, cs = sn_ref[...], cs_ref[...]

    def back(low, high, saved):
        raised = saved[0]
        dprob = jnp.dot(dox, vxt_ref[0, :, low:high], preferred_element_type=F32)
        dscore = (raised.astype(F32) * (dprob * inverse)).astype(BF)
        dvt[:, low:high] += jnp.dot(dout_t, raised, preferred_element_type=F32)
        dkt[:, low:high] += jnp.dot(qc_t, dscore, preferred_element_type=F32)
        da = jnp.dot(dscore, kp_ref[low:high, :], preferred_element_type=F32)
        dqx = jnp.dot(dscore, kx_ref[0, low:high, :], preferred_element_type=F32)
        da1, da2 = da[:, 0:half], da[:, half:width]
        drel = jnp.concatenate([(da1 * sn - da2 * cs).astype(BF), (da1 * cs + da2 * sn).astype(BF)], axis=1)
        dqp = jnp.dot(drel, wr_ref[0], preferred_element_type=F32)
        gwt[...] += jnp.dot(qp_t, drel, preferred_element_type=F32)
        kind = tcol_ref[...]
        over_zero, over_one = dqx[:, 64:65], dqx[:, 67:68]
        same = jnp.where(kind == 1, over_one, over_zero)
        differ = jnp.where(kind == 1, over_zero, over_one)
        head = head_ref[0]
        dqt = differ * head[3:4] + same * head[4:5]
        dqc = jnp.where(lane < 64, dqx, 0.0)
        dq = (dqc + dqp + dqt) * scale
        grads[h, pl.ds(row, QB), :] = dq
        typed = (pltpu.roll(pq, 64, 1) + head[2:3]) * scale
        sums = [dqc * scale, dqp * scale, dqt * scale, differ * typed, same * typed]
        for number, values in enumerate(sums):
            sum_ref[0, number : number + 1, :] += jnp.sum(values, axis=0, keepdims=True)

    @pl.when(i < LONGEST // QB)
    def _():
        back(0, LONGEST, big_ref)

    @pl.when(i >= LONGEST // QB)
    def _():
        back(LONGEST, rows, small_ref)

    @pl.when(i == last)
    def _():
        dk = jnp.transpose(dkt[...], (1, 0))
        dq = grads[h, 0:rows, :]
        pair = jnp.concatenate([dq[:, 0:64], dk], axis=1)
        grads[h, 0:rows, :] = pair
        grads[h, rows : 2 * rows, :] = pair
        dv = jnp.transpose(dvt[...], (1, 0)).astype(BF).astype(F32)
        sum_ref[0, 5:6, 0:64] = jnp.sum(dv, axis=0, keepdims=True)
        blank = jnp.zeros_like(dv)
        rel = jnp.transpose(gwt[...], (1, 0))
        empty = jnp.zeros_like(rel)

        @pl.when(h == 0)
        def _():
            padded = jnp.concatenate([dv, blank], axis=1)
            grads[3, 0:rows, :] = padded
            grads[3, rows : 2 * rows, :] = padded
            rel_ref[:, 0:128] = jnp.concatenate([empty, rel], axis=1)

        @pl.when(h == 1)
        def _():
            rel_ref[:, 128:256] = jnp.concatenate([rel, empty], axis=1)
            padded = grads[3, 0:rows, :] + jnp.concatenate([blank, dv], axis=1)
            grads[3, 0:rows, :] = padded
            grads[3, rows : 2 * rows, :] = padded

        @pl.when(h == 2)
        def _():
            padded = jnp.concatenate([dv, blank], axis=1)
            grads[4, 0:rows, :] = padded
            grads[4, rows : 2 * rows, :] = padded
            rel_ref[:, 128:256] += jnp.concatenate([empty, rel], axis=1)
            spots = ((gkeep_ref, 0), (gsend_ref, 0), (gkeep_ref, part), (gsend_ref, part))
            for mask, (out, low) in zip(masks_of(place), spots):
                at = lax.rem((own ^ mask) * part + rows - start, rows)
                for c in range(5):
                    out[low : low + part, c * 128 : (c + 1) * 128] = grads[c, pl.ds(at, part), :].astype(BF)


def attend_back(place, douts, big, small, ox, qx, pq, kx, vxt, kp, wr, sn, cs, tcol, head):
    rows, width = kp.shape
    blocks = rows // QB
    bigs = LONGEST // QB
    rest = rows - LONGEST
    part = rows // 4
    per_block = lambda h, i: (h, i, 0)
    per_head = lambda h, i: (h, 0, 0)
    whole2 = lambda h, i: (0, 0)
    return pl.pallas_call(
        back_body,
        grid=(3, blocks),
        in_specs=[SM]
        + [pl.BlockSpec((part, 192), whole2)] * 4
        + [
            pl.BlockSpec((1, QB, LONGEST), lambda h, i: (h, jnp.minimum(i, bigs - 1), 0)),
            pl.BlockSpec((1, QB, rest), lambda h, i: (h, jnp.maximum(i - bigs, 0), 0)),
            pl.BlockSpec((1, QB, 128), per_block),
            pl.BlockSpec((1, QB, 128), per_block),
            pl.BlockSpec((1, QB, 128), per_block),
            pl.BlockSpec((1, rows, 128), per_head),
            pl.BlockSpec((1, 128, rows), per_head),
            pl.BlockSpec((rows, width), whole2, pipeline_mode=pl.Buffered(1)),
            pl.BlockSpec((1, width, 128), per_head),
            pl.BlockSpec((QB, width // 2), lambda h, i: (i, 0)),
            pl.BlockSpec((QB, width // 2), lambda h, i: (i, 0)),
            pl.BlockSpec((QB, 1), lambda h, i: (i, 0)),
            pl.BlockSpec((1, 8, 128), per_head),
        ],
        out_specs=[pl.BlockSpec((2 * part, 640), whole2)] * 2
        + [pl.BlockSpec((width, 256), whole2), pl.BlockSpec((1, 8, 128), per_head)],
        out_shape=[jax.ShapeDtypeStruct((2 * part, 640), BF)] * 2
        + [jax.ShapeDtypeStruct((width, 256), F32), jax.ShapeDtypeStruct((3, 8, 128), F32)],
        scratch_shapes=[
            pltpu.VMEM((3, 2 * rows, 128), F32),
            pltpu.VMEM((64, rows), F32),
            pltpu.VMEM((64, rows), F32),
            pltpu.VMEM((64, width), F32),
            pltpu.VMEM((5, 2 * rows, 128), F32),
        ],
        compiler_params=pltpu.CompilerParams(vmem_limit_bytes=44 * MIB, dimension_semantics=("arbitrary", "arbitrary")),
        cost_estimate=pl.CostEstimate(flops=20_000_000_000, bytes_accessed=25_000_000, transcendentals=0),
        name="attend_back",
    )(place, *douts, big, small, ox, qx, pq, kx, vxt, kp, wr, sn, cs, tcol, head)


def reload_body(outward, owners, in_ref, out_ref):
    def move(j, carry):
        if outward:
            out_ref[owners[j]] = in_ref[j]
        else:
            out_ref[j] = in_ref[owners[j]]
        return carry

    lax.fori_loop(0, out_ref.shape[0], move, 0)


def reload(owners, rows, outward):
    return pl.pallas_call(
        functools.partial(reload_body, outward),
        in_specs=[SM, VM],
        out_specs=VM,
        out_shape=jax.ShapeDtypeStruct(rows.shape, rows.dtype),
        compiler_params=pltpu.CompilerParams(vmem_limit_bytes=6 * MIB),
        name="deal" if outward else "reload",
    )(owners, rows)


def qkv_blocks_body(x0, x1, x2, x3, tkeep_ref, tsend_ref, rel_ref, sums_ref, out_ref, acc):
    part = x0.shape[0]
    count, high, _ = out_ref.shape
    rows = high - 8
    fine = rows // 4
    parts = ((x0, tkeep_ref, 0), (x2, tkeep_ref, part), (x1, tsend_ref, 0), (x3, tsend_ref, part))
    for number, (x, t, low) in enumerate(parts):
        value = lax.dot_general(x[...], t[low : low + part, :], (((0,), (0,)), ((), ())), preferred_element_type=F32)
        acc[...] = value if number == 0 else acc[...] + value
    notes = jnp.concatenate([sums_ref[0], sums_ref[1], sums_ref[2], jnp.zeros((8, 384), F32)], axis=1).astype(BF)
    for f in range(count):
        for s in range(4):
            value = acc[(count * s + f) * fine : (count * s + f + 1) * fine, :]
            rel = rel_ref[rows * f + fine * s : rows * f + fine * (s + 1), :]
            low, high = fine * s, fine * (s + 1)
            out_ref[f, low:high, 0:512] = value[:, 0:512].astype(BF)
            out_ref[f, low:high, 512:640] = (value[:, 512:640] + rel[:, 0:128]).astype(BF)
            out_ref[f, low:high, 640:768] = rel[:, 128:256].astype(BF)
        out_ref[f, rows : rows + 8, :] = notes


def qkv_blocks(count, pieces, tkeep, tsend, rel, sums):
    width = pieces[0].shape[1]
    return pl.pallas_call(
        qkv_blocks_body,
        in_specs=[VM] * 8,
        out_specs=VM,
        out_shape=jax.ShapeDtypeStruct((count, width // count + 8, width), BF),
        scratch_shapes=[pltpu.VMEM((width, 640), F32)],
        compiler_params=pltpu.CompilerParams(vmem_limit_bytes=24 * MIB),
        cost_estimate=pl.CostEstimate(flops=2_000_000_000, bytes_accessed=8_000_000, transcendentals=0),
        name="qkv_blocks",
    )(*pieces, tkeep, tsend, rel, sums)


def merge_body(split, *refs):
    count = len(refs) - (2 if split else 1)
    sums = []
    for group in (refs[: count // 2], refs[count // 2 : count]):
        total = group[0][...].astype(F32)
        for ref in group[1:]:
            total = total + ref[...].astype(F32)
        sums.append(total.astype(BF))
    if split:
        refs[count][...], refs[count + 1][...] = sums
    else:
        cut = sums[0].shape[1]
        refs[count][:, :cut, :] = sums[0]
        refs[count][:, cut:, :] = sums[1]


def merge(backs, ins, half, split=True):
    step = min(half, 2)
    first = half // step
    width = backs[0].shape[2]
    heights = [backs[0].shape[1], ins[0].shape[1]]
    heights = heights if split else [sum(heights)]
    block = lambda p: pl.BlockSpec((step,) + p.shape[1:], lambda g: (first + g, 0, 0))
    parts = backs + ins
    return pl.pallas_call(
        functools.partial(merge_body, split),
        grid=(first,),
        in_specs=[block(p) for p in parts],
        out_specs=[pl.BlockSpec((step, h, width), lambda g: (g, 0, 0)) for h in heights],
        out_shape=[jax.ShapeDtypeStruct((half, h, width), BF) for h in heights],
        compiler_params=pltpu.CompilerParams(vmem_limit_bytes=(14 if half == 8 else 60) * MIB, dimension_semantics=("arbitrary",)),
        cost_estimate=pl.CostEstimate(flops=half * 224 * width * 6, bytes_accessed=half * 224 * width * 8, transcendentals=0),
        name="merge",
    )(*parts)


EPS = 1e-09
GELU_A = (2.0 / 3.141592653589793) ** 0.5
GELU_B = 0.044715

def spread_norm(values):
    center = values - jnp.mean(values, axis=1, keepdims=True)
    inverse = lax.rsqrt(jnp.mean(center * center, axis=1, keepdims=True) + EPS)
    return center * inverse, inverse


def middle_body(
    place, a0, a1, a2, a3, x_ref, go_ref, w_ref, vec_ref, bin_ref,
    act_ref, h_ref, u_ref, dz_ref, df_ref, dbr_ref, dr_ref, d0, d1, d2, d3, sum_ref,
    wout, slope, high, normed, acc,
):
    own = place[0]
    width = x_ref.shape[1]
    cols = a0.shape[1]
    vector = lambda n: vec_ref[n : n + 1, :]
    for s in range(4):
        piece = w_ref[:, s, :, 2 * width : 2 * width + cols]
        wout[:, s * cols : (s + 1) * cols] = piece.reshape(width, cols)
    part = lambda mask: wout[pl.ds(pl.multiple_of((own ^ mask) * cols, 64), cols), :]
    masks = masks_of(place)
    total = x_ref[...].astype(F32) + vector(0)
    for mask, piece in zip(masks, (a0, a1, a2, a3)):
        total = total + jnp.dot(piece[...], part(mask), preferred_element_type=F32)
    unit, inverse_one = spread_norm(total)
    normed[...] = unit
    first = unit * vector(1) + vector(2)
    high[...] = first
    h_ref[...] = first.astype(BF)
    acc[...] = first + vector(3)

    def w_in_at(w):
        return w_ref[:, w, :, 0:width].reshape(width, width)

    def w_back_at(w):
        return w_ref[pl.ds(2 * w, 2), :, :, width : 2 * width].reshape(width, width)

    def forward(w, carry):
        at = pl.multiple_of(w * width, 128)
        z = jnp.dot(h_ref[...], w_in_at(w), preferred_element_type=F32) + bin_ref[:, pl.ds(at, width)]
        square = z * z
        bend = jnp.tanh(GELU_A * z * (1.0 + GELU_B * square))
        half = 0.5 + 0.5 * bend
        u = (z * half).astype(BF)
        u_ref[:, pl.ds(at, width)] = u
        slope[:, pl.ds(at, width)] = half + 0.5 * z * (1.0 - bend * bend) * (GELU_A * (1.0 + 3.0 * GELU_B * square))
        acc[...] += jnp.dot(u, w_back_at(w), preferred_element_type=F32)
        return carry

    lax.fori_loop(0, 4, forward, 0)
    unit, inverse_two = spread_norm(acc[...])
    act_ref[...] = (unit * vector(4) + vector(5)).astype(BF)

    def back(gradient, unit, inverse, gain):
        scaled = gradient * gain
        inner = scaled - jnp.mean(scaled, axis=1, keepdims=True)
        return (inner - unit * jnp.mean(scaled * unit, axis=1, keepdims=True)) * inverse

    def note(row, values):
        sum_ref[row : row + 1, :] = jnp.sum(values, axis=0, keepdims=True)

    gradient = go_ref[...].astype(F32)
    note(2, gradient * unit)
    note(3, gradient)
    second = back(gradient, unit, inverse_two, vector(4))
    df = second.astype(BF)
    df_ref[...] = df
    note(5, df.astype(F32))
    acc[...] = second

    def backward(w, carry):
        at = pl.multiple_of(w * width, 128)
        du = lax.dot_general(df_ref[...], w_back_at(w), (((1,), (1,)), ((), ())), preferred_element_type=F32)
        dz = (slope[:, pl.ds(at, width)] * du).astype(BF)
        dz_ref[:, pl.ds(at, width)] = dz
        sum_ref[pl.ds(8 + w, 1), :] = jnp.sum(dz.astype(F32), axis=0, keepdims=True)
        acc[...] += lax.dot_general(dz, w_in_at(w), (((1,), (1,)), ((), ())), preferred_element_type=F32)
        return carry

    lax.fori_loop(0, 4, backward, 0)
    gradient = acc[...]
    unit = normed[...]
    note(0, gradient * unit)
    note(1, gradient)
    dr = back(gradient, unit, inverse_one, vector(1))
    dr_ref[...] = dr
    dbr = dr.astype(BF)
    dbr_ref[...] = dbr
    note(4, dbr.astype(F32))
    sum_ref[6:8, :] = jnp.zeros((2, width), F32)
    sum_ref[12:16, :] = jnp.zeros((4, width), F32)
    for mask, out in zip(masks, (d0, d1, d2, d3)):
        value = lax.dot_general(dbr, part(mask), (((1,), (1,)), ((), ())), preferred_element_type=F32)
        out[...] = value.astype(BF)


def middle(place, pieces, x, out_grad, weights, vectors, bin_full):
    rows, width = x.shape
    cols = pieces[0].shape[1]
    hidden = bin_full.shape[1]
    low = lambda n: jax.ShapeDtypeStruct((rows, n), BF)
    full = lambda r, n: jax.ShapeDtypeStruct((r, n), F32)
    return pl.pallas_call(
        middle_body,
        in_specs=[SM] + [VM] * 9,
        out_specs=[VM] * 12,
        out_shape=[low(width), low(width), low(hidden), low(hidden), low(width), low(width), full(rows, width)]
        + [low(cols)] * 4
        + [full(16, width)],
        scratch_shapes=[
            pltpu.VMEM((width, width), BF),
            pltpu.VMEM((rows, hidden), F32),
            pltpu.VMEM((rows, width), F32),
            pltpu.VMEM((rows, width), F32),
            pltpu.VMEM((rows, width), F32),
        ],
        compiler_params=pltpu.CompilerParams(vmem_limit_bytes=44 * MIB),
        cost_estimate=pl.CostEstimate(flops=8_000_000_000, bytes_accessed=20_000_000, transcendentals=1_000_000),
        name="middle",
    )(place, *pieces, x, out_grad, weights, vectors, bin_full)


def angles_of(position, width):
    half_width = width // 2
    rate_table = 10000.0 ** (-(jnp.arange(half_width, dtype=jnp.float32) / half_width))
    turned = position.astype(jnp.float32)[:, None] * rate_table[None, :]
    return (jnp.sin(turned), jnp.cos(turned))


def contract_rows(left, right):
    return lax.dot_general(
        left, right, (((0,), (0,)), ((), ())), preferred_element_type=jnp.float32
    )


def contract_cols(left, right):
    return lax.dot_general(
        left, right, (((1,), (1,)), ((), ())), preferred_element_type=jnp.float32
    )


def across(values, other):
    seqs, fsdps = lax.axis_size("seq"), lax.axis_size("fsdp")
    pairs = []
    for s in range(seqs):
        for f in range(fsdps):
            to_s, to_f = other(s, f)
            pairs.append((s * fsdps + f, to_s * fsdps + to_f))
    return lax.ppermute(values, ("seq", "fsdp"), pairs)


def to_core(values):
    return across(values, lambda s, f: (s, f ^ 1))


def to_first(values):
    return across(values, lambda s, f: (s ^ (2 if f & 1 else 1), f))


def to_second(values):
    return across(values, lambda s, f: (s ^ (1 if f & 1 else 2), f))


def to_near(values):
    return across(values, lambda s, f: (s, f ^ 2))


def to_far(values):
    return across(values, lambda s, f: (s, f ^ 4))


def to_seq(values, k):
    return across(values, lambda s, f: (s ^ k, f))


def add_parts(parts, low, high):
    total = parts[0][low:high].astype(F32)
    for part in parts[1:]:
        total = total + part[low:high].astype(F32)
    return total


def back_blocks_body(place, u_ref, df_ref, keep_ref, send_ref):
    core = lax.rem(place[0], 2)
    group = u_ref.shape[1] // 4
    for g in range(1):
        acc = lax.dot_general(u_ref[...], df_ref[...], (((0,), (0,)), ((), ())), preferred_element_type=F32)
        at = pl.program_id(0) * 4
        for j in range(4):
            slot = place[1 + at + j]
            value = acc[j * group : (j + 1) * group].astype(BF)

            @pl.when(core == j % 2)
            def _():
                keep_ref[slot] = value

            @pl.when(core != j % 2)
            def _():
                send_ref[slot] = value


def back_blocks(place, u, df):
    rows, hidden = u.shape
    width = df.shape[1]
    out = jax.ShapeDtypeStruct((16, hidden // 32, width), BF)
    return pl.pallas_call(
        back_blocks_body,
        grid=(8,),
        in_specs=[SM, pl.BlockSpec((rows, hidden // 8), lambda g: (0, g)), pl.BlockSpec((rows, width), lambda g: (0, 0))],
        out_specs=[pl.BlockSpec((16, hidden // 32, width), lambda g: (0, 0, 0))] * 2,
        out_shape=[out, out],
        compiler_params=pltpu.CompilerParams(vmem_limit_bytes=24 * MIB, dimension_semantics=("arbitrary",)),
        cost_estimate=pl.CostEstimate(flops=2 * rows * hidden * width, bytes_accessed=8_000_000, transcendentals=0),
        name="back_blocks",
    )(place, u, df)


def in_blocks_body(place, h_ref, dz_ref, a0, a1, a2, a3, db_ref, sum_ref, keep_ref, send_ref):
    even = lax.rem(place[0], 2) == 0
    core = lax.rem(place[0], 2)
    own = lax.div(place[0], 8)
    step = pl.program_id(0)

    def store(block, low, a, b):
        count = a.shape[0]
        keep_ref[place[1 + block + core], pl.ds(low, count), :] = jnp.where(even, a, b).astype(BF)
        send_ref[place[2 + block - core], pl.ds(low, count), :] = jnp.where(even, b, a).astype(BF)

    def put(block, low, acc):
        store(block, low, acc[0:24], acc[24:48])

    def chunk(which):
        for g in range(2):
            acc = lax.dot_general(
                h_ref[:, g * 384 : (g + 1) * 384], dz_ref[...], (((0,), (0,)), ((), ())), preferred_element_type=F32
            )
            for j in range(0, 16, 2):
                put(g * 16 + j, which * 24, acc[j * 24 : (j + 2) * 24])

    for which in range(4):
        pl.when(step == which)(lambda which=which: chunk(which))

    @pl.when(step == 4)
    def _():
        for mask, piece in zip((0, place[33], place[34], 3), (a0, a1, a2, a3)):
            acc = lax.dot_general(piece[...], db_ref[...], (((0,), (0,)), ((), ())), preferred_element_type=F32)
            for j in range(0, 8, 2):
                put((own ^ mask) * 8 + j, 96, acc[j * 24 : (j + 2) * 24])
        width = sum_ref.shape[1]
        line = lax.broadcasted_iota(jnp.int32, (8, width), 0)

        def note(j):
            wide = sum_ref[8 + j // 8 : 9 + j // 8, :] + jnp.zeros((8, width), F32)
            short, wide = (
                pltpu.roll(v, shift, 1) if shift % width else v
                for v, shift in ((sum_ref[0:8, :], width - 24 * j), (wide, width - 96 * (j % 8)))
            )
            return jnp.where(line == 6, wide, short)

        for j in range(0, 32, 2):
            store(j, 120, note(j), note(j + 1))


def in_blocks(place, hidden_low, dz, attn, dbr, sums):
    rows, width = hidden_low.shape
    chunks = dz.shape[1] // width
    out = jax.ShapeDtypeStruct((16, 128, width), BF)
    whole = pl.BlockSpec((rows, width), lambda g: (0, 0))
    return pl.pallas_call(
        in_blocks_body,
        grid=(chunks + 1,),
        in_specs=[SM, whole, pl.BlockSpec((rows, width), lambda g: (0, jnp.minimum(g, chunks - 1)))]
        + [pl.BlockSpec(attn[0].shape, lambda g: (0, 0))] * 4
        + [whole]
        + [pl.BlockSpec(sums.shape, lambda g: (0, 0))],
        out_specs=[pl.BlockSpec((16, 128, width), lambda g: (0, 0, 0))] * 2,
        out_shape=[out, out],
        compiler_params=pltpu.CompilerParams(vmem_limit_bytes=26 * MIB, dimension_semantics=("arbitrary",)),
        cost_estimate=pl.CostEstimate(flops=2 * rows * width * (dz.shape[1] + width), bytes_accessed=12_000_000, transcendentals=0),
        name="in_blocks",
    )(place, hidden_low, dz, *attn, dbr, sums)


def shards(
    inputs,
    w_query,
    w_key,
    w_value,
    b_value,
    w_out,
    b_out,
    norm1_gain,
    norm1_bias,
    w_in,
    b_in,
    w_back,
    b_back,
    norm2_gain,
    norm2_bias,
    w_relative,
    bias_content,
    bias_position,
    bias_type,
    type_embed,
    lengths,
    token_types,
    owners,
    grad_output,
):
    seqs, fsdps = lax.axis_size("seq"), lax.axis_size("fsdp")
    direct = seqs == 4 and fsdps == 8
    own, rank = lax.axis_index("seq"), lax.axis_index("fsdp")
    pack_count = owners.shape[0]
    sliver_rows = inputs.shape[1]
    width = inputs.shape[2]
    local_rows = w_query.shape[0]
    local_cols = width // seqs
    local_heads = w_relative.shape[1]
    scale = DH ** -0.5
    dealt = reload(owners, inputs, True)
    mine = lax.all_to_all(dealt, "fsdp", split_axis=0, concat_axis=1, tiled=True)[0]
    row_count = mine.shape[0]
    chosen = (owners == rank).astype(jnp.int32)
    pack_types = jnp.sum(chosen[:, None] * token_types, axis=0)
    pack_sizes = jnp.sum(chosen[:, None] * lengths, axis=0)
    pack_rows = pack_types.shape[0]

    def head_columns(weight):
        return lax.dynamic_slice_in_dim(weight, own * local_cols, local_cols, 1)

    block = jnp.concatenate(
        [head_columns(w) for w in (w_query, w_key, w_value)] + [w_relative.reshape(local_rows, local_cols)], axis=1
    )
    long_vectors = (b_value, b_out, norm1_gain, norm1_bias, b_back, norm2_gain, norm2_bias, b_in)
    head_vectors = (bias_content, bias_position, bias_type, type_embed[0], type_embed[1])

    def placed_at(value, row, lane):
        value = value.reshape(-1, value.shape[-1])
        return jnp.pad(value, ((row, 8 - row - value.shape[0]), (lane, width - lane - value.shape[1])))

    corner = placed_at(b_value, 0, 0)
    for number, value in enumerate(long_vectors[1:]):
        corner = corner + placed_at(value, number + 1, 0)
    for number, value in enumerate(head_vectors[:3]):
        corner = corner + placed_at(value, 0, (number + 3) * 128)
    for number, value in enumerate(head_vectors[3:]):
        corner = corner + placed_at(value, 3, (number + 3) * 128)
    early = lax.all_gather(jnp.concatenate([block, corner], axis=0), "fsdp", axis=0)
    qkvr = early[:, :local_rows].reshape(width, width)
    corners = early[:, local_rows:].astype(F32)
    full = [corners[:, n, : v.shape[0]].reshape(-1) for n, v in enumerate(long_vectors)]
    bv_full, bo_full, gain_one, shift_one, bback_full, gain_two, shift_two, bin_full = full
    heads = []
    for number, value in enumerate(head_vectors):
        row = 0 if number < 3 else 3
        lane = (number % 3 + 3) * 128
        each = corners[:, row : row + local_heads, lane : lane + value.shape[1]]
        heads.append(jnp.moveaxis(each, 0, 1).reshape(local_heads, DH))
    content_full, position_full, typebias_full, embed_zero, embed_one = heads
    bv_own = lax.dynamic_slice_in_dim(bv_full, own * local_cols, local_cols, 0)
    head = jnp.stack(
        [
            content_full,
            position_full,
            typebias_full,
            embed_zero,
            embed_one,
            bv_own.reshape(local_heads, DH),
        ],
        axis=1,
    )
    head = jnp.pad(head, ((0, 0), (0, 2), (0, 64)))

    deep = w_back.shape[0] // seqs
    late = jnp.concatenate(
        [
            lax.dynamic_slice_in_dim(w_in, own * width, width, 1),
            lax.dynamic_slice_in_dim(w_back, own * deep, deep, 0),
            head_columns(w_out),
            jnp.zeros((local_rows, 64), BF),
        ],
        axis=1,
    )
    late = lax.all_gather(late, ("fsdp", "seq"), axis=0).reshape(fsdps, seqs, local_rows, -1)
    if not direct:
        eighth_rows = width // 8
        turned_in = jnp.swapaxes(late, 1, 2).reshape(8, eighth_rows, seqs, -1)
        natural = late[..., width : 2 * width].reshape(8, seqs, eighth_rows, width)
        turned_in = jnp.swapaxes(turned_in, 1, 2)
        late = jnp.concatenate([turned_in[..., :width], natural, turned_in[..., 2 * width :]], axis=-1)

    longest = jnp.argmax(pack_sizes).astype(jnp.int32)
    start = jnp.sum(jnp.where(jnp.arange(3) < longest, pack_sizes, 0))
    near = jnp.sum(jnp.where(jnp.arange(3) == (longest + 1) % 3, pack_sizes, 0))
    parity = rank & 1
    place = jnp.stack([own, start, near, 1 + parity, 2 - parity]).astype(jnp.int32)
    row_index = jnp.arange(pack_rows, dtype=jnp.int32)
    position = jnp.where(
        row_index < LONGEST,
        row_index,
        jnp.where(row_index < LONGEST + near, row_index - LONGEST, row_index - LONGEST - near),
    )
    sine, cosine = angles_of(position, width)
    key_pos = jnp.concatenate([cosine, sine], axis=-1).astype(BF)
    key_pos_t = key_pos.T
    turned_types = lax.dynamic_slice_in_dim(
        jnp.concatenate([pack_types, pack_types]), start, pack_rows, 0
    )[:, None]
    wrel = qkvr[:, 3 * local_cols :].reshape(width, local_heads, DH)
    wrel_rows = jnp.pad(jnp.transpose(wrel, (1, 0, 2)), ((0, 0), (0, 0), (0, 64)))
    wrel_cols = jnp.pad(jnp.transpose(wrel, (1, 2, 0)), ((0, 0), (0, 64), (0, 0)))
    together = lambda n: qkvr[:, n * local_cols : (n + 1) * local_cols].reshape(width, local_heads, DH)
    paired = jnp.concatenate([together(0), together(1)], axis=2).reshape(width, 2 * local_cols)
    w_qkv = jnp.concatenate([paired, qkvr[:, 2 * local_cols : 3 * local_cols], jnp.zeros((width, 64), BF)], axis=1)

    pieces = [mine, to_first(mine), to_second(mine)]
    pieces.append(to_second(pieces[1]))
    pieces, wrel_rows = lax.optimization_barrier((pieces, wrel_rows))
    qx, pq, kx, kxt, vx, vxt = project(place, pieces, w_qkv, head, turned_types)
    big, small, ox, *head_out = attend(place, qx, pq, kxt, vx, key_pos_t, wrel_cols, sine, cosine)
    order = own ^ jnp.arange(seqs, dtype=jnp.int32)
    deal = lambda v: [v[0], to_first(v[1]), to_second(v[2]), to_seq(v[3], 3)]
    attn = deal(head_out)
    mid_vectors = jnp.stack([bo_full, gain_one, shift_one, bback_full, gain_two, shift_two, gain_two, gain_two])
    result, hidden_low, act_low, pre_grad, ffn_grad, branch_grad, sum_one_grad, *douts, short_sums = middle(
        place, attn, mine, grad_output[0], late, mid_vectors, bin_full[None]
    )
    activations = result.reshape(1, row_count, width)
    douts = deal(douts)
    devices = seqs * fsdps
    device = own * fsdps + rank
    fine = width // devices
    deep = act_low.shape[1] // devices
    kept_place = jnp.where((order == 1) | (order == 2), jnp.where(parity == 1, 3 - order, order), order)
    if direct:
        relative = jnp.arange(32, dtype=jnp.int32) ^ device
        bit = lambda n: (relative >> n) & 1
        flip = (bit(0) ^ parity) == 1
        one, two = jnp.where(flip, bit(4), bit(3)), jnp.where(flip, bit(3), bit(4))
        me, masks = device[None], place[3:5]
        in_table = jnp.concatenate([me, one * 8 + two * 4 + bit(1) * 2 + bit(2), masks]).astype(jnp.int32)
        back_table = jnp.concatenate([me, bit(1) * 8 + one * 4 + two * 2 + bit(2), masks]).astype(jnp.int32)
        kept, sent = in_blocks(in_table, hidden_low, pre_grad, attn, branch_grad, short_sums)
        ins = [kept, to_core(sent)]
        kept, sent = back_blocks(back_table, act_low, ffn_grad)
        backs = [kept, to_core(sent)]
        back_out, in_out = merge(backs, ins, 8)
        douts, back_out, in_out = lax.optimization_barrier((douts, back_out, in_out))
        backs.append(to_near(back_out))
        ins.append(to_first(in_out))
    else:
        scatter = lambda v: lax.psum_scatter(v, ("seq", "fsdp"), scatter_dimension=0, tiled=True)
        w_back_grad = scatter(contract_rows(act_low, ffn_grad))
        w_in_grad = scatter(contract_rows(hidden_low, pre_grad))
        spun = contract_rows(jnp.concatenate(attn, axis=1), branch_grad).reshape(seqs, local_cols, width)
        w_out_grad = scatter(jnp.take(spun, kept_place, axis=0).reshape(width, width))

    tkeep, tsend, rel, sums = attend_back(
        place, douts, big, small, ox, qx, pq, kx, vxt, key_pos, wrel_rows, sine, cosine, turned_types, head
    )
    if direct:
        bundle = qkv_blocks(fsdps, pieces, tkeep, tsend, rel, sums)
    else:
        grad = contract_rows(pieces[0], tkeep[:row_count]) + contract_rows(pieces[2], tkeep[row_count:])
        grad = grad + contract_rows(pieces[1], tsend[:row_count]) + contract_rows(pieces[3], tsend[row_count:])
        grad = jnp.swapaxes(grad.reshape(seqs, fsdps, fine, 640), 0, 1).reshape(fsdps, local_rows, 640)
        tall = rel.reshape(fsdps, local_rows, 256)
        bundle = jnp.concatenate([grad[..., :512], grad[..., 512:] + tall[..., :128], tall[..., 128:]], axis=2)
        notes = jnp.concatenate([sums[0], sums[1], sums[2], jnp.zeros((8, 384), F32)], axis=1)
        bundle = jnp.concatenate([bundle, jnp.broadcast_to(notes[None], (fsdps,) + notes.shape)], axis=1).astype(BF)
    total = lax.psum_scatter(bundle, "fsdp", scatter_dimension=0, tiled=True)[0].astype(F32)
    dx_send = contract_cols(tsend, w_qkv).astype(BF)
    if direct:
        dx_send, backs, ins, bundle = lax.optimization_barrier((dx_send, backs, ins, bundle))
        back_out, in_out = merge(backs, ins, 4)
        backs.append(to_first(back_out))
        ins.append(to_second(in_out))
    dx_first = to_first(dx_send)
    dx_keep = contract_cols(tkeep, w_qkv)
    if direct:
        dx_first, backs, ins = lax.optimization_barrier((dx_first, backs, ins))
    dx_out = (dx_keep[row_count:] + dx_first[row_count:].astype(F32)).astype(BF)
    dx_second = to_second(dx_out)
    if direct:
        back_out, in_out = merge(backs, ins, 2)
        backs.append(to_second(back_out))
        ins.append(to_near(in_out))
        dx_second, backs, ins = lax.optimization_barrier((dx_second, backs, ins))
    input_rows = sum_one_grad + dx_keep[:row_count] + dx_first[:row_count].astype(F32) + dx_second.astype(F32)
    input_rows = input_rows.astype(BF).reshape(fsdps, sliver_rows, width)
    returned = lax.all_to_all(input_rows, "fsdp", split_axis=0, concat_axis=0, tiled=True)
    input_grad = reload(owners, returned, False)
    if direct:
        far_out, total = lax.optimization_barrier((merge(backs, ins, 1, False)[0], total))
        far = to_far(far_out)
        cut = kept.shape[1]
    if not direct:
        short_sums = lax.psum(short_sums, ("seq", "fsdp"))
        short_grads = lax.dynamic_slice(short_sums, (0, device * fine), (8, fine))
        in_bias_grad = lax.dynamic_slice(short_sums, (8 + device * deep // width, device * deep % width), (1, deep))[0]
    own_qkv = total[:local_rows].astype(BF).reshape(seqs, fine, width)
    block_for = lambda mask: lax.dynamic_index_in_dim(own_qkv, own ^ mask, 0, keepdims=True)
    swapped = jnp.concatenate(deal([block_for(m) for m in (0, place[3], place[4], 3)]), axis=0)
    swapped = jnp.take(swapped, kept_place, axis=0).astype(F32)
    both = swapped[:, :, : 2 * local_cols].reshape(seqs, fine, local_heads, 2, DH)
    both = jnp.transpose(both, (3, 1, 0, 2, 4)).reshape(2, fine, width)
    w_value_grad = jnp.transpose(swapped[:, :, 2 * local_cols : 3 * local_cols], (1, 0, 2)).reshape(fine, width)
    if direct:
        _, _, far, _ = lax.optimization_barrier((both, w_value_grad, far, input_grad))
        w_back_grad = add_parts(backs + [far[:, :cut]], 0, 1)[0]
        in_total = add_parts(ins + [far[:, cut:]], 0, 1)[0]
        w_in_grad = jnp.concatenate([in_total[c * 24 : (c + 1) * 24] for c in range(4)], axis=1)
        w_out_grad = in_total[96:120]
        short_grads, in_bias_grad = in_total[120:128, :fine], in_total[126, :deep]
    rel_total = total[:local_rows, 3 * local_cols :].reshape(local_rows, local_heads, DH)
    notes = total[local_rows:, :384].reshape(8, 3, 128)
    eighth = DH // fsdps
    mine_sums = lax.dynamic_slice(notes, (0, 0, rank * eighth), (8, 3, eighth))
    value_bias_grad = lax.dynamic_slice(notes[5, :, :DH].reshape(-1), (rank * fine,), (fine,))
    return (
        activations,
        input_grad,
        both[0],
        both[1],
        w_value_grad,
        value_bias_grad,
        w_out_grad,
        short_grads[4],
        short_grads[0],
        short_grads[1],
        w_in_grad,
        in_bias_grad,
        w_back_grad,
        short_grads[5],
        short_grads[2],
        short_grads[3],
        rel_total,
        mine_sums[0],
        mine_sums[1],
        mine_sums[2],
        mine_sums[3:5],
    )


def solution(mesh):
    placed = (
        P(None, ("seq", "fsdp"), None),
        P("fsdp", None),
        P("fsdp", None),
        P("fsdp", None),
        P("fsdp"),
        P("fsdp", None),
        P("fsdp"),
        P("fsdp"),
        P("fsdp"),
        P("fsdp", None),
        P("fsdp"),
        P("fsdp", None),
        P("fsdp"),
        P("fsdp"),
        P("fsdp"),
        P("fsdp", "seq", None),
        P("seq", "fsdp"),
        P("seq", "fsdp"),
        P("seq", "fsdp"),
        P(None, "seq", "fsdp"),
        P(),
        P(),
        P(),
        P("fsdp", "seq", None),
    )
    return jax.shard_map(
        shards,
        mesh=mesh,
        in_specs=placed,
        out_specs=(
            P("fsdp", "seq", None),
            P(None, ("seq", "fsdp"), None),
            P(("seq", "fsdp"), None),
            P(("seq", "fsdp"), None),
            P(("seq", "fsdp"), None),
            P(("seq", "fsdp")),
            P(("seq", "fsdp"), None),
            P(("seq", "fsdp")),
            P(("seq", "fsdp")),
            P(("seq", "fsdp")),
            P(("seq", "fsdp"), None),
            P(("seq", "fsdp")),
            P(("seq", "fsdp"), None),
            P(("seq", "fsdp")),
            P(("seq", "fsdp")),
            P(("seq", "fsdp")),
            P("fsdp", "seq", None),
            P("seq", "fsdp"),
            P("seq", "fsdp"),
            P("seq", "fsdp"),
            P(None, "seq", "fsdp"),
        ),
        check_vma=False,
    )
```

```python
import functools

import jax
import jax.numpy as jnp
from jax import lax
from jax.experimental import pallas as pl
from jax.experimental.pallas import tpu as pltpu
from jax.sharding import PartitionSpec as P

DH = 64
LONGEST = 1024
QB = 256
BLOCKED = -1e30
BF = jnp.bfloat16
F32 = jnp.float32
VM = pl.BlockSpec(memory_space=pltpu.VMEM)
SM = pl.BlockSpec(memory_space=pltpu.SMEM)
MIB = 1024 * 1024


def lanes_of(rows, width=128):
    return lax.broadcasted_iota(jnp.int32, (rows, width), 1)


def split3(value):
    high = value.astype(BF).astype(F32)
    rest = value - high
    middle = rest.astype(BF).astype(F32)
    return high, middle, rest - middle


def masks_of(place):
    return 0, place[3], place[4], 3


def pick(lane, first, columns, base):
    for number, column in enumerate(columns):
        base = jnp.where(lane == first + number, column, base)
    return base


def project_body(place, x0, x1, x2, x3, w_ref, head_ref, tcol_ref, qx_ref, pq_ref, kx_ref, kxt_ref, vx_ref, vxt_ref, rolled):
    own, start, near = place[0], place[1], place[2]
    scale = DH ** -0.5
    rows = qx_ref.shape[1]
    part = x0.shape[0]
    for mask, piece in zip(masks_of(place), (x0, x1, x2, x3)):
        y = jnp.dot(piece[...], w_ref[...], preferred_element_type=F32)
        base = pl.multiple_of((own ^ mask) * part, 8)
        for c in range(5):
            column = y[:, c * 128 : (c + 1) * 128]
            rolled[c, pl.ds(base, part), :] = column
            rolled[c, pl.ds(pl.multiple_of(base + rows, 8), part), :] = column

    def block(r, carry):
        row = pl.multiple_of(r * QB, QB)
        lane = lanes_of(QB)
        kind = tcol_ref[pl.ds(row, QB), :]
        index = row + lax.broadcasted_iota(jnp.int32, (QB, 1), 0)
        small = index >= LONGEST
        first = jnp.where(small & (index < LONGEST + near), 1.0, 0.0)
        second = jnp.where(small & (index >= LONGEST + near), 1.0, 0.0)
        one = jnp.where(kind == 1, 1.0, 0.0)
        zero = 1.0 - one
        for h in range(3):
            both = rolled[h, pl.ds(start + row, QB), :].astype(BF).astype(F32)
            if h < 2:
                v = rolled[3, pl.ds(start + row, QB), :]
                v = v if h == 0 else pltpu.roll(v, 64, 1)
            else:
                v = rolled[4, pl.ds(start + row, QB), :]
            head = head_ref[h]
            content = (both + head[0:1]) * scale
            position = ((both + head[1:2]) * scale).astype(BF)
            typed = (both + head[2:3]) * scale
            differ = jnp.sum(typed * head[3:4], axis=1, keepdims=True)
            same = jnp.sum(typed * head[4:5], axis=1, keepdims=True)
            for_zero = jnp.where(kind == 1, differ, same)
            for_one = jnp.where(kind == 1, same, differ)
            columns = [*split3(for_zero), *split3(for_one), second * BLOCKED, first * BLOCKED]
            qx = pick(lane, 64, columns, jnp.where(lane < 64, content, 0.0)).astype(BF)
            qx_ref[h, pl.ds(row, QB), :] = qx
            raw = pltpu.roll(both, 64, 1)
            pq_ref[h, pl.ds(row, QB), :] = jnp.where(lane < 64, position.astype(F32), raw).astype(BF)
            kx = pick(lane, 64, [zero, zero, zero, one, one, one, first, second], jnp.where(lane < 64, raw, 0.0))
            kx_ref[h, pl.ds(row, QB), :] = kx.astype(BF)
            kxt_ref[h, :, pl.ds(row, QB)] = jnp.transpose(kx, (1, 0)).astype(BF)
            vx = jnp.where(lane < 64, v + head[5:6], jnp.where(lane < 67, 1.0, 0.0)).astype(BF)
            vx_ref[h, pl.ds(row, QB), :] = vx
            vxt_ref[h, :, pl.ds(row, QB)] = jnp.transpose(vx.astype(F32), (1, 0)).astype(BF)
        return carry

    lax.fori_loop(0, rows // QB, block, 0)


def project(place, pieces, w_qkv, head, tcol):
    rows = 4 * pieces[0].shape[0]
    tall = jax.ShapeDtypeStruct((3, rows, 128), BF)
    wide = jax.ShapeDtypeStruct((3, 128, rows), BF)
    return pl.pallas_call(
        project_body,
        in_specs=[SM] + [VM] * 7,
        out_specs=[VM] * 6,
        out_shape=[tall, tall, tall, wide, tall, wide],
        scratch_shapes=[pltpu.VMEM((5, 2 * rows, 128), F32)],
        compiler_params=pltpu.CompilerParams(vmem_limit_bytes=26 * MIB),
        cost_estimate=pl.CostEstimate(flops=2 * rows * 768 * 640, bytes_accessed=10_000_000, transcendentals=0),
        name="project",
    )(place, *pieces, w_qkv, head, tcol)


def attend_body(place, qx_ref, pq_ref, kxt_ref, vx_ref, kpt_ref, wrt_ref, sn_ref, cs_ref, big_ref, small_ref, ox_ref, o0, o1, o2, o3, keys, left, outs):
    h, i = pl.program_id(0), pl.program_id(1)
    own, start = place[0], place[1]
    width = kpt_ref.shape[0]
    half = width // 2
    rows = kpt_ref.shape[1]

    @pl.when((h == 0) & (i == 0))
    def _():
        keys[0:width, :] = kpt_ref[...]

    @pl.when(i == 0)
    def _():
        keys[width:, :] = kxt_ref[0]

    rel = jnp.dot(pq_ref[0], wrt_ref[0], preferred_element_type=F32)
    r1, r2 = rel[:, :half], rel[:, half:]
    sn, cs = sn_ref[...], cs_ref[...]
    left[:, 0:half] = (r1 * sn + r2 * cs).astype(BF)
    left[:, half:width] = (r2 * sn - r1 * cs).astype(BF)
    left[:, width:] = qx_ref[0]

    def attend(low, high, store):
        score = jnp.dot(left[...], keys[:, low:high], preferred_element_type=F32)
        top = jnp.max(score, axis=1, keepdims=True)
        raised = jnp.exp(score - top).astype(BF)
        store[0] = raised
        mixed = jnp.dot(raised, vx_ref[0, low:high, :], preferred_element_type=F32)
        inverse = 1.0 / mixed[:, 64:65]
        lane = lanes_of(QB)
        ox = jnp.where(lane < 64, mixed * inverse, jnp.where(lane == 64, inverse, 0.0))
        ox_ref[0] = ox
        row = pl.multiple_of(i * QB, QB)
        outs[h, pl.ds(row, QB), :] = ox
        outs[h, pl.ds(pl.multiple_of(row + rows, QB), QB), :] = ox

    @pl.when(i < LONGEST // QB)
    def _():
        attend(0, LONGEST, big_ref)

    @pl.when(i >= LONGEST // QB)
    def _():
        attend(LONGEST, rows, small_ref)

    @pl.when((h == 2) & (i == pl.num_programs(1) - 1))
    def _():
        part = o0.shape[0]
        for mask, out in zip(masks_of(place), (o0, o1, o2, o3)):
            at = lax.rem((own ^ mask) * part + rows - start, rows)
            out[...] = jnp.concatenate([outs[g, pl.ds(at, part), :][:, 0:64] for g in range(3)], axis=1).astype(BF)


def attend(place, qx, pq, kxt, vx, kpt, wrt, sn, cs):
    rows = qx.shape[1]
    width = kpt.shape[0]
    blocks = rows // QB
    bigs = LONGEST // QB
    rest = rows - LONGEST
    per_block = lambda h, i: (h, i, 0)
    per_head = lambda h, i: (h, 0, 0)
    whole2 = lambda h, i: (0, 0)
    part = rows // 4
    out_piece = jax.ShapeDtypeStruct((part, 192), BF)
    return pl.pallas_call(
        attend_body,
        grid=(3, blocks),
        in_specs=[
            SM,
            pl.BlockSpec((1, QB, 128), per_block),
            pl.BlockSpec((1, QB, 128), per_block),
            pl.BlockSpec((1, 128, rows), per_head),
            pl.BlockSpec((1, rows, 128), per_head),
            pl.BlockSpec((width, rows), whole2, pipeline_mode=pl.Buffered(1)),
            pl.BlockSpec((1, 128, width), per_head),
            pl.BlockSpec((QB, width // 2), lambda h, i: (i, 0)),
            pl.BlockSpec((QB, width // 2), lambda h, i: (i, 0)),
        ],
        out_specs=[
            pl.BlockSpec((1, QB, LONGEST), lambda h, i: (h, jnp.minimum(i, bigs - 1), 0)),
            pl.BlockSpec((1, QB, rest), lambda h, i: (h, jnp.maximum(i - bigs, 0), 0)),
            pl.BlockSpec((1, QB, 128), per_block),
        ]
        + [pl.BlockSpec((part, 192), whole2)] * 4,
        out_shape=[
            jax.ShapeDtypeStruct((3, LONGEST, LONGEST), BF),
            jax.ShapeDtypeStruct((3, rest, rest), BF),
            jax.ShapeDtypeStruct((3, rows, 128), F32),
        ]
        + [out_piece] * 4,
        scratch_shapes=[
            pltpu.VMEM((width + 128, rows), BF),
            pltpu.VMEM((QB, width + 128), BF),
            pltpu.VMEM((3, 2 * rows, 128), F32),
        ],
        compiler_params=pltpu.CompilerParams(vmem_limit_bytes=26 * MIB, dimension_semantics=("arbitrary", "arbitrary")),
        cost_estimate=pl.CostEstimate(flops=12_000_000_000, bytes_accessed=20_000_000, transcendentals=4_000_000),
        name="attend",
    )(place, qx, pq, kxt, vx, kpt, wrt, sn, cs)


def back_body(place, d0, d1, d2, d3, big_ref, small_ref, ox_ref, qx_ref, pq_ref, kx_ref, vxt_ref, kp_ref, wr_ref, sn_ref, cs_ref, tcol_ref, head_ref, gkeep_ref, gsend_ref, rel_ref, sum_ref, douts, dkt, dvt, gwt, grads):
    h, i = pl.program_id(0), pl.program_id(1)
    own, start = place[0], place[1]
    rows, width = kp_ref.shape
    half = width // 2
    scale = DH ** -0.5
    part = d0.shape[0]
    last = pl.num_programs(1) - 1
    row = pl.multiple_of(i * QB, QB)
    again = pl.multiple_of(row + rows, QB)

    @pl.when((h == 0) & (i == 0))
    def _():
        blank = jnp.zeros((part, 64), F32)
        for mask, piece in zip(masks_of(place), (d0, d1, d2, d3)):
            values = piece[...].astype(F32)
            base = pl.multiple_of((own ^ mask) * part, 8)
            for g in range(3):
                padded = jnp.concatenate([values[:, g * 64 : (g + 1) * 64], blank], axis=1)
                douts[g, pl.ds(base, part), :] = padded
                douts[g, pl.ds(pl.multiple_of(base + rows, 8), part), :] = padded

    @pl.when(i == 0)
    def _():
        dkt[...] = jnp.zeros_like(dkt)
        dvt[...] = jnp.zeros_like(dvt)
        gwt[...] = jnp.zeros_like(gwt)
        sum_ref[...] = jnp.zeros_like(sum_ref)

    lane = lanes_of(QB)
    dout = douts[h, pl.ds(start + row, QB), :]
    ox = ox_ref[0]
    inverse = ox[:, 64:65]
    dot_row = jnp.sum(dout * ox, axis=1, keepdims=True)
    dox = pick(lane, 64, [-x for x in split3(dot_row)], dout).astype(BF)
    dout_t = jnp.transpose(dout * inverse, (1, 0))[0:64].astype(BF)
    qx = qx_ref[0]
    qc_t = jnp.transpose(qx.astype(F32), (1, 0))[0:64].astype(BF)
    pq = pq_ref[0].astype(F32)
    qp_t = jnp.transpose(pq, (1, 0))[0:64].astype(BF)
    sn, cs = sn_ref[...], cs_ref[...]

    def back(low, high, saved):
        raised = saved[0]
        dprob = jnp.dot(dox, vxt_ref[0, :, low:high], preferred_element_type=F32)
        dscore = (raised.astype(F32) * (dprob * inverse)).astype(BF)
        dvt[:, low:high] += jnp.dot(dout_t, raised, preferred_element_type=F32)
        dkt[:, low:high] += jnp.dot(qc_t, dscore, preferred_element_type=F32)
        da = jnp.dot(dscore, kp_ref[low:high, :], preferred_element_type=F32)
        dqx = jnp.dot(dscore, kx_ref[0, low:high, :], preferred_element_type=F32)
        da1, da2 = da[:, 0:half], da[:, half:width]
        drel = jnp.concatenate([(da1 * sn - da2 * cs).astype(BF), (da1 * cs + da2 * sn).astype(BF)], axis=1)
        dqp = jnp.dot(drel, wr_ref[0], preferred_element_type=F32)
        gwt[...] += jnp.dot(qp_t, drel, preferred_element_type=F32)
        kind = tcol_ref[...]
        over_zero, over_one = dqx[:, 64:65], dqx[:, 67:68]
        same = jnp.where(kind == 1, over_one, over_zero)
        differ = jnp.where(kind == 1, over_zero, over_one)
        head = head_ref[0]
        dqt = differ * head[3:4] + same * head[4:5]
        dqc = jnp.where(lane < 64, dqx, 0.0)
        dq = (dqc + dqp + dqt) * scale
        grads[h, pl.ds(row, QB), :] = dq
        typed = (pltpu.roll(pq, 64, 1) + head[2:3]) * scale
        sums = [dqc * scale, dqp * scale, dqt * scale, differ * typed, same * typed]
        for number, values in enumerate(sums):
            sum_ref[0, number : number + 1, :] += jnp.sum(values, axis=0, keepdims=True)

    @pl.when(i < LONGEST // QB)
    def _():
        back(0, LONGEST, big_ref)

    @pl.when(i >= LONGEST // QB)
    def _():
        back(LONGEST, rows, small_ref)

    @pl.when(i == last)
    def _():
        dk = jnp.transpose(dkt[...], (1, 0))
        dq = grads[h, 0:rows, :]
        pair = jnp.concatenate([dq[:, 0:64], dk], axis=1)
        grads[h, 0:rows, :] = pair
        grads[h, rows : 2 * rows, :] = pair
        dv = jnp.transpose(dvt[...], (1, 0)).astype(BF).astype(F32)
        sum_ref[0, 5:6, 0:64] = jnp.sum(dv, axis=0, keepdims=True)
        blank = jnp.zeros_like(dv)
        rel = jnp.transpose(gwt[...], (1, 0))
        empty = jnp.zeros_like(rel)

        @pl.when(h == 0)
        def _():
            padded = jnp.concatenate([dv, blank], axis=1)
            grads[3, 0:rows, :] = padded
            grads[3, rows : 2 * rows, :] = padded
            rel_ref[:, 0:128] = jnp.concatenate([empty, rel], axis=1)

        @pl.when(h == 1)
        def _():
            rel_ref[:, 128:256] = jnp.concatenate([rel, empty], axis=1)
            padded = grads[3, 0:rows, :] + jnp.concatenate([blank, dv], axis=1)
            grads[3, 0:rows, :] = padded
            grads[3, rows : 2 * rows, :] = padded

        @pl.when(h == 2)
        def _():
            padded = jnp.concatenate([dv, blank], axis=1)
            grads[4, 0:rows, :] = padded
            grads[4, rows : 2 * rows, :] = padded
            rel_ref[:, 128:256] += jnp.concatenate([empty, rel], axis=1)
            spots = ((gkeep_ref, 0), (gsend_ref, 0), (gkeep_ref, part), (gsend_ref, part))
            for mask, (out, low) in zip(masks_of(place), spots):
                at = lax.rem((own ^ mask) * part + rows - start, rows)
                for c in range(5):
                    out[low : low + part, c * 128 : (c + 1) * 128] = grads[c, pl.ds(at, part), :].astype(BF)


def attend_back(place, douts, big, small, ox, qx, pq, kx, vxt, kp, wr, sn, cs, tcol, head):
    rows, width = kp.shape
    blocks = rows // QB
    bigs = LONGEST // QB
    rest = rows - LONGEST
    part = rows // 4
    per_block = lambda h, i: (h, i, 0)
    per_head = lambda h, i: (h, 0, 0)
    whole2 = lambda h, i: (0, 0)
    return pl.pallas_call(
        back_body,
        grid=(3, blocks),
        in_specs=[SM]
        + [pl.BlockSpec((part, 192), whole2)] * 4
        + [
            pl.BlockSpec((1, QB, LONGEST), lambda h, i: (h, jnp.minimum(i, bigs - 1), 0)),
            pl.BlockSpec((1, QB, rest), lambda h, i: (h, jnp.maximum(i - bigs, 0), 0)),
            pl.BlockSpec((1, QB, 128), per_block),
            pl.BlockSpec((1, QB, 128), per_block),
            pl.BlockSpec((1, QB, 128), per_block),
            pl.BlockSpec((1, rows, 128), per_head),
            pl.BlockSpec((1, 128, rows), per_head),
            pl.BlockSpec((rows, width), whole2, pipeline_mode=pl.Buffered(1)),
            pl.BlockSpec((1, width, 128), per_head),
            pl.BlockSpec((QB, width // 2), lambda h, i: (i, 0)),
            pl.BlockSpec((QB, width // 2), lambda h, i: (i, 0)),
            pl.BlockSpec((QB, 1), lambda h, i: (i, 0)),
            pl.BlockSpec((1, 8, 128), per_head),
        ],
        out_specs=[pl.BlockSpec((2 * part, 640), whole2)] * 2
        + [pl.BlockSpec((width, 256), whole2), pl.BlockSpec((1, 8, 128), per_head)],
        out_shape=[jax.ShapeDtypeStruct((2 * part, 640), BF)] * 2
        + [jax.ShapeDtypeStruct((width, 256), F32), jax.ShapeDtypeStruct((3, 8, 128), F32)],
        scratch_shapes=[
            pltpu.VMEM((3, 2 * rows, 128), F32),
            pltpu.VMEM((64, rows), F32),
            pltpu.VMEM((64, rows), F32),
            pltpu.VMEM((64, width), F32),
            pltpu.VMEM((5, 2 * rows, 128), F32),
        ],
        compiler_params=pltpu.CompilerParams(vmem_limit_bytes=36 * MIB, dimension_semantics=("arbitrary", "arbitrary")),
        cost_estimate=pl.CostEstimate(flops=20_000_000_000, bytes_accessed=25_000_000, transcendentals=0),
        name="attend_back",
    )(place, *douts, big, small, ox, qx, pq, kx, vxt, kp, wr, sn, cs, tcol, head)


def reload_body(outward, owners, in_ref, out_ref):
    def move(j, carry):
        if outward:
            out_ref[owners[j]] = in_ref[j]
        else:
            out_ref[j] = in_ref[owners[j]]
        return carry

    lax.fori_loop(0, out_ref.shape[0], move, 0)


def reload(owners, rows, outward):
    return pl.pallas_call(
        functools.partial(reload_body, outward),
        in_specs=[SM, VM],
        out_specs=VM,
        out_shape=jax.ShapeDtypeStruct(rows.shape, rows.dtype),
        compiler_params=pltpu.CompilerParams(vmem_limit_bytes=6 * MIB),
        name="deal" if outward else "reload",
    )(owners, rows)


def qkv_blocks_body(x0, x1, x2, x3, tkeep_ref, tsend_ref, rel_ref, sums_ref, out_ref, acc):
    part = x0.shape[0]
    count, high, _ = out_ref.shape
    rows = high - 8
    fine = rows // 4
    parts = ((x0, tkeep_ref, 0), (x2, tkeep_ref, part), (x1, tsend_ref, 0), (x3, tsend_ref, part))
    for number, (x, t, low) in enumerate(parts):
        value = lax.dot_general(x[...], t[low : low + part, :], (((0,), (0,)), ((), ())), preferred_element_type=F32)
        acc[...] = value if number == 0 else acc[...] + value
    notes = jnp.concatenate([sums_ref[0], sums_ref[1], sums_ref[2], jnp.zeros((8, 384), F32)], axis=1).astype(BF)
    for f in range(count):
        for s in range(4):
            value = acc[(count * s + f) * fine : (count * s + f + 1) * fine, :]
            rel = rel_ref[rows * f + fine * s : rows * f + fine * (s + 1), :]
            low, high = fine * s, fine * (s + 1)
            out_ref[f, low:high, 0:512] = value[:, 0:512].astype(BF)
            out_ref[f, low:high, 512:640] = (value[:, 512:640] + rel[:, 0:128]).astype(BF)
            out_ref[f, low:high, 640:768] = rel[:, 128:256].astype(BF)
        out_ref[f, rows : rows + 8, :] = notes


def qkv_blocks(count, pieces, tkeep, tsend, rel, sums):
    width = pieces[0].shape[1]
    return pl.pallas_call(
        qkv_blocks_body,
        in_specs=[VM] * 8,
        out_specs=VM,
        out_shape=jax.ShapeDtypeStruct((count, width // count + 8, width), BF),
        scratch_shapes=[pltpu.VMEM((width, 640), F32)],
        compiler_params=pltpu.CompilerParams(vmem_limit_bytes=20 * MIB),
        cost_estimate=pl.CostEstimate(flops=2_000_000_000, bytes_accessed=8_000_000, transcendentals=0),
        name="qkv_blocks",
    )(*pieces, tkeep, tsend, rel, sums)


def merge_body(split, *refs):
    count = len(refs) - (2 if split else 1)
    sums = []
    for group in (refs[: count // 2], refs[count // 2 : count]):
        total = group[0][...].astype(F32)
        for ref in group[1:]:
            total = total + ref[...].astype(F32)
        sums.append(total.astype(BF))
    if split:
        refs[count][...], refs[count + 1][...] = sums
    else:
        cut = sums[0].shape[1]
        refs[count][:, :cut, :] = sums[0]
        refs[count][:, cut:, :] = sums[1]


def merge(backs, ins, half, split=True):
    step = min(half, 2)
    first = half // step
    width = backs[0].shape[2]
    heights = [backs[0].shape[1], ins[0].shape[1]]
    heights = heights if split else [sum(heights)]
    block = lambda p: pl.BlockSpec((step,) + p.shape[1:], lambda g: (first + g, 0, 0))
    parts = backs + ins
    return pl.pallas_call(
        functools.partial(merge_body, split),
        grid=(first,),
        in_specs=[block(p) for p in parts],
        out_specs=[pl.BlockSpec((step, h, width), lambda g: (g, 0, 0)) for h in heights],
        out_shape=[jax.ShapeDtypeStruct((half, h, width), BF) for h in heights],
        compiler_params=pltpu.CompilerParams(vmem_limit_bytes=(14 if half == 8 else 60) * MIB, dimension_semantics=("arbitrary",)),
        cost_estimate=pl.CostEstimate(flops=half * 224 * width * 6, bytes_accessed=half * 224 * width * 8, transcendentals=0),
        name="merge",
    )(*parts)


EPS = 1e-09
GELU_A = (2.0 / 3.141592653589793) ** 0.5
GELU_B = 0.044715

def spread_norm(values):
    center = values - jnp.mean(values, axis=1, keepdims=True)
    inverse = lax.rsqrt(jnp.mean(center * center, axis=1, keepdims=True) + EPS)
    return center * inverse, inverse


def middle_body(
    place, a0, a1, a2, a3, x_ref, go_ref, w_far, vec_ref, bin_ref,
    act_ref, h_ref, u_ref, dz_ref, df_ref, dbr_ref, dr_ref, d0, d1, d2, d3, sum_ref,
    wout, slope, high, normed, acc, w_ref, arrived,
):
    own = place[0]
    width = x_ref.shape[1]

    def piece_of(number, *at):
        return pltpu.make_async_copy(w_far.at[at], w_ref.at[at], arrived.at[number])

    every = slice(None)
    out_piece = piece_of(0, every, every, every, slice(2 * width, w_far.shape[3]))
    in_piece = lambda w: piece_of(1 + w, every, pl.ds(w, 1), every, slice(0, width))
    back_piece = lambda w: piece_of(5 + w, pl.ds(2 * w, 2), every, every, slice(width, 2 * width))
    out_piece.start()
    for w in range(4):
        in_piece(w).start()
        back_piece(w).start()
    out_piece.wait()
    cols = a0.shape[1]
    vector = lambda n: vec_ref[n : n + 1, :]
    for s in range(4):
        piece = w_ref[:, s, :, 2 * width : 2 * width + cols]
        wout[:, s * cols : (s + 1) * cols] = piece.reshape(width, cols)
    part = lambda mask: wout[pl.ds(pl.multiple_of((own ^ mask) * cols, 64), cols), :]
    masks = masks_of(place)
    total = x_ref[...].astype(F32) + vector(0)
    for mask, piece in zip(masks, (a0, a1, a2, a3)):
        total = total + jnp.dot(piece[...], part(mask), preferred_element_type=F32)
    unit, inverse_one = spread_norm(total)
    normed[...] = unit
    first = unit * vector(1) + vector(2)
    high[...] = first
    h_ref[...] = first.astype(BF)
    acc[...] = first + vector(3)

    def w_in_at(w):
        return w_ref[:, w, :, 0:width].reshape(width, width)

    def w_back_at(w):
        return w_ref[pl.ds(2 * w, 2), :, :, width : 2 * width].reshape(width, width)

    def forward(w, carry):
        at = pl.multiple_of(w * width, 128)
        in_piece(w).wait()
        z = jnp.dot(h_ref[...], w_in_at(w), preferred_element_type=F32) + bin_ref[:, pl.ds(at, width)]
        square = z * z
        bend = jnp.tanh(GELU_A * z * (1.0 + GELU_B * square))
        half = 0.5 + 0.5 * bend
        u = (z * half).astype(BF)
        u_ref[:, pl.ds(at, width)] = u
        slope[:, pl.ds(at, width)] = half + 0.5 * z * (1.0 - bend * bend) * (GELU_A * (1.0 + 3.0 * GELU_B * square))
        back_piece(w).wait()
        acc[...] += jnp.dot(u, w_back_at(w), preferred_element_type=F32)
        return carry

    lax.fori_loop(0, 4, forward, 0)
    unit, inverse_two = spread_norm(acc[...])
    act_ref[...] = (unit * vector(4) + vector(5)).astype(BF)

    def back(gradient, unit, inverse, gain):
        scaled = gradient * gain
        inner = scaled - jnp.mean(scaled, axis=1, keepdims=True)
        return (inner - unit * jnp.mean(scaled * unit, axis=1, keepdims=True)) * inverse

    def note(row, values):
        sum_ref[row : row + 1, :] = jnp.sum(values, axis=0, keepdims=True)

    gradient = go_ref[...].astype(F32)
    note(2, gradient * unit)
    note(3, gradient)
    second = back(gradient, unit, inverse_two, vector(4))
    df = second.astype(BF)
    df_ref[...] = df
    note(5, df.astype(F32))
    acc[...] = second

    def backward(w, carry):
        at = pl.multiple_of(w * width, 128)
        du = lax.dot_general(df_ref[...], w_back_at(w), (((1,), (1,)), ((), ())), preferred_element_type=F32)
        dz = (slope[:, pl.ds(at, width)] * du).astype(BF)
        dz_ref[:, pl.ds(at, width)] = dz
        sum_ref[pl.ds(8 + w, 1), :] = jnp.sum(dz.astype(F32), axis=0, keepdims=True)
        acc[...] += lax.dot_general(dz, w_in_at(w), (((1,), (1,)), ((), ())), preferred_element_type=F32)
        return carry

    lax.fori_loop(0, 4, backward, 0)
    gradient = acc[...]
    unit = normed[...]
    note(0, gradient * unit)
    note(1, gradient)
    dr = back(gradient, unit, inverse_one, vector(1))
    dr_ref[...] = dr
    dbr = dr.astype(BF)
    dbr_ref[...] = dbr
    note(4, dbr.astype(F32))
    sum_ref[6:8, :] = jnp.zeros((2, width), F32)
    sum_ref[12:16, :] = jnp.zeros((4, width), F32)
    for mask, out in zip(masks, (d0, d1, d2, d3)):
        value = lax.dot_general(dbr, part(mask), (((1,), (1,)), ((), ())), preferred_element_type=F32)
        out[...] = value.astype(BF)


def middle(place, pieces, x, out_grad, weights, vectors, bin_full):
    rows, width = x.shape
    cols = pieces[0].shape[1]
    hidden = bin_full.shape[1]
    low = lambda n: jax.ShapeDtypeStruct((rows, n), BF)
    full = lambda r, n: jax.ShapeDtypeStruct((r, n), F32)
    return pl.pallas_call(
        middle_body,
        in_specs=[SM] + [VM] * 6 + [pl.BlockSpec(memory_space=pl.ANY)] + [VM] * 2,
        out_specs=[VM] * 12,
        out_shape=[low(width), low(width), low(hidden), low(hidden), low(width), low(width), full(rows, width)]
        + [low(cols)] * 4
        + [full(16, width)],
        scratch_shapes=[
            pltpu.VMEM((width, width), BF),
            pltpu.VMEM((rows, hidden), F32),
            pltpu.VMEM((rows, width), F32),
            pltpu.VMEM((rows, width), F32),
            pltpu.VMEM((rows, width), F32),
            pltpu.VMEM(weights.shape, BF),
            pltpu.SemaphoreType.DMA((9,)),
        ],
        compiler_params=pltpu.CompilerParams(vmem_limit_bytes=34 * MIB),
        cost_estimate=pl.CostEstimate(flops=8_000_000_000, bytes_accessed=20_000_000, transcendentals=1_000_000),
        name="middle",
    )(place, *pieces, x, out_grad, weights, vectors, bin_full)


def angles_of(position, width):
    half_width = width // 2
    rate_table = 10000.0 ** (-(jnp.arange(half_width, dtype=jnp.float32) / half_width))
    turned = position.astype(jnp.float32)[:, None] * rate_table[None, :]
    return (jnp.sin(turned), jnp.cos(turned))


def contract_rows(left, right):
    return lax.dot_general(
        left, right, (((0,), (0,)), ((), ())), preferred_element_type=jnp.float32
    )


def contract_cols(left, right):
    return lax.dot_general(
        left, right, (((1,), (1,)), ((), ())), preferred_element_type=jnp.float32
    )


def across(values, other):
    seqs, fsdps = lax.axis_size("seq"), lax.axis_size("fsdp")
    pairs = []
    for s in range(seqs):
        for f in range(fsdps):
            to_s, to_f = other(s, f)
            pairs.append((s * fsdps + f, to_s * fsdps + to_f))
    return lax.ppermute(values, ("seq", "fsdp"), pairs)


def to_core(values):
    return across(values, lambda s, f: (s, f ^ 1))


def to_first(values):
    return across(values, lambda s, f: (s ^ (2 if f & 1 else 1), f))


def to_second(values):
    return across(values, lambda s, f: (s ^ (1 if f & 1 else 2), f))


def to_near(values):
    return across(values, lambda s, f: (s, f ^ 2))


def to_far(values):
    return across(values, lambda s, f: (s, f ^ 4))


def to_seq(values, k):
    return across(values, lambda s, f: (s ^ k, f))


def add_parts(parts, low, high):
    total = parts[0][low:high].astype(F32)
    for part in parts[1:]:
        total = total + part[low:high].astype(F32)
    return total


def back_blocks_body(place, u_ref, df_ref, keep_ref, send_ref):
    core = lax.rem(place[0], 2)
    group = u_ref.shape[1] // 4
    for g in range(1):
        acc = lax.dot_general(u_ref[...], df_ref[...], (((0,), (0,)), ((), ())), preferred_element_type=F32)
        at = pl.program_id(0) * 4
        for j in range(4):
            slot = place[1 + at + j]
            value = acc[j * group : (j + 1) * group].astype(BF)

            @pl.when(core == j % 2)
            def _():
                keep_ref[slot] = value

            @pl.when(core != j % 2)
            def _():
                send_ref[slot] = value


def back_blocks(place, u, df):
    rows, hidden = u.shape
    width = df.shape[1]
    out = jax.ShapeDtypeStruct((16, hidden // 32, width), BF)
    return pl.pallas_call(
        back_blocks_body,
        grid=(8,),
        in_specs=[SM, pl.BlockSpec((rows, hidden // 8), lambda g: (0, g)), pl.BlockSpec((rows, width), lambda g: (0, 0))],
        out_specs=[pl.BlockSpec((16, hidden // 32, width), lambda g: (0, 0, 0))] * 2,
        out_shape=[out, out],
        compiler_params=pltpu.CompilerParams(vmem_limit_bytes=16 * MIB, dimension_semantics=("arbitrary",)),
        cost_estimate=pl.CostEstimate(flops=2 * rows * hidden * width, bytes_accessed=8_000_000, transcendentals=0),
        name="back_blocks",
    )(place, u, df)


def in_blocks_body(place, h_ref, dz_ref, a0, a1, a2, a3, db_ref, sum_ref, keep_ref, send_ref):
    even = lax.rem(place[0], 2) == 0
    core = lax.rem(place[0], 2)
    own = lax.div(place[0], 8)
    step = pl.program_id(0)

    def store(block, low, a, b):
        count = a.shape[0]
        keep_ref[place[1 + block + core], pl.ds(low, count), :] = jnp.where(even, a, b).astype(BF)
        send_ref[place[2 + block - core], pl.ds(low, count), :] = jnp.where(even, b, a).astype(BF)

    def put(block, low, acc):
        store(block, low, acc[0:24], acc[24:48])

    def chunk(which):
        for g in range(2):
            acc = lax.dot_general(
                h_ref[:, g * 384 : (g + 1) * 384], dz_ref[...], (((0,), (0,)), ((), ())), preferred_element_type=F32
            )
            for j in range(0, 16, 2):
                put(g * 16 + j, which * 24, acc[j * 24 : (j + 2) * 24])

    for which in range(4):
        pl.when(step == which)(lambda which=which: chunk(which))

    @pl.when(step == 4)
    def _():
        for mask, piece in zip((0, place[33], place[34], 3), (a0, a1, a2, a3)):
            acc = lax.dot_general(piece[...], db_ref[...], (((0,), (0,)), ((), ())), preferred_element_type=F32)
            for j in range(0, 8, 2):
                put((own ^ mask) * 8 + j, 96, acc[j * 24 : (j + 2) * 24])
        width = sum_ref.shape[1]
        line = lax.broadcasted_iota(jnp.int32, (8, width), 0)

        def note(j):
            wide = sum_ref[8 + j // 8 : 9 + j // 8, :] + jnp.zeros((8, width), F32)
            short, wide = (
                pltpu.roll(v, shift, 1) if shift % width else v
                for v, shift in ((sum_ref[0:8, :], width - 24 * j), (wide, width - 96 * (j % 8)))
            )
            return jnp.where(line == 6, wide, short)

        for j in range(0, 32, 2):
            store(j, 120, note(j), note(j + 1))


def in_blocks(place, hidden_low, dz, attn, dbr, sums):
    rows, width = hidden_low.shape
    chunks = dz.shape[1] // width
    out = jax.ShapeDtypeStruct((16, 128, width), BF)
    whole = pl.BlockSpec((rows, width), lambda g: (0, 0))
    return pl.pallas_call(
        in_blocks_body,
        grid=(chunks + 1,),
        in_specs=[SM, whole, pl.BlockSpec((rows, width), lambda g: (0, jnp.minimum(g, chunks - 1)))]
        + [pl.BlockSpec(attn[0].shape, lambda g: (0, 0))] * 4
        + [whole]
        + [pl.BlockSpec(sums.shape, lambda g: (0, 0))],
        out_specs=[pl.BlockSpec((16, 128, width), lambda g: (0, 0, 0))] * 2,
        out_shape=[out, out],
        compiler_params=pltpu.CompilerParams(vmem_limit_bytes=18 * MIB, dimension_semantics=("arbitrary",)),
        cost_estimate=pl.CostEstimate(flops=2 * rows * width * (dz.shape[1] + width), bytes_accessed=12_000_000, transcendentals=0),
        name="in_blocks",
    )(place, hidden_low, dz, *attn, dbr, sums)


def shards(
    inputs,
    w_query,
    w_key,
    w_value,
    b_value,
    w_out,
    b_out,
    norm1_gain,
    norm1_bias,
    w_in,
    b_in,
    w_back,
    b_back,
    norm2_gain,
    norm2_bias,
    w_relative,
    bias_content,
    bias_position,
    bias_type,
    type_embed,
    lengths,
    token_types,
    owners,
    grad_output,
):
    seqs, fsdps = lax.axis_size("seq"), lax.axis_size("fsdp")
    direct = seqs == 4 and fsdps == 8
    own, rank = lax.axis_index("seq"), lax.axis_index("fsdp")
    pack_count = owners.shape[0]
    sliver_rows = inputs.shape[1]
    width = inputs.shape[2]
    local_rows = w_query.shape[0]
    local_cols = width // seqs
    local_heads = w_relative.shape[1]
    scale = DH ** -0.5
    dealt = reload(owners, inputs, True)
    mine = lax.all_to_all(dealt, "fsdp", split_axis=0, concat_axis=1, tiled=True)[0]
    row_count = mine.shape[0]
    chosen = (owners == rank).astype(jnp.int32)
    pack_types = jnp.sum(chosen[:, None] * token_types, axis=0)
    pack_sizes = jnp.sum(chosen[:, None] * lengths, axis=0)
    pack_rows = pack_types.shape[0]

    def head_columns(weight):
        return lax.dynamic_slice_in_dim(weight, own * local_cols, local_cols, 1)

    block = jnp.concatenate(
        [head_columns(w) for w in (w_query, w_key, w_value)] + [w_relative.reshape(local_rows, local_cols)], axis=1
    )
    long_vectors = (b_value, b_out, norm1_gain, norm1_bias, b_back, norm2_gain, norm2_bias, b_in)
    head_vectors = (bias_content, bias_position, bias_type, type_embed[0], type_embed[1])

    def placed_at(value, row, lane):
        value = value.reshape(-1, value.shape[-1])
        return jnp.pad(value, ((row, 8 - row - value.shape[0]), (lane, width - lane - value.shape[1])))

    corner = placed_at(b_value, 0, 0)
    for number, value in enumerate(long_vectors[1:]):
        corner = corner + placed_at(value, number + 1, 0)
    for number, value in enumerate(head_vectors[:3]):
        corner = corner + placed_at(value, 0, (number + 3) * 128)
    for number, value in enumerate(head_vectors[3:]):
        corner = corner + placed_at(value, 3, (number + 3) * 128)
    early = lax.all_gather(jnp.concatenate([block, corner], axis=0), "fsdp", axis=0)
    qkvr = early[:, :local_rows].reshape(width, width)
    corners = early[:, local_rows:].astype(F32)
    full = [corners[:, n, : v.shape[0]].reshape(-1) for n, v in enumerate(long_vectors)]
    bv_full, bo_full, gain_one, shift_one, bback_full, gain_two, shift_two, bin_full = full
    heads = []
    for number, value in enumerate(head_vectors):
        row = 0 if number < 3 else 3
        lane = (number % 3 + 3) * 128
        each = corners[:, row : row + local_heads, lane : lane + value.shape[1]]
        heads.append(jnp.moveaxis(each, 0, 1).reshape(local_heads, DH))
    content_full, position_full, typebias_full, embed_zero, embed_one = heads
    bv_own = lax.dynamic_slice_in_dim(bv_full, own * local_cols, local_cols, 0)
    head = jnp.stack(
        [
            content_full,
            position_full,
            typebias_full,
            embed_zero,
            embed_one,
            bv_own.reshape(local_heads, DH),
        ],
        axis=1,
    )
    head = jnp.pad(head, ((0, 0), (0, 2), (0, 64)))

    deep = w_back.shape[0] // seqs
    late = jnp.concatenate(
        [
            lax.dynamic_slice_in_dim(w_in, own * width, width, 1),
            lax.dynamic_slice_in_dim(w_back, own * deep, deep, 0),
            head_columns(w_out),
            jnp.zeros((local_rows, 64), BF),
        ],
        axis=1,
    )
    late = lax.all_gather(late, ("fsdp", "seq"), axis=0).reshape(fsdps, seqs, local_rows, -1)
    if not direct:
        eighth_rows = width // 8
        turned_in = jnp.swapaxes(late, 1, 2).reshape(8, eighth_rows, seqs, -1)
        natural = late[..., width : 2 * width].reshape(8, seqs, eighth_rows, width)
        turned_in = jnp.swapaxes(turned_in, 1, 2)
        late = jnp.concatenate([turned_in[..., :width], natural, turned_in[..., 2 * width :]], axis=-1)

    longest = jnp.argmax(pack_sizes).astype(jnp.int32)
    start = jnp.sum(jnp.where(jnp.arange(3) < longest, pack_sizes, 0))
    near = jnp.sum(jnp.where(jnp.arange(3) == (longest + 1) % 3, pack_sizes, 0))
    parity = rank & 1
    place = jnp.stack([own, start, near, 1 + parity, 2 - parity]).astype(jnp.int32)
    row_index = jnp.arange(pack_rows, dtype=jnp.int32)
    position = jnp.where(
        row_index < LONGEST,
        row_index,
        jnp.where(row_index < LONGEST + near, row_index - LONGEST, row_index - LONGEST - near),
    )
    sine, cosine = angles_of(position, width)
    key_pos = jnp.concatenate([cosine, sine], axis=-1).astype(BF)
    key_pos_t = key_pos.T
    turned_types = lax.dynamic_slice_in_dim(
        jnp.concatenate([pack_types, pack_types]), start, pack_rows, 0
    )[:, None]
    wrel = qkvr[:, 3 * local_cols :].reshape(width, local_heads, DH)
    wrel_rows = jnp.pad(jnp.transpose(wrel, (1, 0, 2)), ((0, 0), (0, 0), (0, 64)))
    wrel_cols = jnp.pad(jnp.transpose(wrel, (1, 2, 0)), ((0, 0), (0, 64), (0, 0)))
    together = lambda n: qkvr[:, n * local_cols : (n + 1) * local_cols].reshape(width, local_heads, DH)
    paired = jnp.concatenate([together(0), together(1)], axis=2).reshape(width, 2 * local_cols)
    w_qkv = jnp.concatenate([paired, qkvr[:, 2 * local_cols : 3 * local_cols], jnp.zeros((width, 64), BF)], axis=1)

    pieces = [mine, to_first(mine), to_second(mine)]
    pieces.append(to_second(pieces[1]))
    pieces, wrel_rows = lax.optimization_barrier((pieces, wrel_rows))
    qx, pq, kx, kxt, vx, vxt = project(place, pieces, w_qkv, head, turned_types)
    big, small, ox, *head_out = attend(place, qx, pq, kxt, vx, key_pos_t, wrel_cols, sine, cosine)
    order = own ^ jnp.arange(seqs, dtype=jnp.int32)
    deal = lambda v: [v[0], to_first(v[1]), to_second(v[2]), to_seq(v[3], 3)]
    attn = deal(head_out)
    mid_vectors = jnp.stack([bo_full, gain_one, shift_one, bback_full, gain_two, shift_two, gain_two, gain_two])
    result, hidden_low, act_low, pre_grad, ffn_grad, branch_grad, sum_one_grad, *douts, short_sums = middle(
        place, attn, mine, grad_output[0], late, mid_vectors, bin_full[None]
    )
    activations = result.reshape(1, row_count, width)
    douts = deal(douts)
    devices = seqs * fsdps
    device = own * fsdps + rank
    fine = width // devices
    deep = act_low.shape[1] // devices
    kept_place = jnp.where((order == 1) | (order == 2), jnp.where(parity == 1, 3 - order, order), order)
    if direct:
        relative = jnp.arange(32, dtype=jnp.int32) ^ device
        bit = lambda n: (relative >> n) & 1
        flip = (bit(0) ^ parity) == 1
        one, two = jnp.where(flip, bit(4), bit(3)), jnp.where(flip, bit(3), bit(4))
        me, masks = device[None], place[3:5]
        in_table = jnp.concatenate([me, one * 8 + two * 4 + bit(1) * 2 + bit(2), masks]).astype(jnp.int32)
        back_table = jnp.concatenate([me, bit(1) * 8 + one * 4 + two * 2 + bit(2), masks]).astype(jnp.int32)
        kept, sent = in_blocks(in_table, hidden_low, pre_grad, attn, branch_grad, short_sums)
        ins = [kept, to_core(sent)]
        kept, sent = back_blocks(back_table, act_low, ffn_grad)
        backs = [kept, to_core(sent)]
        back_out, in_out = merge(backs, ins, 8)
        qx, back_out, in_out = lax.optimization_barrier((qx, back_out, in_out))
        backs.append(to_near(back_out))
        ins.append(to_first(in_out))
    else:
        scatter = lambda v: lax.psum_scatter(v, ("seq", "fsdp"), scatter_dimension=0, tiled=True)
        w_back_grad = scatter(contract_rows(act_low, ffn_grad))
        w_in_grad = scatter(contract_rows(hidden_low, pre_grad))
        spun = contract_rows(jnp.concatenate(attn, axis=1), branch_grad).reshape(seqs, local_cols, width)
        w_out_grad = scatter(jnp.take(spun, kept_place, axis=0).reshape(width, width))

    tkeep, tsend, rel, sums = attend_back(
        place, douts, big, small, ox, qx, pq, kx, vxt, key_pos, wrel_rows, sine, cosine, turned_types, head
    )
    if direct:
        bundle = qkv_blocks(fsdps, pieces, tkeep, tsend, rel, sums)
    else:
        grad = contract_rows(pieces[0], tkeep[:row_count]) + contract_rows(pieces[2], tkeep[row_count:])
        grad = grad + contract_rows(pieces[1], tsend[:row_count]) + contract_rows(pieces[3], tsend[row_count:])
        grad = jnp.swapaxes(grad.reshape(seqs, fsdps, fine, 640), 0, 1).reshape(fsdps, local_rows, 640)
        tall = rel.reshape(fsdps, local_rows, 256)
        bundle = jnp.concatenate([grad[..., :512], grad[..., 512:] + tall[..., :128], tall[..., 128:]], axis=2)
        notes = jnp.concatenate([sums[0], sums[1], sums[2], jnp.zeros((8, 384), F32)], axis=1)
        bundle = jnp.concatenate([bundle, jnp.broadcast_to(notes[None], (fsdps,) + notes.shape)], axis=1).astype(BF)
    total = lax.psum_scatter(bundle, "fsdp", scatter_dimension=0, tiled=True)[0].astype(F32)
    dx_send = contract_cols(tsend, w_qkv).astype(BF)
    if direct:
        dx_send, backs, ins, bundle = lax.optimization_barrier((dx_send, backs, ins, bundle))
        back_out, in_out = merge(backs, ins, 4)
        backs.append(to_first(back_out))
        ins.append(to_second(in_out))
    dx_first = to_first(dx_send)
    dx_keep = contract_cols(tkeep, w_qkv)
    if direct:
        dx_first, backs, ins = lax.optimization_barrier((dx_first, backs, ins))
    dx_out = (dx_keep[row_count:] + dx_first[row_count:].astype(F32)).astype(BF)
    dx_second = to_second(dx_out)
    if direct:
        back_out, in_out = merge(backs, ins, 2)
        backs.append(to_second(back_out))
        ins.append(to_near(in_out))
        dx_second, backs, ins = lax.optimization_barrier((dx_second, backs, ins))
    input_rows = sum_one_grad + dx_keep[:row_count] + dx_first[:row_count].astype(F32) + dx_second.astype(F32)
    input_rows = input_rows.astype(BF).reshape(fsdps, sliver_rows, width)
    returned = lax.all_to_all(input_rows, "fsdp", split_axis=0, concat_axis=0, tiled=True)
    input_grad = reload(owners, returned, False)
    if direct:
        far_out, total = lax.optimization_barrier((merge(backs, ins, 1, False)[0], total))
        far = to_far(far_out)
        cut = kept.shape[1]
    if not direct:
        short_sums = lax.psum(short_sums, ("seq", "fsdp"))
        short_grads = lax.dynamic_slice(short_sums, (0, device * fine), (8, fine))
        in_bias_grad = lax.dynamic_slice(short_sums, (8 + device * deep // width, device * deep % width), (1, deep))[0]
    own_qkv = total[:local_rows].astype(BF).reshape(seqs, fine, width)
    block_for = lambda mask: lax.dynamic_index_in_dim(own_qkv, own ^ mask, 0, keepdims=True)
    swapped = jnp.concatenate(deal([block_for(m) for m in (0, place[3], place[4], 3)]), axis=0)
    swapped = jnp.take(swapped, kept_place, axis=0).astype(F32)
    both = swapped[:, :, : 2 * local_cols].reshape(seqs, fine, local_heads, 2, DH)
    both = jnp.transpose(both, (3, 1, 0, 2, 4)).reshape(2, fine, width)
    w_value_grad = jnp.transpose(swapped[:, :, 2 * local_cols : 3 * local_cols], (1, 0, 2)).reshape(fine, width)
    if direct:
        _, _, far, _ = lax.optimization_barrier((both, w_value_grad, far, input_grad))
        w_back_grad = add_parts(backs + [far[:, :cut]], 0, 1)[0]
        in_total = add_parts(ins + [far[:, cut:]], 0, 1)[0]
        w_in_grad = jnp.concatenate([in_total[c * 24 : (c + 1) * 24] for c in range(4)], axis=1)
        w_out_grad = in_total[96:120]
        short_grads, in_bias_grad = in_total[120:128, :fine], in_total[126, :deep]
    rel_total = total[:local_rows, 3 * local_cols :].reshape(local_rows, local_heads, DH)
    notes = total[local_rows:, :384].reshape(8, 3, 128)
    eighth = DH // fsdps
    mine_sums = lax.dynamic_slice(notes, (0, 0, rank * eighth), (8, 3, eighth))
    value_bias_grad = lax.dynamic_slice(notes[5, :, :DH].reshape(-1), (rank * fine,), (fine,))
    return (
        activations,
        input_grad,
        both[0],
        both[1],
        w_value_grad,
        value_bias_grad,
        w_out_grad,
        short_grads[4],
        short_grads[0],
        short_grads[1],
        w_in_grad,
        in_bias_grad,
        w_back_grad,
        short_grads[5],
        short_grads[2],
        short_grads[3],
        rel_total,
        mine_sums[0],
        mine_sums[1],
        mine_sums[2],
        mine_sums[3:5],
    )


def solution(mesh):
    placed = (
        P(None, ("seq", "fsdp"), None),
        P("fsdp", None),
        P("fsdp", None),
        P("fsdp", None),
        P("fsdp"),
        P("fsdp", None),
        P("fsdp"),
        P("fsdp"),
        P("fsdp"),
        P("fsdp", None),
        P("fsdp"),
        P("fsdp", None),
        P("fsdp"),
        P("fsdp"),
        P("fsdp"),
        P("fsdp", "seq", None),
        P("seq", "fsdp"),
        P("seq", "fsdp"),
        P("seq", "fsdp"),
        P(None, "seq", "fsdp"),
        P(),
        P(),
        P(),
        P("fsdp", "seq", None),
    )
    return jax.shard_map(
        shards,
        mesh=mesh,
        in_specs=placed,
        out_specs=(
            P("fsdp", "seq", None),
            P(None, ("seq", "fsdp"), None),
            P(("seq", "fsdp"), None),
            P(("seq", "fsdp"), None),
            P(("seq", "fsdp"), None),
            P(("seq", "fsdp")),
            P(("seq", "fsdp"), None),
            P(("seq", "fsdp")),
            P(("seq", "fsdp")),
            P(("seq", "fsdp")),
            P(("seq", "fsdp"), None),
            P(("seq", "fsdp")),
            P(("seq", "fsdp"), None),
            P(("seq", "fsdp")),
            P(("seq", "fsdp")),
            P(("seq", "fsdp")),
            P("fsdp", "seq", None),
            P("seq", "fsdp"),
            P("seq", "fsdp"),
            P("seq", "fsdp"),
            P(None, "seq", "fsdp"),
        ),
        check_vma=False,
    )
```

```python
import functools

import jax
import jax.numpy as jnp
from jax import lax
from jax.experimental import pallas as pl
from jax.experimental.pallas import tpu as pltpu
from jax.sharding import PartitionSpec as P

DH = 64
LONGEST = 1024
QB = 256
BLOCKED = -1e30
BF = jnp.bfloat16
F32 = jnp.float32
VM = pl.BlockSpec(memory_space=pltpu.VMEM)
SM = pl.BlockSpec(memory_space=pltpu.SMEM)
MIB = 1024 * 1024


def lanes_of(rows, width=128):
    return lax.broadcasted_iota(jnp.int32, (rows, width), 1)


def split3(value):
    high = value.astype(BF).astype(F32)
    rest = value - high
    middle = rest.astype(BF).astype(F32)
    return high, middle, rest - middle


def masks_of(place):
    return 0, place[3], place[4], 3


def pick(lane, first, columns, base):
    for number, column in enumerate(columns):
        base = jnp.where(lane == first + number, column, base)
    return base


def project_body(place, x0, x1, x2, x3, w_ref, head_ref, tcol_ref, qx_ref, pq_ref, kx_ref, kxt_ref, vx_ref, vxt_ref, rolled):
    own, start, near = place[0], place[1], place[2]
    scale = DH ** -0.5
    rows = qx_ref.shape[1]
    part = x0.shape[0]
    for mask, piece in zip(masks_of(place), (x0, x1, x2, x3)):
        y = jnp.dot(piece[...], w_ref[...], preferred_element_type=F32)
        base = pl.multiple_of((own ^ mask) * part, 8)
        for c in range(5):
            column = y[:, c * 128 : (c + 1) * 128]
            rolled[c, pl.ds(base, part), :] = column
            rolled[c, pl.ds(pl.multiple_of(base + rows, 8), part), :] = column

    def block(r, carry):
        row = pl.multiple_of(r * QB, QB)
        lane = lanes_of(QB)
        kind = tcol_ref[pl.ds(row, QB), :]
        index = row + lax.broadcasted_iota(jnp.int32, (QB, 1), 0)
        small = index >= LONGEST
        first = jnp.where(small & (index < LONGEST + near), 1.0, 0.0)
        second = jnp.where(small & (index >= LONGEST + near), 1.0, 0.0)
        one = jnp.where(kind == 1, 1.0, 0.0)
        zero = 1.0 - one
        for h in range(3):
            both = rolled[h, pl.ds(start + row, QB), :].astype(BF).astype(F32)
            if h < 2:
                v = rolled[3, pl.ds(start + row, QB), :]
                v = v if h == 0 else pltpu.roll(v, 64, 1)
            else:
                v = rolled[4, pl.ds(start + row, QB), :]
            head = head_ref[h]
            content = (both + head[0:1]) * scale
            position = ((both + head[1:2]) * scale).astype(BF)
            typed = (both + head[2:3]) * scale
            differ = jnp.sum(typed * head[3:4], axis=1, keepdims=True)
            same = jnp.sum(typed * head[4:5], axis=1, keepdims=True)
            for_zero = jnp.where(kind == 1, differ, same)
            for_one = jnp.where(kind == 1, same, differ)
            columns = [*split3(for_zero), *split3(for_one), second * BLOCKED, first * BLOCKED]
            qx = pick(lane, 64, columns, jnp.where(lane < 64, content, 0.0)).astype(BF)
            qx_ref[h, pl.ds(row, QB), :] = qx
            raw = pltpu.roll(both, 64, 1)
            pq_ref[h, pl.ds(row, QB), :] = jnp.where(lane < 64, position.astype(F32), raw).astype(BF)
            kx = pick(lane, 64, [zero, zero, zero, one, one, one, first, second], jnp.where(lane < 64, raw, 0.0))
            kx_ref[h, pl.ds(row, QB), :] = kx.astype(BF)
            kxt_ref[h, :, pl.ds(row, QB)] = jnp.transpose(kx, (1, 0)).astype(BF)
            vx = jnp.where(lane < 64, v + head[5:6], jnp.where(lane < 67, 1.0, 0.0)).astype(BF)
            vx_ref[h, pl.ds(row, QB), :] = vx
            vxt_ref[h, :, pl.ds(row, QB)] = jnp.transpose(vx.astype(F32), (1, 0)).astype(BF)
        return carry

    lax.fori_loop(0, rows // QB, block, 0)


def project(place, pieces, w_qkv, head, tcol):
    rows = 4 * pieces[0].shape[0]
    tall = jax.ShapeDtypeStruct((3, rows, 128), BF)
    wide = jax.ShapeDtypeStruct((3, 128, rows), BF)
    return pl.pallas_call(
        project_body,
        in_specs=[SM] + [VM] * 7,
        out_specs=[VM] * 6,
        out_shape=[tall, tall, tall, wide, tall, wide],
        scratch_shapes=[pltpu.VMEM((5, 2 * rows, 128), F32)],
        compiler_params=pltpu.CompilerParams(vmem_limit_bytes=26 * MIB),
        cost_estimate=pl.CostEstimate(flops=2 * rows * 768 * 640, bytes_accessed=10_000_000, transcendentals=0),
        name="project",
    )(place, *pieces, w_qkv, head, tcol)


def attend_body(place, qx_ref, pq_ref, kxt_ref, vx_ref, kpt_ref, wrt_ref, sn_ref, cs_ref, big_ref, small_ref, ox_ref, o0, o1, o2, o3, keys, left, outs):
    h, i = pl.program_id(0), pl.program_id(1)
    own, start = place[0], place[1]
    width = kpt_ref.shape[0]
    half = width // 2
    rows = kpt_ref.shape[1]

    @pl.when((h == 0) & (i == 0))
    def _():
        keys[0:width, :] = kpt_ref[...]

    @pl.when(i == 0)
    def _():
        keys[width:, :] = kxt_ref[0]

    rel = jnp.dot(pq_ref[0], wrt_ref[0], preferred_element_type=F32)
    r1, r2 = rel[:, :half], rel[:, half:]
    sn, cs = sn_ref[...], cs_ref[...]
    left[:, 0:half] = (r1 * sn + r2 * cs).astype(BF)
    left[:, half:width] = (r2 * sn - r1 * cs).astype(BF)
    left[:, width:] = qx_ref[0]

    def attend(low, high, store):
        score = jnp.dot(left[...], keys[:, low:high], preferred_element_type=F32)
        top = jnp.max(score, axis=1, keepdims=True)
        raised = jnp.exp(score - top).astype(BF)
        store[0] = raised
        mixed = jnp.dot(raised, vx_ref[0, low:high, :], preferred_element_type=F32)
        inverse = 1.0 / mixed[:, 64:65]
        lane = lanes_of(QB)
        ox = jnp.where(lane < 64, mixed * inverse, jnp.where(lane == 64, inverse, 0.0))
        ox_ref[0] = ox
        row = pl.multiple_of(i * QB, QB)
        outs[h, pl.ds(row, QB), :] = ox
        outs[h, pl.ds(pl.multiple_of(row + rows, QB), QB), :] = ox

    @pl.when(i < LONGEST // QB)
    def _():
        attend(0, LONGEST, big_ref)

    @pl.when(i >= LONGEST // QB)
    def _():
        attend(LONGEST, rows, small_ref)

    @pl.when((h == 2) & (i == pl.num_programs(1) - 1))
    def _():
        part = o0.shape[0]
        for mask, out in zip(masks_of(place), (o0, o1, o2, o3)):
            at = lax.rem((own ^ mask) * part + rows - start, rows)
            out[...] = jnp.concatenate([outs[g, pl.ds(at, part), :][:, 0:64] for g in range(3)], axis=1).astype(BF)


def attend(place, qx, pq, kxt, vx, kpt, wrt, sn, cs):
    rows = qx.shape[1]
    width = kpt.shape[0]
    blocks = rows // QB
    bigs = LONGEST // QB
    rest = rows - LONGEST
    per_block = lambda h, i: (h, i, 0)
    per_head = lambda h, i: (h, 0, 0)
    whole2 = lambda h, i: (0, 0)
    part = rows // 4
    out_piece = jax.ShapeDtypeStruct((part, 192), BF)
    return pl.pallas_call(
        attend_body,
        grid=(3, blocks),
        in_specs=[
            SM,
            pl.BlockSpec((1, QB, 128), per_block),
            pl.BlockSpec((1, QB, 128), per_block),
            pl.BlockSpec((1, 128, rows), per_head),
            pl.BlockSpec((1, rows, 128), per_head),
            pl.BlockSpec((width, rows), whole2, pipeline_mode=pl.Buffered(1)),
            pl.BlockSpec((1, 128, width), per_head),
            pl.BlockSpec((QB, width // 2), lambda h, i: (i, 0)),
            pl.BlockSpec((QB, width // 2), lambda h, i: (i, 0)),
        ],
        out_specs=[
            pl.BlockSpec((1, QB, LONGEST), lambda h, i: (h, jnp.minimum(i, bigs - 1), 0)),
            pl.BlockSpec((1, QB, rest), lambda h, i: (h, jnp.maximum(i - bigs, 0), 0)),
            pl.BlockSpec((1, QB, 128), per_block),
        ]
        + [pl.BlockSpec((part, 192), whole2)] * 4,
        out_shape=[
            jax.ShapeDtypeStruct((3, LONGEST, LONGEST), BF),
            jax.ShapeDtypeStruct((3, rest, rest), BF),
            jax.ShapeDtypeStruct((3, rows, 128), F32),
        ]
        + [out_piece] * 4,
        scratch_shapes=[
            pltpu.VMEM((width + 128, rows), BF),
            pltpu.VMEM((QB, width + 128), BF),
            pltpu.VMEM((3, 2 * rows, 128), F32),
        ],
        compiler_params=pltpu.CompilerParams(vmem_limit_bytes=26 * MIB, dimension_semantics=("arbitrary", "arbitrary")),
        cost_estimate=pl.CostEstimate(flops=12_000_000_000, bytes_accessed=20_000_000, transcendentals=4_000_000),
        name="attend",
    )(place, qx, pq, kxt, vx, kpt, wrt, sn, cs)


def back_body(place, d0, d1, d2, d3, big_ref, small_ref, ox_ref, qx_ref, pq_ref, kx_ref, vxt_ref, kp_ref, wr_ref, sn_ref, cs_ref, tcol_ref, head_ref, gkeep_ref, gsend_ref, rel_ref, sum_ref, douts, dkt, dvt, gwt, grads):
    h, i = pl.program_id(0), pl.program_id(1)
    own, start = place[0], place[1]
    rows, width = kp_ref.shape
    half = width // 2
    scale = DH ** -0.5
    part = d0.shape[0]
    last = pl.num_programs(1) - 1
    row = pl.multiple_of(i * QB, QB)
    again = pl.multiple_of(row + rows, QB)

    @pl.when((h == 0) & (i == 0))
    def _():
        blank = jnp.zeros((part, 64), F32)
        for mask, piece in zip(masks_of(place), (d0, d1, d2, d3)):
            values = piece[...].astype(F32)
            base = pl.multiple_of((own ^ mask) * part, 8)
            for g in range(3):
                padded = jnp.concatenate([values[:, g * 64 : (g + 1) * 64], blank], axis=1)
                douts[g, pl.ds(base, part), :] = padded
                douts[g, pl.ds(pl.multiple_of(base + rows, 8), part), :] = padded

    @pl.when(i == 0)
    def _():
        dkt[...] = jnp.zeros_like(dkt)
        dvt[...] = jnp.zeros_like(dvt)
        gwt[...] = jnp.zeros_like(gwt)
        sum_ref[...] = jnp.zeros_like(sum_ref)

    lane = lanes_of(QB)
    dout = douts[h, pl.ds(start + row, QB), :]
    ox = ox_ref[0]
    inverse = ox[:, 64:65]
    dot_row = jnp.sum(dout * ox, axis=1, keepdims=True)
    dox = pick(lane, 64, [-x for x in split3(dot_row)], dout).astype(BF)
    dout_t = jnp.transpose(dout * inverse, (1, 0))[0:64].astype(BF)
    qx = qx_ref[0]
    qc_t = jnp.transpose(qx.astype(F32), (1, 0))[0:64].astype(BF)
    pq = pq_ref[0].astype(F32)
    qp_t = jnp.transpose(pq, (1, 0))[0:64].astype(BF)
    sn, cs = sn_ref[...], cs_ref[...]

    def back(low, high, saved):
        raised = saved[0]
        dprob = jnp.dot(dox, vxt_ref[0, :, low:high], preferred_element_type=F32)
        dscore = (raised.astype(F32) * (dprob * inverse)).astype(BF)
        dvt[:, low:high] += jnp.dot(dout_t, raised, preferred_element_type=F32)
        dkt[:, low:high] += jnp.dot(qc_t, dscore, preferred_element_type=F32)
        da = jnp.dot(dscore, kp_ref[low:high, :], preferred_element_type=F32)
        dqx = jnp.dot(dscore, kx_ref[0, low:high, :], preferred_element_type=F32)
        da1, da2 = da[:, 0:half], da[:, half:width]
        drel = jnp.concatenate([(da1 * sn - da2 * cs).astype(BF), (da1 * cs + da2 * sn).astype(BF)], axis=1)
        dqp = jnp.dot(drel, wr_ref[0], preferred_element_type=F32)
        gwt[...] += jnp.dot(qp_t, drel, preferred_element_type=F32)
        kind = tcol_ref[...]
        over_zero, over_one = dqx[:, 64:65], dqx[:, 67:68]
        same = jnp.where(kind == 1, over_one, over_zero)
        differ = jnp.where(kind == 1, over_zero, over_one)
        head = head_ref[0]
        dqt = differ * head[3:4] + same * head[4:5]
        dqc = jnp.where(lane < 64, dqx, 0.0)
        dq = (dqc + dqp + dqt) * scale
        grads[h, pl.ds(row, QB), :] = dq
        typed = (pltpu.roll(pq, 64, 1) + head[2:3]) * scale
        sums = [dqc * scale, dqp * scale, dqt * scale, differ * typed, same * typed]
        for number, values in enumerate(sums):
            sum_ref[0, number : number + 1, :] += jnp.sum(values, axis=0, keepdims=True)

    @pl.when(i < LONGEST // QB)
    def _():
        back(0, LONGEST, big_ref)

    @pl.when(i >= LONGEST // QB)
    def _():
        back(LONGEST, rows, small_ref)

    @pl.when(i == last)
    def _():
        dk = jnp.transpose(dkt[...], (1, 0))
        dq = grads[h, 0:rows, :]
        pair = jnp.concatenate([dq[:, 0:64], dk], axis=1)
        grads[h, 0:rows, :] = pair
        grads[h, rows : 2 * rows, :] = pair
        dv = jnp.transpose(dvt[...], (1, 0)).astype(BF).astype(F32)
        sum_ref[0, 5:6, 0:64] = jnp.sum(dv, axis=0, keepdims=True)
        blank = jnp.zeros_like(dv)
        rel = jnp.transpose(gwt[...], (1, 0))
        empty = jnp.zeros_like(rel)

        @pl.when(h == 0)
        def _():
            padded = jnp.concatenate([dv, blank], axis=1)
            grads[3, 0:rows, :] = padded
            grads[3, rows : 2 * rows, :] = padded
            rel_ref[:, 0:128] = jnp.concatenate([empty, rel], axis=1)

        @pl.when(h == 1)
        def _():
            rel_ref[:, 128:256] = jnp.concatenate([rel, empty], axis=1)
            padded = grads[3, 0:rows, :] + jnp.concatenate([blank, dv], axis=1)
            grads[3, 0:rows, :] = padded
            grads[3, rows : 2 * rows, :] = padded

        @pl.when(h == 2)
        def _():
            padded = jnp.concatenate([dv, blank], axis=1)
            grads[4, 0:rows, :] = padded
            grads[4, rows : 2 * rows, :] = padded
            rel_ref[:, 128:256] += jnp.concatenate([empty, rel], axis=1)
            spots = ((gkeep_ref, 0), (gsend_ref, 0), (gkeep_ref, part), (gsend_ref, part))
            for mask, (out, low) in zip(masks_of(place), spots):
                at = lax.rem((own ^ mask) * part + rows - start, rows)
                for c in range(5):
                    out[low : low + part, c * 128 : (c + 1) * 128] = grads[c, pl.ds(at, part), :].astype(BF)


def attend_back(place, douts, big, small, ox, qx, pq, kx, vxt, kp, wr, sn, cs, tcol, head):
    rows, width = kp.shape
    blocks = rows // QB
    bigs = LONGEST // QB
    rest = rows - LONGEST
    part = rows // 4
    per_block = lambda h, i: (h, i, 0)
    per_head = lambda h, i: (h, 0, 0)
    whole2 = lambda h, i: (0, 0)
    return pl.pallas_call(
        back_body,
        grid=(3, blocks),
        in_specs=[SM]
        + [pl.BlockSpec((part, 192), whole2)] * 4
        + [
            pl.BlockSpec((1, QB, LONGEST), lambda h, i: (h, jnp.minimum(i, bigs - 1), 0)),
            pl.BlockSpec((1, QB, rest), lambda h, i: (h, jnp.maximum(i - bigs, 0), 0)),
            pl.BlockSpec((1, QB, 128), per_block),
            pl.BlockSpec((1, QB, 128), per_block),
            pl.BlockSpec((1, QB, 128), per_block),
            pl.BlockSpec((1, rows, 128), per_head),
            pl.BlockSpec((1, 128, rows), per_head),
            pl.BlockSpec((rows, width), whole2, pipeline_mode=pl.Buffered(1)),
            pl.BlockSpec((1, width, 128), per_head),
            pl.BlockSpec((QB, width // 2), lambda h, i: (i, 0)),
            pl.BlockSpec((QB, width // 2), lambda h, i: (i, 0)),
            pl.BlockSpec((QB, 1), lambda h, i: (i, 0)),
            pl.BlockSpec((1, 8, 128), per_head),
        ],
        out_specs=[pl.BlockSpec((2 * part, 640), whole2)] * 2
        + [pl.BlockSpec((width, 256), whole2), pl.BlockSpec((1, 8, 128), per_head)],
        out_shape=[jax.ShapeDtypeStruct((2 * part, 640), BF)] * 2
        + [jax.ShapeDtypeStruct((width, 256), F32), jax.ShapeDtypeStruct((3, 8, 128), F32)],
        scratch_shapes=[
            pltpu.VMEM((3, 2 * rows, 128), F32),
            pltpu.VMEM((64, rows), F32),
            pltpu.VMEM((64, rows), F32),
            pltpu.VMEM((64, width), F32),
            pltpu.VMEM((5, 2 * rows, 128), F32),
        ],
        compiler_params=pltpu.CompilerParams(vmem_limit_bytes=36 * MIB, dimension_semantics=("arbitrary", "arbitrary")),
        cost_estimate=pl.CostEstimate(flops=20_000_000_000, bytes_accessed=25_000_000, transcendentals=0),
        name="attend_back",
    )(place, *douts, big, small, ox, qx, pq, kx, vxt, kp, wr, sn, cs, tcol, head)


def reload_body(outward, owners, in_ref, out_ref):
    def move(j, carry):
        if outward:
            out_ref[owners[j]] = in_ref[j]
        else:
            out_ref[j] = in_ref[owners[j]]
        return carry

    lax.fori_loop(0, out_ref.shape[0], move, 0)


def reload(owners, rows, outward):
    return pl.pallas_call(
        functools.partial(reload_body, outward),
        in_specs=[SM, VM],
        out_specs=VM,
        out_shape=jax.ShapeDtypeStruct(rows.shape, rows.dtype),
        compiler_params=pltpu.CompilerParams(vmem_limit_bytes=6 * MIB),
        name="deal" if outward else "reload",
    )(owners, rows)


def qkv_blocks_body(x0, x1, x2, x3, tkeep_ref, tsend_ref, rel_ref, sums_ref, out_ref, acc):
    part = x0.shape[0]
    count, high, _ = out_ref.shape
    rows = high - 8
    fine = rows // 4
    parts = ((x0, tkeep_ref, 0), (x2, tkeep_ref, part), (x1, tsend_ref, 0), (x3, tsend_ref, part))
    for number, (x, t, low) in enumerate(parts):
        value = lax.dot_general(x[...], t[low : low + part, :], (((0,), (0,)), ((), ())), preferred_element_type=F32)
        acc[...] = value if number == 0 else acc[...] + value
    notes = jnp.concatenate([sums_ref[0], sums_ref[1], sums_ref[2], jnp.zeros((8, 384), F32)], axis=1).astype(BF)
    for f in range(count):
        for s in range(4):
            value = acc[(count * s + f) * fine : (count * s + f + 1) * fine, :]
            rel = rel_ref[rows * f + fine * s : rows * f + fine * (s + 1), :]
            low, high = fine * s, fine * (s + 1)
            out_ref[f, low:high, 0:512] = value[:, 0:512].astype(BF)
            out_ref[f, low:high, 512:640] = (value[:, 512:640] + rel[:, 0:128]).astype(BF)
            out_ref[f, low:high, 640:768] = rel[:, 128:256].astype(BF)
        out_ref[f, rows : rows + 8, :] = notes


def qkv_blocks(count, pieces, tkeep, tsend, rel, sums):
    width = pieces[0].shape[1]
    return pl.pallas_call(
        qkv_blocks_body,
        in_specs=[VM] * 8,
        out_specs=VM,
        out_shape=jax.ShapeDtypeStruct((count, width // count + 8, width), BF),
        scratch_shapes=[pltpu.VMEM((width, 640), F32)],
        compiler_params=pltpu.CompilerParams(vmem_limit_bytes=20 * MIB),
        cost_estimate=pl.CostEstimate(flops=2_000_000_000, bytes_accessed=8_000_000, transcendentals=0),
        name="qkv_blocks",
    )(*pieces, tkeep, tsend, rel, sums)


def merge_body(split, *refs):
    count = len(refs) - (2 if split else 1)
    sums = []
    for group in (refs[: count // 2], refs[count // 2 : count]):
        total = group[0][...].astype(F32)
        for ref in group[1:]:
            total = total + ref[...].astype(F32)
        sums.append(total.astype(BF))
    if split:
        refs[count][...], refs[count + 1][...] = sums
    else:
        cut = sums[0].shape[1]
        refs[count][:, :cut, :] = sums[0]
        refs[count][:, cut:, :] = sums[1]


def merge(backs, ins, half, split=True):
    step = min(half, 2)
    first = half // step
    width = backs[0].shape[2]
    heights = [backs[0].shape[1], ins[0].shape[1]]
    heights = heights if split else [sum(heights)]
    block = lambda p: pl.BlockSpec((step,) + p.shape[1:], lambda g: (first + g, 0, 0))
    parts = backs + ins
    return pl.pallas_call(
        functools.partial(merge_body, split),
        grid=(first,),
        in_specs=[block(p) for p in parts],
        out_specs=[pl.BlockSpec((step, h, width), lambda g: (g, 0, 0)) for h in heights],
        out_shape=[jax.ShapeDtypeStruct((half, h, width), BF) for h in heights],
        compiler_params=pltpu.CompilerParams(vmem_limit_bytes=(14 if half == 8 else 60) * MIB, dimension_semantics=("arbitrary",)),
        cost_estimate=pl.CostEstimate(flops=half * 224 * width * 6, bytes_accessed=half * 224 * width * 8, transcendentals=0),
        name="merge",
    )(*parts)


EPS = 1e-09
GELU_A = (2.0 / 3.141592653589793) ** 0.5
GELU_B = 0.044715

def spread_norm(values):
    center = values - jnp.mean(values, axis=1, keepdims=True)
    inverse = lax.rsqrt(jnp.mean(center * center, axis=1, keepdims=True) + EPS)
    return center * inverse, inverse


def middle_body(
    place, a0, a1, a2, a3, x_ref, go_ref, w_far, vec_ref, bin_ref,
    act_ref, h_ref, u_ref, dz_ref, df_ref, dbr_ref, dr_ref, d0, d1, d2, d3, sum_ref,
    wout, slope, high, normed, acc, w_ref, arrived,
):
    own = place[0]
    width = x_ref.shape[1]

    def piece_of(number, *at):
        return pltpu.make_async_copy(w_far.at[at], w_ref.at[at], arrived.at[number])

    every = slice(None)
    out_piece = piece_of(0, every, every, every, slice(2 * width, w_far.shape[3]))
    in_piece = lambda w: piece_of(1 + w, every, pl.ds(w, 1), every, slice(0, width))
    back_piece = lambda w: piece_of(5 + w, pl.ds(2 * w, 2), every, every, slice(width, 2 * width))
    out_piece.start()
    for w in range(4):
        in_piece(w).start()
        back_piece(w).start()
    out_piece.wait()
    cols = a0.shape[1]
    vector = lambda n: vec_ref[n : n + 1, :]
    for s in range(4):
        piece = w_ref[:, s, :, 2 * width : 2 * width + cols]
        wout[:, s * cols : (s + 1) * cols] = piece.reshape(width, cols)
    part = lambda mask: wout[pl.ds(pl.multiple_of((own ^ mask) * cols, 64), cols), :]
    masks = masks_of(place)
    total = x_ref[...].astype(F32) + vector(0)
    for mask, piece in zip(masks, (a0, a1, a2, a3)):
        total = total + jnp.dot(piece[...], part(mask), preferred_element_type=F32)
    unit, inverse_one = spread_norm(total)
    normed[...] = unit
    first = unit * vector(1) + vector(2)
    high[...] = first
    h_ref[...] = first.astype(BF)
    acc[...] = first + vector(3)

    def w_in_at(w):
        return w_ref[:, w, :, 0:width].reshape(width, width)

    def w_back_at(w):
        return w_ref[pl.ds(2 * w, 2), :, :, width : 2 * width].reshape(width, width)

    def forward(w, carry):
        at = pl.multiple_of(w * width, 128)
        in_piece(w).wait()
        z = jnp.dot(h_ref[...], w_in_at(w), preferred_element_type=F32) + bin_ref[:, pl.ds(at, width)]
        square = z * z
        bend = jnp.tanh(GELU_A * z * (1.0 + GELU_B * square))
        half = 0.5 + 0.5 * bend
        u = (z * half).astype(BF)
        u_ref[:, pl.ds(at, width)] = u
        slope[:, pl.ds(at, width)] = half + 0.5 * z * (1.0 - bend * bend) * (GELU_A * (1.0 + 3.0 * GELU_B * square))
        back_piece(w).wait()
        acc[...] += jnp.dot(u, w_back_at(w), preferred_element_type=F32)
        return carry

    lax.fori_loop(0, 4, forward, 0)
    unit, inverse_two = spread_norm(acc[...])
    act_ref[...] = (unit * vector(4) + vector(5)).astype(BF)

    def back(gradient, unit, inverse, gain):
        scaled = gradient * gain
        inner = scaled - jnp.mean(scaled, axis=1, keepdims=True)
        return (inner - unit * jnp.mean(scaled * unit, axis=1, keepdims=True)) * inverse

    def note(row, values):
        sum_ref[row : row + 1, :] = jnp.sum(values, axis=0, keepdims=True)

    gradient = go_ref[...].astype(F32)
    note(2, gradient * unit)
    note(3, gradient)
    second = back(gradient, unit, inverse_two, vector(4))
    df = second.astype(BF)
    df_ref[...] = df
    note(5, df.astype(F32))
    acc[...] = second

    def backward(w, carry):
        at = pl.multiple_of(w * width, 128)
        du = lax.dot_general(df_ref[...], w_back_at(w), (((1,), (1,)), ((), ())), preferred_element_type=F32)
        dz = (slope[:, pl.ds(at, width)] * du).astype(BF)
        dz_ref[:, pl.ds(at, width)] = dz
        sum_ref[pl.ds(8 + w, 1), :] = jnp.sum(dz.astype(F32), axis=0, keepdims=True)
        acc[...] += lax.dot_general(dz, w_in_at(w), (((1,), (1,)), ((), ())), preferred_element_type=F32)
        return carry

    lax.fori_loop(0, 4, backward, 0)
    gradient = acc[...]
    unit = normed[...]
    note(0, gradient * unit)
    note(1, gradient)
    dr = back(gradient, unit, inverse_one, vector(1))
    dr_ref[...] = dr
    dbr = dr.astype(BF)
    dbr_ref[...] = dbr
    note(4, dbr.astype(F32))
    sum_ref[6:8, :] = jnp.zeros((2, width), F32)
    sum_ref[12:16, :] = jnp.zeros((4, width), F32)
    for mask, out in zip(masks, (d0, d1, d2, d3)):
        value = lax.dot_general(dbr, part(mask), (((1,), (1,)), ((), ())), preferred_element_type=F32)
        out[...] = value.astype(BF)


def middle(place, pieces, x, out_grad, weights, vectors, bin_full):
    rows, width = x.shape
    cols = pieces[0].shape[1]
    hidden = bin_full.shape[1]
    low = lambda n: jax.ShapeDtypeStruct((rows, n), BF)
    full = lambda r, n: jax.ShapeDtypeStruct((r, n), F32)
    return pl.pallas_call(
        middle_body,
        in_specs=[SM] + [VM] * 6 + [pl.BlockSpec(memory_space=pl.ANY)] + [VM] * 2,
        out_specs=[VM] * 12,
        out_shape=[low(width), low(width), low(hidden), low(hidden), low(width), low(width), full(rows, width)]
        + [low(cols)] * 4
        + [full(16, width)],
        scratch_shapes=[
            pltpu.VMEM((width, width), BF),
            pltpu.VMEM((rows, hidden), F32),
            pltpu.VMEM((rows, width), F32),
            pltpu.VMEM((rows, width), F32),
            pltpu.VMEM((rows, width), F32),
            pltpu.VMEM(weights.shape, BF),
            pltpu.SemaphoreType.DMA((9,)),
        ],
        compiler_params=pltpu.CompilerParams(vmem_limit_bytes=34 * MIB),
        cost_estimate=pl.CostEstimate(flops=8_000_000_000, bytes_accessed=20_000_000, transcendentals=1_000_000),
        name="middle",
    )(place, *pieces, x, out_grad, weights, vectors, bin_full)


def angles_of(position, width):
    half_width = width // 2
    rate_table = 10000.0 ** (-(jnp.arange(half_width, dtype=jnp.float32) / half_width))
    turned = position.astype(jnp.float32)[:, None] * rate_table[None, :]
    return (jnp.sin(turned), jnp.cos(turned))


def contract_rows(left, right):
    return lax.dot_general(
        left, right, (((0,), (0,)), ((), ())), preferred_element_type=jnp.float32
    )


def contract_cols(left, right):
    return lax.dot_general(
        left, right, (((1,), (1,)), ((), ())), preferred_element_type=jnp.float32
    )


def across(values, other):
    seqs, fsdps = lax.axis_size("seq"), lax.axis_size("fsdp")
    pairs = []
    for s in range(seqs):
        for f in range(fsdps):
            to_s, to_f = other(s, f)
            pairs.append((s * fsdps + f, to_s * fsdps + to_f))
    return lax.ppermute(values, ("seq", "fsdp"), pairs)


def to_core(values):
    return across(values, lambda s, f: (s, f ^ 1))


def to_first(values):
    return across(values, lambda s, f: (s ^ (2 if f & 1 else 1), f))


def to_second(values):
    return across(values, lambda s, f: (s ^ (1 if f & 1 else 2), f))


def to_near(values):
    return across(values, lambda s, f: (s, f ^ 2))


def to_far(values):
    return across(values, lambda s, f: (s, f ^ 4))


def to_seq(values, k):
    return across(values, lambda s, f: (s ^ k, f))


def add_parts(parts, low, high):
    total = parts[0][low:high].astype(F32)
    for part in parts[1:]:
        total = total + part[low:high].astype(F32)
    return total


def back_blocks_body(place, u_ref, df_ref, keep_ref, send_ref):
    core = lax.rem(place[0], 2)
    group = u_ref.shape[1] // 4
    for g in range(1):
        acc = lax.dot_general(u_ref[...], df_ref[...], (((0,), (0,)), ((), ())), preferred_element_type=F32)
        at = pl.program_id(0) * 4
        for j in range(4):
            slot = place[1 + at + j]
            value = acc[j * group : (j + 1) * group].astype(BF)

            @pl.when(core == j % 2)
            def _():
                keep_ref[slot] = value

            @pl.when(core != j % 2)
            def _():
                send_ref[slot] = value


def back_blocks(place, u, df):
    rows, hidden = u.shape
    width = df.shape[1]
    out = jax.ShapeDtypeStruct((16, hidden // 32, width), BF)
    return pl.pallas_call(
        back_blocks_body,
        grid=(8,),
        in_specs=[SM, pl.BlockSpec((rows, hidden // 8), lambda g: (0, g)), pl.BlockSpec((rows, width), lambda g: (0, 0))],
        out_specs=[pl.BlockSpec((16, hidden // 32, width), lambda g: (0, 0, 0))] * 2,
        out_shape=[out, out],
        compiler_params=pltpu.CompilerParams(vmem_limit_bytes=16 * MIB, dimension_semantics=("arbitrary",)),
        cost_estimate=pl.CostEstimate(flops=2 * rows * hidden * width, bytes_accessed=8_000_000, transcendentals=0),
        name="back_blocks",
    )(place, u, df)


def in_blocks_body(place, h_ref, dz_ref, a0, a1, a2, a3, db_ref, sum_ref, keep_ref, send_ref):
    even = lax.rem(place[0], 2) == 0
    core = lax.rem(place[0], 2)
    own = lax.div(place[0], 8)
    step = pl.program_id(0)

    def store(block, low, a, b):
        count = a.shape[0]
        keep_ref[place[1 + block + core], pl.ds(low, count), :] = jnp.where(even, a, b).astype(BF)
        send_ref[place[2 + block - core], pl.ds(low, count), :] = jnp.where(even, b, a).astype(BF)

    def put(block, low, acc):
        store(block, low, acc[0:24], acc[24:48])

    def chunk(which):
        for g in range(2):
            acc = lax.dot_general(
                h_ref[:, g * 384 : (g + 1) * 384], dz_ref[...], (((0,), (0,)), ((), ())), preferred_element_type=F32
            )
            for j in range(0, 16, 2):
                put(g * 16 + j, pl.multiple_of(which * 24, 8), acc[j * 24 : (j + 2) * 24])

    pl.when(step < 4)(lambda: chunk(step))

    @pl.when(step == 4)
    def _():
        for mask, piece in zip((0, place[33], place[34], 3), (a0, a1, a2, a3)):
            acc = lax.dot_general(piece[...], db_ref[...], (((0,), (0,)), ((), ())), preferred_element_type=F32)
            for j in range(0, 8, 2):
                put((own ^ mask) * 8 + j, 96, acc[j * 24 : (j + 2) * 24])
        width = sum_ref.shape[1]
        line = lax.broadcasted_iota(jnp.int32, (8, width), 0)

        def note(j):
            wide = sum_ref[8 + j // 8 : 9 + j // 8, :] + jnp.zeros((8, width), F32)
            short, wide = (
                pltpu.roll(v, shift, 1) if shift % width else v
                for v, shift in ((sum_ref[0:8, :], width - 24 * j), (wide, width - 96 * (j % 8)))
            )
            return jnp.where(line == 6, wide, short)

        for j in range(0, 32, 2):
            store(j, 120, note(j), note(j + 1))


def in_blocks(place, hidden_low, dz, attn, dbr, sums):
    rows, width = hidden_low.shape
    chunks = dz.shape[1] // width
    out = jax.ShapeDtypeStruct((16, 128, width), BF)
    whole = pl.BlockSpec((rows, width), lambda g: (0, 0))
    return pl.pallas_call(
        in_blocks_body,
        grid=(chunks + 1,),
        in_specs=[SM, whole, pl.BlockSpec((rows, width), lambda g: (0, jnp.minimum(g, chunks - 1)))]
        + [pl.BlockSpec(attn[0].shape, lambda g: (0, 0))] * 4
        + [whole]
        + [pl.BlockSpec(sums.shape, lambda g: (0, 0))],
        out_specs=[pl.BlockSpec((16, 128, width), lambda g: (0, 0, 0))] * 2,
        out_shape=[out, out],
        compiler_params=pltpu.CompilerParams(vmem_limit_bytes=18 * MIB, dimension_semantics=("arbitrary",)),
        cost_estimate=pl.CostEstimate(flops=2 * rows * width * (dz.shape[1] + width), bytes_accessed=12_000_000, transcendentals=0),
        name="in_blocks",
    )(place, hidden_low, dz, *attn, dbr, sums)


def shards(
    inputs,
    w_query,
    w_key,
    w_value,
    b_value,
    w_out,
    b_out,
    norm1_gain,
    norm1_bias,
    w_in,
    b_in,
    w_back,
    b_back,
    norm2_gain,
    norm2_bias,
    w_relative,
    bias_content,
    bias_position,
    bias_type,
    type_embed,
    lengths,
    token_types,
    owners,
    grad_output,
):
    seqs, fsdps = lax.axis_size("seq"), lax.axis_size("fsdp")
    direct = seqs == 4 and fsdps == 8
    own, rank = lax.axis_index("seq"), lax.axis_index("fsdp")
    pack_count = owners.shape[0]
    sliver_rows = inputs.shape[1]
    width = inputs.shape[2]
    local_rows = w_query.shape[0]
    local_cols = width // seqs
    local_heads = w_relative.shape[1]
    scale = DH ** -0.5
    dealt = reload(owners, inputs, True)
    mine = lax.all_to_all(dealt, "fsdp", split_axis=0, concat_axis=1, tiled=True)[0]
    row_count = mine.shape[0]
    chosen = (owners == rank).astype(jnp.int32)
    pack_types = jnp.sum(chosen[:, None] * token_types, axis=0)
    pack_sizes = jnp.sum(chosen[:, None] * lengths, axis=0)
    pack_rows = pack_types.shape[0]

    def head_columns(weight):
        return lax.dynamic_slice_in_dim(weight, own * local_cols, local_cols, 1)

    block = jnp.concatenate(
        [head_columns(w) for w in (w_query, w_key, w_value)] + [w_relative.reshape(local_rows, local_cols)], axis=1
    )
    long_vectors = (b_value, b_out, norm1_gain, norm1_bias, b_back, norm2_gain, norm2_bias, b_in)
    head_vectors = (bias_content, bias_position, bias_type, type_embed[0], type_embed[1])

    def placed_at(value, row, lane):
        value = value.reshape(-1, value.shape[-1])
        return jnp.pad(value, ((row, 8 - row - value.shape[0]), (lane, width - lane - value.shape[1])))

    corner = placed_at(b_value, 0, 0)
    for number, value in enumerate(long_vectors[1:]):
        corner = corner + placed_at(value, number + 1, 0)
    for number, value in enumerate(head_vectors[:3]):
        corner = corner + placed_at(value, 0, (number + 3) * 128)
    for number, value in enumerate(head_vectors[3:]):
        corner = corner + placed_at(value, 3, (number + 3) * 128)
    early = lax.all_gather(jnp.concatenate([block, corner], axis=0), "fsdp", axis=0)
    qkvr = early[:, :local_rows].reshape(width, width)
    corners = early[:, local_rows:].astype(F32)
    full = [corners[:, n, : v.shape[0]].reshape(-1) for n, v in enumerate(long_vectors)]
    bv_full, bo_full, gain_one, shift_one, bback_full, gain_two, shift_two, bin_full = full
    heads = []
    for number, value in enumerate(head_vectors):
        row = 0 if number < 3 else 3
        lane = (number % 3 + 3) * 128
        each = corners[:, row : row + local_heads, lane : lane + value.shape[1]]
        heads.append(jnp.moveaxis(each, 0, 1).reshape(local_heads, DH))
    content_full, position_full, typebias_full, embed_zero, embed_one = heads
    bv_own = lax.dynamic_slice_in_dim(bv_full, own * local_cols, local_cols, 0)
    head = jnp.stack(
        [
            content_full,
            position_full,
            typebias_full,
            embed_zero,
            embed_one,
            bv_own.reshape(local_heads, DH),
        ],
        axis=1,
    )
    head = jnp.pad(head, ((0, 0), (0, 2), (0, 64)))

    deep = w_back.shape[0] // seqs
    late = jnp.concatenate(
        [
            lax.dynamic_slice_in_dim(w_in, own * width, width, 1),
            lax.dynamic_slice_in_dim(w_back, own * deep, deep, 0),
            head_columns(w_out),
            jnp.zeros((local_rows, 64), BF),
        ],
        axis=1,
    )
    late = lax.all_gather(late, ("fsdp", "seq"), axis=0).reshape(fsdps, seqs, local_rows, -1)
    if not direct:
        eighth_rows = width // 8
        turned_in = jnp.swapaxes(late, 1, 2).reshape(8, eighth_rows, seqs, -1)
        natural = late[..., width : 2 * width].reshape(8, seqs, eighth_rows, width)
        turned_in = jnp.swapaxes(turned_in, 1, 2)
        late = jnp.concatenate([turned_in[..., :width], natural, turned_in[..., 2 * width :]], axis=-1)

    longest = jnp.argmax(pack_sizes).astype(jnp.int32)
    start = jnp.sum(jnp.where(jnp.arange(3) < longest, pack_sizes, 0))
    near = jnp.sum(jnp.where(jnp.arange(3) == (longest + 1) % 3, pack_sizes, 0))
    parity = rank & 1
    place = jnp.stack([own, start, near, 1 + parity, 2 - parity]).astype(jnp.int32)
    row_index = jnp.arange(pack_rows, dtype=jnp.int32)
    position = jnp.where(
        row_index < LONGEST,
        row_index,
        jnp.where(row_index < LONGEST + near, row_index - LONGEST, row_index - LONGEST - near),
    )
    sine, cosine = angles_of(position, width)
    key_pos = jnp.concatenate([cosine, sine], axis=-1).astype(BF)
    key_pos_t = key_pos.T
    turned_types = lax.dynamic_slice_in_dim(
        jnp.concatenate([pack_types, pack_types]), start, pack_rows, 0
    )[:, None]
    wrel = qkvr[:, 3 * local_cols :].reshape(width, local_heads, DH)
    wrel_rows = jnp.pad(jnp.transpose(wrel, (1, 0, 2)), ((0, 0), (0, 0), (0, 64)))
    wrel_cols = jnp.pad(jnp.transpose(wrel, (1, 2, 0)), ((0, 0), (0, 64), (0, 0)))
    together = lambda n: qkvr[:, n * local_cols : (n + 1) * local_cols].reshape(width, local_heads, DH)
    paired = jnp.concatenate([together(0), together(1)], axis=2).reshape(width, 2 * local_cols)
    w_qkv = jnp.concatenate([paired, qkvr[:, 2 * local_cols : 3 * local_cols], jnp.zeros((width, 64), BF)], axis=1)

    pieces = [mine, to_first(mine), to_second(mine)]
    pieces.append(to_second(pieces[1]))
    pieces, wrel_rows = lax.optimization_barrier((pieces, wrel_rows))
    qx, pq, kx, kxt, vx, vxt = project(place, pieces, w_qkv, head, turned_types)
    big, small, ox, *head_out = attend(place, qx, pq, kxt, vx, key_pos_t, wrel_cols, sine, cosine)
    order = own ^ jnp.arange(seqs, dtype=jnp.int32)
    deal = lambda v: [v[0], to_first(v[1]), to_second(v[2]), to_seq(v[3], 3)]
    attn = deal(head_out)
    mid_vectors = jnp.stack([bo_full, gain_one, shift_one, bback_full, gain_two, shift_two, gain_two, gain_two])
    result, hidden_low, act_low, pre_grad, ffn_grad, branch_grad, sum_one_grad, *douts, short_sums = middle(
        place, attn, mine, grad_output[0], late, mid_vectors, bin_full[None]
    )
    activations = result.reshape(1, row_count, width)
    douts = deal(douts)
    devices = seqs * fsdps
    device = own * fsdps + rank
    fine = width // devices
    deep = act_low.shape[1] // devices
    kept_place = jnp.where((order == 1) | (order == 2), jnp.where(parity == 1, 3 - order, order), order)
    if direct:
        relative = jnp.arange(32, dtype=jnp.int32) ^ device
        bit = lambda n: (relative >> n) & 1
        flip = (bit(0) ^ parity) == 1
        one, two = jnp.where(flip, bit(4), bit(3)), jnp.where(flip, bit(3), bit(4))
        me, masks = device[None], place[3:5]
        in_table = jnp.concatenate([me, one * 8 + two * 4 + bit(1) * 2 + bit(2), masks]).astype(jnp.int32)
        back_table = jnp.concatenate([me, bit(1) * 8 + one * 4 + two * 2 + bit(2), masks]).astype(jnp.int32)
        kept, sent = in_blocks(in_table, hidden_low, pre_grad, attn, branch_grad, short_sums)
        ins = [kept, to_core(sent)]
        kept, sent = back_blocks(back_table, act_low, ffn_grad)
        backs = [kept, to_core(sent)]
        back_out, in_out = merge(backs, ins, 8)
        qx, back_out, in_out = lax.optimization_barrier((qx, back_out, in_out))
        backs.append(to_near(back_out))
        ins.append(to_first(in_out))
    else:
        scatter = lambda v: lax.psum_scatter(v, ("seq", "fsdp"), scatter_dimension=0, tiled=True)
        w_back_grad = scatter(contract_rows(act_low, ffn_grad))
        w_in_grad = scatter(contract_rows(hidden_low, pre_grad))
        spun = contract_rows(jnp.concatenate(attn, axis=1), branch_grad).reshape(seqs, local_cols, width)
        w_out_grad = scatter(jnp.take(spun, kept_place, axis=0).reshape(width, width))

    tkeep, tsend, rel, sums = attend_back(
        place, douts, big, small, ox, qx, pq, kx, vxt, key_pos, wrel_rows, sine, cosine, turned_types, head
    )
    if direct:
        bundle = qkv_blocks(fsdps, pieces, tkeep, tsend, rel, sums)
    else:
        grad = contract_rows(pieces[0], tkeep[:row_count]) + contract_rows(pieces[2], tkeep[row_count:])
        grad = grad + contract_rows(pieces[1], tsend[:row_count]) + contract_rows(pieces[3], tsend[row_count:])
        grad = jnp.swapaxes(grad.reshape(seqs, fsdps, fine, 640), 0, 1).reshape(fsdps, local_rows, 640)
        tall = rel.reshape(fsdps, local_rows, 256)
        bundle = jnp.concatenate([grad[..., :512], grad[..., 512:] + tall[..., :128], tall[..., 128:]], axis=2)
        notes = jnp.concatenate([sums[0], sums[1], sums[2], jnp.zeros((8, 384), F32)], axis=1)
        bundle = jnp.concatenate([bundle, jnp.broadcast_to(notes[None], (fsdps,) + notes.shape)], axis=1).astype(BF)
    total = lax.psum_scatter(bundle, "fsdp", scatter_dimension=0, tiled=True)[0].astype(F32)
    dx_send = contract_cols(tsend, w_qkv).astype(BF)
    if direct:
        dx_send, backs, ins, bundle = lax.optimization_barrier((dx_send, backs, ins, bundle))
        back_out, in_out = merge(backs, ins, 4)
        backs.append(to_first(back_out))
        ins.append(to_second(in_out))
    dx_first = to_first(dx_send)
    dx_keep = contract_cols(tkeep, w_qkv)
    if direct:
        dx_first, backs, ins = lax.optimization_barrier((dx_first, backs, ins))
    dx_out = (dx_keep[row_count:] + dx_first[row_count:].astype(F32)).astype(BF)
    dx_second = to_second(dx_out)
    if direct:
        back_out, in_out = merge(backs, ins, 2)
        backs.append(to_second(back_out))
        ins.append(to_near(in_out))
        dx_second, backs, ins = lax.optimization_barrier((dx_second, backs, ins))
    input_rows = sum_one_grad + dx_keep[:row_count] + dx_first[:row_count].astype(F32) + dx_second.astype(F32)
    input_rows = input_rows.astype(BF).reshape(fsdps, sliver_rows, width)
    returned = lax.all_to_all(input_rows, "fsdp", split_axis=0, concat_axis=0, tiled=True)
    input_grad = reload(owners, returned, False)
    if direct:
        far_out, total = lax.optimization_barrier((merge(backs, ins, 1, False)[0], total))
        far = to_far(far_out)
        cut = kept.shape[1]
    if not direct:
        short_sums = lax.psum(short_sums, ("seq", "fsdp"))
        short_grads = lax.dynamic_slice(short_sums, (0, device * fine), (8, fine))
        in_bias_grad = lax.dynamic_slice(short_sums, (8 + device * deep // width, device * deep % width), (1, deep))[0]
    own_qkv = total[:local_rows].astype(BF).reshape(seqs, fine, width)
    block_for = lambda mask: lax.dynamic_index_in_dim(own_qkv, own ^ mask, 0, keepdims=True)
    swapped = jnp.concatenate(deal([block_for(m) for m in (0, place[3], place[4], 3)]), axis=0)
    swapped = jnp.take(swapped, kept_place, axis=0).astype(F32)
    both = swapped[:, :, : 2 * local_cols].reshape(seqs, fine, local_heads, 2, DH)
    both = jnp.transpose(both, (3, 1, 0, 2, 4)).reshape(2, fine, width)
    w_value_grad = jnp.transpose(swapped[:, :, 2 * local_cols : 3 * local_cols], (1, 0, 2)).reshape(fine, width)
    if direct:
        _, _, far, _ = lax.optimization_barrier((both, w_value_grad, far, input_grad))
        w_back_grad = add_parts(backs + [far[:, :cut]], 0, 1)[0]
        in_total = add_parts(ins + [far[:, cut:]], 0, 1)[0]
        w_in_grad = jnp.concatenate([in_total[c * 24 : (c + 1) * 24] for c in range(4)], axis=1)
        w_out_grad = in_total[96:120]
        short_grads, in_bias_grad = in_total[120:128, :fine], in_total[126, :deep]
    rel_total = total[:local_rows, 3 * local_cols :].reshape(local_rows, local_heads, DH)
    notes = total[local_rows:, :384].reshape(8, 3, 128)
    eighth = DH // fsdps
    mine_sums = lax.dynamic_slice(notes, (0, 0, rank * eighth), (8, 3, eighth))
    value_bias_grad = lax.dynamic_slice(notes[5, :, :DH].reshape(-1), (rank * fine,), (fine,))
    return (
        activations,
        input_grad,
        both[0],
        both[1],
        w_value_grad,
        value_bias_grad,
        w_out_grad,
        short_grads[4],
        short_grads[0],
        short_grads[1],
        w_in_grad,
        in_bias_grad,
        w_back_grad,
        short_grads[5],
        short_grads[2],
        short_grads[3],
        rel_total,
        mine_sums[0],
        mine_sums[1],
        mine_sums[2],
        mine_sums[3:5],
    )


def solution(mesh):
    placed = (
        P(None, ("seq", "fsdp"), None),
        P("fsdp", None),
        P("fsdp", None),
        P("fsdp", None),
        P("fsdp"),
        P("fsdp", None),
        P("fsdp"),
        P("fsdp"),
        P("fsdp"),
        P("fsdp", None),
        P("fsdp"),
        P("fsdp", None),
        P("fsdp"),
        P("fsdp"),
        P("fsdp"),
        P("fsdp", "seq", None),
        P("seq", "fsdp"),
        P("seq", "fsdp"),
        P("seq", "fsdp"),
        P(None, "seq", "fsdp"),
        P(),
        P(),
        P(),
        P("fsdp", "seq", None),
    )
    return jax.shard_map(
        shards,
        mesh=mesh,
        in_specs=placed,
        out_specs=(
            P("fsdp", "seq", None),
            P(None, ("seq", "fsdp"), None),
            P(("seq", "fsdp"), None),
            P(("seq", "fsdp"), None),
            P(("seq", "fsdp"), None),
            P(("seq", "fsdp")),
            P(("seq", "fsdp"), None),
            P(("seq", "fsdp")),
            P(("seq", "fsdp")),
            P(("seq", "fsdp")),
            P(("seq", "fsdp"), None),
            P(("seq", "fsdp")),
            P(("seq", "fsdp"), None),
            P(("seq", "fsdp")),
            P(("seq", "fsdp")),
            P(("seq", "fsdp")),
            P("fsdp", "seq", None),
            P("seq", "fsdp"),
            P("seq", "fsdp"),
            P("seq", "fsdp"),
            P(None, "seq", "fsdp"),
        ),
        check_vma=False,
    )
```
